32 devices in a mesh: dom: 8 (over y, x, core), st: 4 (over z).
Axes of the slice: x: 2, y: 2, z: 4, core: 2. Of those that a mesh axis runs over, the one named last changes fastest.
Arguments:
- start_block: bfloat16 [2, 64, 128, 729], P(None, 'dom', 'st'), may hold values from -48 to 48
- resident: bfloat16 [1024, 64, 729], P('st', 'dom'), may hold values from -0.09375 to 0.09375
- stiffness: bfloat16 [729, 729], replicated, may hold values from -0.21875 to 0.21875
- cell_scale: float32 [64], P('dom'), may hold values from 0.5 to 2
- potential: float32 [64, 729], P('dom'), may hold values from -1 to 1
- cell_count: int32 [8], P('dom'), may hold values from 2 to 8, as said below
- face_index: int32 [8, 2, 81], P('dom'), may hold values from 0 to 5831, as said below
Outputs:
- rotated: bfloat16 [2, 64, 128, 729], P(None, 'dom', 'st')
The draws below stay inside these ranges and needn't reach their ends.
Inputs may be any that keep to these rules, and one draw needn't show every extreme that they name: Domain d has cell_count[d] live cells in its first slots; some domain has 8 and some has 2. face_index[d, 0, :] lists each node of the last face of domain d's last live cell once, face_index[d, 1, :] each node of the first face of its cell 0 once, as flat indices cell * 729 + node; the k-th entries of face_index[d, 0] and face_index[d + 1, 1] are the same mesh node.
All inputs are finite; a program needn't handle non-finite values.
Results may differ from the reference program's by a relative error of at most 0.0075.
Values may be sent and summed in bfloat16 or wider, within the bound.
A program may use at most 64 MiB of HBM per device.

```python
import math
import jax
import jax.numpy as jnp
from jax import lax

NODES = 729
FACE = 81
STATES = 128
RES = 1024
BLOCKS = 2
CAP = 8
NCELL = 64


def domain_counts(key):
    base_key = jax.random.fold_in(key, 7)
    domain_total = NCELL // CAP
    counts = jax.random.randint(base_key, (domain_total,), 2, CAP + 1)
    chosen = jax.random.permutation(jax.random.fold_in(base_key, 1), domain_total)
    counts = counts.at[chosen[0]].set(CAP)
    counts = counts.at[chosen[1]].set(2)
    return counts.astype(jnp.int32)


def draw_cell_count(key, part):
    return domain_counts(key)


def face_order(sub_key):
    return jax.random.permutation(sub_key, FACE).astype(jnp.int32)


def draw_face_index(key, part):
    counts = domain_counts(key)
    domain_total = NCELL // CAP
    face_keys = jax.random.split(jax.random.fold_in(key, 11), domain_total)
    face_orders = jax.vmap(face_order)(face_keys)
    out_row = (counts[:, None] - 1) * NODES + (NODES - FACE) + face_orders
    previous = jnp.concatenate([face_orders[-1:], face_orders[:-1]], 0)
    return jnp.stack([out_row, previous], 1).astype(jnp.int32)


def draw_start_block(key, part):
    raw_key = jax.random.fold_in(key, 21)
    mix_key = jax.random.fold_in(key, 22)
    scale_key = jax.random.fold_in(key, 23)
    raw_values = jax.random.truncated_normal(raw_key, -4.0, 4.0, (BLOCKS, NCELL, STATES, NODES), jnp.float32)
    spread = jnp.exp(jax.random.uniform(scale_key, (NCELL,), jnp.float32, 0.0, math.log(10.0)))
    coupling = jax.random.truncated_normal(mix_key, -2.0, 2.0, (BLOCKS, STATES, STATES), jnp.float32)
    mixing = jnp.eye(STATES, dtype=jnp.float32)[None] + 0.25 / STATES ** 0.5 * coupling
    mixed_values = jnp.einsum('kcsn,kst->kctn', raw_values, mixing)
    mixed_values = mixed_values * spread[None, :, None, None]
    return jnp.clip(mixed_values, -48.0, 48.0).astype(jnp.bfloat16)


def steps_of(own_key, dims, pieces, low, top_value):
    factor_of = 1.0
    for dim, parts in pieces:
        heights = jax.random.uniform(jax.random.fold_in(jax.random.fold_in(own_key, 6), dim), (parts,), jnp.float32, low / len(pieces), top_value / len(pieces))
        factor_of = factor_of * jnp.repeat(jnp.exp(heights), dims[dim] // parts).reshape((-1,) + (1,) * (len(dims) - 1 - dim))
    return factor_of


def normal_values(key, shape, deviation, bound, cuts=(), kind=jnp.bfloat16):
    loudness = steps_of(key, shape, cuts, -0.22, 0.18) if cuts else 1.0
    drawn = jax.random.normal(key, shape, jnp.float32) * deviation * loudness
    return jnp.minimum(jnp.maximum(drawn, -bound), bound).astype(kind)


def setup_inputs(seed: int = 0) -> dict:
    splits = jax.random.split(jax.random.key(seed), 8)
    return {
        "start_block": draw_start_block(jax.random.fold_in(splits[7], 71), 0),
        "resident": normal_values(splits[1], (RES, NCELL, NODES), ((0.3 / (RES * NCELL * NODES) ** 0.5) ** 0.5), 0.09375, ((0, 4), (1, 8))),
        "stiffness": normal_values(splits[2], (NODES, NODES), NODES ** -0.5, 0.21875),
        "cell_scale": jnp.clip(jnp.exp(math.log(2.0) - 1.3862944 * jax.random.uniform(splits[3], (NCELL,), jnp.float32) ** steps_of(splits[3], (NCELL,), ((0, 8),), -0.2, 0.2)), 0.5, 2.0),
        "potential": jnp.clip(jax.random.uniform(splits[4], (NCELL, NODES), jnp.float32, -1.0, 1.0) * steps_of(splits[4], (NCELL, NODES), ((0, 8),), -0.4, 0.0), -1.0, 1.0),
        "cell_count": draw_cell_count(jax.random.fold_in(splits[7], 71), 0),
        "face_index": draw_face_index(jax.random.fold_in(splits[7], 71), 0),
    }


CENTER = 0.5
HALF_WIDTH = 2.0
EPSILON = 1e-06

def operate(in_field, stiffness, cell_scale, potential, live_slots, face_index):
    slot_count, state_count, node_count = in_field.shape
    local_sum = jnp.dot(in_field.reshape(slot_count * state_count, node_count), stiffness, preferred_element_type=jnp.float32).reshape(slot_count, state_count, node_count)
    local_sum = cell_scale[:, None, None] * local_sum + potential[:, None, :] * in_field.astype(jnp.float32)
    local_sum = local_sum.reshape(NCELL // CAP, CAP, state_count, node_count)
    right_face = local_sum[:, :-1, :, NODES - FACE:]
    left_face = local_sum[:, 1:, :, :FACE]
    pair_live = live_slots[:, 1:, None, None]
    local_sum = local_sum.at[:, :-1, :, NODES - FACE:].set(right_face + pair_live * left_face)
    local_sum = local_sum.at[:, 1:, :, :FACE].set(left_face + pair_live * right_face)
    domains = jnp.arange(NCELL // CAP).astype(jnp.int32)[:, None]
    out_cells = face_index[:, 0, :] // NODES
    out_nodes = face_index[:, 0, :] % NODES
    in_cells = face_index[:, 1, :] // NODES
    in_nodes = face_index[:, 1, :] % NODES
    outgoing = local_sum[domains, out_cells, :, out_nodes]
    incoming = local_sum[domains, in_cells, :, in_nodes]
    zero_face = jnp.zeros_like(outgoing[:1])
    from_left = jnp.concatenate([zero_face, outgoing[:-1]], 0)
    from_right = jnp.concatenate([incoming[1:], zero_face], 0)
    local_sum = local_sum.at[domains, in_cells, :, in_nodes].add(from_left)
    local_sum = local_sum.at[domains, out_cells, :, out_nodes].add(from_right)
    local_sum = local_sum * live_slots[:, :, None, None]
    return local_sum.reshape(slot_count, state_count, node_count)

def coefficients(correlation, inner_product_matrix, total_nodes):
    mean_square = jnp.diagonal(inner_product_matrix) / total_nodes + EPSILON
    inverse_root = lax.rsqrt(mean_square)
    normed = inner_product_matrix * inverse_root[:, None] * inverse_root[None, :] / total_nodes
    identity = jnp.eye(inner_product_matrix.shape[0], dtype=jnp.float32)
    mixing = inverse_root[:, None] * (1.5 * identity - 0.5 * normed)
    projected_states = jnp.dot(correlation, mixing, precision=lax.Precision.HIGHEST, preferred_element_type=jnp.float32)
    return (mixing.astype(jnp.bfloat16), projected_states.astype(jnp.bfloat16))

def reference(start_block, resident, stiffness, cell_scale, potential, cell_count, face_index):
    live_slots = (jnp.arange(CAP)[None, :] < cell_count[:, None]).astype(jnp.float32)
    live_mask = live_slots.reshape(-1).astype(jnp.bfloat16)[:, None, None]
    total_nodes = float(NCELL * NODES)

    def apply_h(in_field):
        return operate(in_field, stiffness, cell_scale, potential, live_slots, face_index)
    results = []
    for block_index in range(BLOCKS):
        first_states = start_block[block_index] * live_mask
        first_wide = first_states.astype(jnp.float32)
        step_one = ((apply_h(first_states) - CENTER * first_wide) / HALF_WIDTH).astype(jnp.bfloat16)
        filtered = (2.0 * (apply_h(step_one) - CENTER * step_one.astype(jnp.float32)) / HALF_WIDTH - first_wide).astype(jnp.bfloat16)
        filtered_broad_states = filtered.astype(jnp.float32)
        inner_product_matrix = jnp.einsum('ptw,phw->th', filtered_broad_states, filtered_broad_states)

        def add_correlation(domain, running_total):
            start_cell = (domain * CAP).astype(jnp.int32)
            resident_state_rows = lax.dynamic_slice_in_dim(resident, start_cell, CAP, 1).astype(jnp.float32)
            block_column_count = lax.dynamic_slice_in_dim(filtered_broad_states, start_cell, CAP, 0)
            return running_total + jnp.einsum('jpu,pzu->jz', resident_state_rows, block_column_count)
        correlation = lax.fori_loop(0, NCELL // CAP, add_correlation, jnp.zeros((RES, STATES), jnp.float32))
        mixing, projected_states = coefficients(correlation, inner_product_matrix, total_nodes)
        broad_mixing_weight = mixing.astype(jnp.float32)
        projected_broad_states = projected_states.astype(jnp.float32)

        def rotate(domain):
            start_cell = (domain * CAP).astype(jnp.int32)
            resident_state_rows = lax.dynamic_slice_in_dim(resident, start_cell, CAP, 1).astype(jnp.float32)
            block_column_count = lax.dynamic_slice_in_dim(filtered_broad_states, start_cell, CAP, 0)
            retained_portion = jnp.einsum('ghy,hw->gwy', block_column_count, broad_mixing_weight)
            series_term_sum = jnp.einsum('es,evd->vsd', projected_broad_states, resident_state_rows)
            return retained_portion - series_term_sum
        rotated = lax.map(rotate, jnp.arange(NCELL // CAP).astype(jnp.int32)).reshape(NCELL, STATES, NODES)
        results.append(rotated.astype(jnp.bfloat16) * live_mask)
    return jnp.stack(results)
```

```python
from functools import partial

import jax
import jax.numpy as jnp
from jax import lax
from jax.experimental import pallas as pl
from jax.experimental.pallas import tpu as pltpu
from jax.sharding import PartitionSpec as P

CENTER = 0.5
HALF_WIDTH = 2.0
EPSILON = 1e-06
F32 = jnp.float32
BF16 = jnp.bfloat16
WIRE = BF16
RIGHT, LEFT = 0, 1
MESH = pl.DeviceIdType.MESH


def dot_nn(a, b, precision=None):
    return lax.dot_general(
        a, b, (((1,), (0,)), ((), ())), precision=precision, preferred_element_type=F32
    )


def dot_nt(a, b, precision=None):
    return lax.dot_general(
        a, b, (((1,), (1,)), ((), ())), precision=precision, preferred_element_type=F32
    )


def both(*conditions):
    found = conditions[0]
    for condition in conditions[1:]:
        found = jnp.logical_and(found, condition)
    return found


def kernel(
    sizes,
    scale_ref,
    count_ref,
    start_ref,
    res_hbm,
    stiff_ref,
    pot_ref,
    face_ref,
    out_ref,
    local,
    inner,
    states,
    part,
    wire,
    part_recv,
    total,
    mix,
    proj,
    share,
    share_recv,
    res_in,
    res_wide,
    res_ref,
    res_near,
    proj_near,
    retained,
    face_out,
    face_in,
    face_send_sem,
    face_recv_sem,
    gather_send_sem,
    gather_recv_sem,
    one_send_sem,
    one_recv_sem,
    two_send_sem,
    two_recv_sem,
    share_send_sem,
    share_recv_sem,
    load_sem,
    near_send_sem,
    near_recv_sem,
    coef_send_sem,
    coef_recv_sem,
):
    doms, sts, blocks, cells, width, nodes, face, res, rows, moved = sizes
    total_states = sts * width
    total_nodes = float(doms * cells * nodes)
    window = (nodes - face) // 128 * 128
    offset = nodes - face - window
    d = lax.axis_index("dom")
    s = lax.axis_index("st")
    has_right, has_left = s < sts - 1, s > 0
    has_next, has_prev = d < doms - 1, d > 0
    own = pl.ds(pl.multiple_of(s * width, width), width)
    steps = sts - 1
    last_step = jnp.maximum(s, steps - s)
    pending = []
    count = count_ref[0]
    scale = [scale_ref[c] for c in range(cells)]
    live = [jnp.where(c < count, 1.0, 0.0).astype(F32) for c in range(cells)]
    last = [jnp.where(c == count - 1, 1.0, 0.0).astype(F32) for c in range(cells)]
    load = pltpu.make_async_copy(res_hbm, res_in, load_sem)
    load.start()

    origin = {RIGHT: s == 0, LEFT: s == steps}
    sends = {RIGHT: has_right, LEFT: has_left}
    receives = {RIGHT: has_left, LEFT: has_right}
    near_end = {RIGHT: s == 1, LEFT: s == steps - 1}

    def to(way):
        return s + 1 if way == RIGHT else s - 1

    def dom_peer(k):
        return lax.rem(d + k, doms)

    barrier = pltpu.get_barrier_semaphore()

    def greet(k, carry):
        pl.semaphore_signal(barrier, inc=1, device_id={"dom": dom_peer(k)}, device_id_type=MESH)
        return carry

    lax.fori_loop(1, doms, greet, 0)
    for way in (RIGHT, LEFT):

        @pl.when(sends[way])
        def _():
            pl.semaphore_signal(barrier, inc=1, device_id={"st": to(way)}, device_id_type=MESH)

    neighbours = has_right.astype(jnp.int32) + has_left.astype(jnp.int32)
    pl.semaphore_wait(barrier, doms - 1 + neighbours)

    def remote(src, dst, send_sem, recv_sem, axis, peer):
        return pltpu.make_async_remote_copy(
            src_ref=src,
            dst_ref=dst,
            send_sem=send_sem,
            recv_sem=recv_sem,
            device_id={axis: peer},
            device_id_type=MESH,
        )

    def one_hot(row, first, extent):
        node = lax.broadcasted_iota(jnp.int32, (extent, face), 0) + first
        if row == 0:
            node = node + (count - 1) * nodes
        return jnp.where(face_ref[0, row : row + 1, :] == node, 1.0, 0.0).astype(F32)

    def mask(c):
        return live[c].astype(BF16)

    def relayout():
        load.wait()
        for chunk in range(nodes // face):
            at = slice(chunk * face, (chunk + 1) * face)
            wide = res_in[at].astype(F32).reshape(face * cells, res)
            for h in range(res // 128):
                lanes = slice(h * 128, (h + 1) * 128)
                res_wide[h] = wide[:, lanes]
                for c in range(cells):
                    res_ref[c, at, lanes] = res_wide[h, pl.ds(c, face, stride=cells), :].astype(BF16)


    def rows_of(c):
        return slice(c * width, (c + 1) * width)

    def face_copy(step, b, way):
        return remote(
            face_out.at[step, b, way],
            face_in.at[step, b, way],
            face_send_sem.at[step, b, way],
            face_recv_sem.at[step, b, way],
            "dom",
            d + 1 if way == RIGHT else d - 1,
        )

    def first(b, c):
        if c is None:
            return jnp.concatenate([first(b, i) for i in range(cells)], axis=0)
        return start_ref[b, c] * mask(c)

    def second(b, c):
        return inner[b] if c is None else inner[b, rows_of(c), :]

    def operator_begin(step, b):
        field = partial(second if step else first, b)
        local[b] = dot_nn(field(None), stiff_ref[...])
        last_tail = jnp.zeros((width, nodes - window), F32)
        for c in range(cells):
            value = scale[c] * local[b, rows_of(c), :] + pot_ref[c : c + 1, :] * field(c).astype(F32)
            local[b, rows_of(c), :] = value
            last_tail = last_tail + last[c] * value[:, window:]
        face_out[step, b, RIGHT] = dot_nn(
            last_tail, one_hot(0, window, nodes - window), lax.Precision.HIGHEST
        )
        face_out[step, b, LEFT] = dot_nn(
            local[b, rows_of(0), :face], one_hot(1, 0, face), lax.Precision.HIGHEST
        )
        for way, there in ((RIGHT, has_next), (LEFT, has_prev)):

            @pl.when(there)
            def _():
                face_copy(step, b, way).start()

            pending.append((there, partial(face_copy, step, b, way)))
        for c in range(cells - 1):
            pair = live[c + 1]
            tail = local[b, rows_of(c), window:]
            head = local[b, rows_of(c + 1), :face]
            padded = head
            if offset:
                padded = jnp.concatenate([jnp.zeros((width, offset), F32), head], axis=1)
            local[b, rows_of(c), window:] = tail + pair * padded
            local[b, rows_of(c + 1), :face] = head + pair * tail[:, offset:]

    def operator_end(step, b):
        for way, source in ((RIGHT, has_prev), (LEFT, has_next)):

            @pl.when(source)
            def _():
                face_copy(step, b, way).wait_recv()

            @pl.when(jnp.logical_not(source))
            def _():
                face_in[step, b, way] = jnp.zeros((width, face), F32)

        local[b, rows_of(0), :face] += dot_nt(
            face_in[step, b, RIGHT], one_hot(1, 0, face), lax.Precision.HIGHEST
        )
        tail_add = dot_nt(
            face_in[step, b, LEFT], one_hot(0, window, nodes - window), lax.Precision.HIGHEST
        )
        for c in range(cells):
            local[b, rows_of(c), window:] += last[c] * tail_add
        for c in range(cells):
            value = live[c] * local[b, rows_of(c), :]
            if step == 0:
                inner[b, rows_of(c), :] = (
                    (value - CENTER * first(b, c).astype(F32)) / HALF_WIDTH
                ).astype(BF16)
            else:
                states[b, c, own, :] = (
                    2.0 * (value - CENTER * second(b, c).astype(F32)) / HALF_WIDTH
                    - first(b, c).astype(F32)
                ).astype(BF16)


    def of_shard(shard):
        return pl.ds(pl.multiple_of(shard * width, width), width)

    def gather_copy(b, way, shard, c):
        at = states.at[b, c, of_shard(shard), :]
        return remote(
            at, at, gather_send_sem.at[b, way, shard], gather_recv_sem.at[b, shard, c], "st", to(way)
        )

    def gather_whole(b, way, shard):
        at = states.at[b, :, of_shard(shard), :]
        return remote(
            at, at, gather_send_sem.at[b, way, shard], gather_recv_sem.at[b, shard, 0], "st", to(way)
        )

    def gather_own(b, way, there):
        @pl.when(both(there, sends[way]))
        def _():
            def one(c, carry):
                gather_copy(b, way, s, c).start()
                return carry

            lax.fori_loop(0, cells, one, 0)

    def gather_start(b, k):
        gather_own(b, RIGHT, s == k)
        gather_own(b, LEFT, s + k == steps)

    def gather_flat(b, begin, end):
        def one(i, carry):
            k = lax.div(i, cells) + 1
            c = lax.rem(i, cells)
            for way, shard, here in ((LEFT, s + k, s + k < sts), (RIGHT, s - k, s >= k)):

                @pl.when(here)
                def _():
                    gather_copy(b, way, shard, c).wait_recv()

                    @pl.when(sends[way])
                    def _():
                        gather_copy(b, way, shard, c).start()

            @pl.when(k == last_step)
            def _():
                contract(b, c)

            if b + 1 < blocks:

                @pl.when(c == cells - 1)
                def _():
                    gather_start(b + 1, k)

            return carry

        lax.fori_loop(begin, end, one, 0)

    def gather_drain(b):
        def one(shard, carry):
            for way, passed in ((RIGHT, shard <= s), (LEFT, shard >= s)):

                @pl.when(both(passed, sends[way]))
                def _():
                    gather_whole(b, way, shard).wait_send()

            return carry

        lax.fori_loop(0, sts, one, 0)


    def contract(b, c):
        block = states[b, c]
        found = dot_nn(block, res_ref[c])
        for h in range(res // total_states):
            at = slice(h * total_states, (h + 1) * total_states)
            part[b, at, :] += found[:, at]
        part[b, res : res + total_states, :] += dot_nt(block, block)

    def slice_of(peer):
        return pl.ds(pl.multiple_of(peer * rows, 16), rows)

    def one_copy(b, k):
        peer = dom_peer(k)
        return remote(
            wire.at[b, slice_of(peer)],
            part_recv.at[b, k],
            one_send_sem.at[b, k],
            one_recv_sem.at[b, k],
            "dom",
            peer,
        )

    def two_copy(b, k):
        at = total.at[b, slice_of(d)]
        return remote(at, at, two_send_sem.at[b, k], two_recv_sem.at[b, k], "dom", dom_peer(k))

    def from_peer(b, k):
        peer = dom_peer(doms - k)
        at = total.at[b, slice_of(peer)]
        return remote(at, at, two_send_sem.at[b, k], two_recv_sem.at[b, k], "dom", peer)

    def peers(body):
        def step(k, carry):
            body(k)
            return carry

        lax.fori_loop(1, doms, step, 0)

    def reduce_start(b):
        wire[b] = part[b].astype(WIRE)
        peers(lambda k: one_copy(b, k).start())

    def reduce_middle(b):
        def add(k, found):
            one_copy(b, k).wait_recv()
            return found + part_recv[b, k].astype(F32)

        found = lax.fori_loop(1, doms, add, part[b, slice_of(d), :])
        total[b, slice_of(d), :] = found.astype(WIRE)
        peers(lambda k: two_copy(b, k).start())

    def reduce_end(b):
        peers(lambda k: from_peer(b, k).wait_recv())

    def reduce_drain(b):
        def one(k):
            one_copy(b, k).wait_send()
            two_copy(b, k).wait_send()

        peers(one)

    def coefficients(b):
        gram = total[b, res : res + total_states, :].astype(F32)
        shape = (total_states, total_states)
        eye = (
            lax.broadcasted_iota(jnp.int32, shape, 0) == lax.broadcasted_iota(jnp.int32, shape, 1)
        ).astype(F32)
        along = jnp.sum(gram * eye, axis=0, keepdims=True) / total_nodes + EPSILON
        down = jnp.sum(gram * eye, axis=1, keepdims=True) / total_nodes + EPSILON
        root_i, root_j = lax.rsqrt(along), lax.rsqrt(down)
        mixing = root_i * (1.5 * eye - 0.5 * (gram * root_i * root_j / total_nodes))
        mix[b] = mixing.astype(BF16)
        for h in range(res // total_states):
            at = slice(h * total_states, (h + 1) * total_states)
            proj[b, :, at] = dot_nn(
                mixing, total[b, at, :].astype(F32), lax.Precision.HIGHEST
            ).astype(BF16)


    def near_copy(way, c):
        return remote(
            res_ref.at[c],
            res_near.at[way, c],
            near_send_sem.at[way, c],
            near_recv_sem.at[way, c],
            "st",
            to(way),
        )

    def near_start(c):
        if c >= moved:
            return
        for way in (RIGHT, LEFT):
            there = both(origin[way], sends[way])

            @pl.when(there)
            def _():
                near_copy(way, c).start()

            pending.append((there, partial(near_copy, way, c)))

    def coef_copy(b, way):
        return remote(
            proj.at[b],
            proj_near.at[way, b],
            coef_send_sem.at[way, b],
            coef_recv_sem.at[way, b],
            "st",
            to(way),
        )

    def coef_start(b):
        if not moved:
            return
        for way in (RIGHT, LEFT):
            there = both(origin[way], sends[way])

            @pl.when(there)
            def _():
                coef_copy(b, way).start()

            pending.append((there, partial(coef_copy, b, way)))


    def share_copy(b, t, way, c):
        return remote(
            share.at[b, t, c],
            share_recv.at[way, b, t, c],
            share_send_sem.at[b, t],
            share_recv_sem.at[way, b, t, c],
            "st",
            to(way),
        )

    def share_whole(b, t, way, begin):
        at = pl.ds(begin, cells - begin)
        return remote(
            share.at[b, t, at],
            share_recv.at[way, b, t, at],
            share_send_sem.at[b, t],
            share_recv_sem.at[way, b, t, 0],
            "st",
            to(way),
        )

    def ahead(way):
        if way == RIGHT:
            return steps - s, lambda i: steps - i
        return s, lambda i: i

    def share_start(b):
        def one(c, carry):
            found = dot_nt(proj[b], res_ref[c])
            for t in range(sts):
                piece = found[t * width : (t + 1) * width, :]
                share[b, t, c] = piece.astype(BF16)

                @pl.when(t == s)
                def _():
                    retained[b, c] = -piece

            for way in (RIGHT, LEFT):

                @pl.when(both(origin[way], c >= moved))
                def _():
                    number, target = ahead(way)

                    def send(i, carry):
                        share_copy(b, target(i), way, c).start()
                        return carry

                    lax.fori_loop(0, number, send, 0)

            return carry

        lax.fori_loop(0, cells, one, 0)

    def share_drain(b):
        def one(t, carry):
            for way, passed in ((RIGHT, t > s), (LEFT, t < s)):

                @pl.when(both(passed, origin[way]))
                def _():
                    share_whole(b, t, way, moved).wait_send()

                @pl.when(both(passed, jnp.logical_not(origin[way])))
                def _():
                    share_whole(b, t, way, 0).wait_send()

            return carry

        lax.fori_loop(0, sts, one, 0)

    def retain(b):
        def one(c, carry):
            retained[b, c] += dot_nn(mix[b, own, :], states[b, c])
            return carry

        lax.fori_loop(0, cells, one, 0)

    def absorb(b, way, c):
        number, target = ahead(way)

        def one(i, carry):
            t = target(i)
            share_copy(b, t, way, c).wait_recv()
            share[b, t, c] = (
                share[b, t, c].astype(F32) + share_recv[way, b, t, c].astype(F32)
            ).astype(BF16)
            share_copy(b, t, way, c).start()
            return carry

        lax.fori_loop(0, number, one, 0)
        share_copy(b, s, way, c).wait_recv()
        retained[b, c] -= share_recv[way, b, s, c].astype(F32)

    def absorb_near(b, way, c):
        if b == 0:
            near_copy(way, c).wait_recv()

        @pl.when(c == 0)
        def _():
            coef_copy(b, way).wait_recv()

        found = dot_nt(proj_near[way, b], res_near[way, c])
        for t in reversed(range(sts)) if way == RIGHT else range(sts):
            piece = found[t * width : (t + 1) * width, :]

            @pl.when(t > s if way == RIGHT else t < s)
            def _():
                share[b, t, c] = (share[b, t, c].astype(F32) + piece).astype(BF16)
                share_copy(b, t, way, c).start()

            @pl.when(t == s)
            def _():
                retained[b, c] -= piece

    def chain(b, begin, end):
        def one(j, carry):
            for way, lag in ((RIGHT, s), (LEFT, steps - s)):
                c = j - lag
                here = both(receives[way], c >= 0, c < cells)
                near = both(near_end[way], c < moved)
                if moved:

                    @pl.when(both(here, near))
                    def _():
                        absorb_near(b, way, c)

                @pl.when(both(here, jnp.logical_not(near)))
                def _():
                    absorb(b, way, c)

            c = j - last_step

            @pl.when(both(c >= 0, c < cells))
            def _():
                alive = jnp.where(c < count, 1.0, 0.0).astype(BF16)
                out_ref[b, c] = retained[b, c].astype(BF16) * alive

            return carry

        lax.fori_loop(begin, end, one, 0)


    for b in range(blocks):
        part[b] = jnp.zeros(part.shape[1:], F32)
    for b in range(blocks):
        operator_begin(0, b)
        if b == 0:
            relayout()
            near_start(0)
    for b in range(blocks):
        operator_end(0, b)
        operator_begin(1, b)
    for b in range(blocks):
        operator_end(1, b)
        if b == 0:
            for k in range(sts):
                gather_start(0, k)
            near_start(1)
        if b == 1:
            gather_start(1, 0)
    for c in range(2, moved):
        near_start(c)

    half = cells // 2
    whole = steps * cells
    links = cells + steps
    cut_one, cut_two = links // 3 + 2, links // 3 + 5
    gather_flat(0, 0, whole)
    reduce_start(0)
    for b in range(blocks):
        following, previous = b + 1 < blocks, b > 0
        if following:
            gather_flat(b + 1, 0, half)
        if previous:
            chain(b - 1, 0, cut_one)
        reduce_middle(b)
        if following:
            gather_flat(b + 1, half, cells)
        if previous:
            chain(b - 1, cut_one, cut_two)
        reduce_end(b)
        coefficients(b)
        coef_start(b)
        share_start(b)
        if previous:
            chain(b - 1, cut_two, links)
        retain(b)
        if following:
            gather_flat(b + 1, cells, whole)
            reduce_start(b + 1)
    chain(blocks - 1, 0, links)

    for there, make in pending:

        @pl.when(there)
        def _():
            make().wait_send()

    for b in range(blocks):
        gather_drain(b)
        reduce_drain(b)
        share_drain(b)


def on_device(start_block, resident, stiffness, cell_scale, potential, cell_count, face_index):
    blocks, cells, width, nodes = start_block.shape
    res = resident.shape[0]
    face = face_index.shape[2]
    doms, sts = lax.axis_size("dom"), lax.axis_size("st")
    total_states = sts * width
    rows = -(-(res + total_states) // (16 * doms)) * 16
    moved = 3 * cells // 8 if sts > 3 else 0
    sizes = (doms, sts, blocks, cells, width, nodes, face, res, rows, moved)
    near = max(moved, 1)
    dma = pltpu.SemaphoreType.DMA
    vmem = pl.BlockSpec(memory_space=pltpu.VMEM)
    smem = pl.BlockSpec(memory_space=pltpu.SMEM)
    return pl.pallas_call(
        partial(kernel, sizes),
        out_shape=jax.ShapeDtypeStruct((blocks, cells, width, nodes), BF16),
        in_specs=[smem, smem, vmem, pl.BlockSpec(memory_space=pl.ANY), vmem, vmem, vmem],
        out_specs=vmem,
        scratch_shapes=[
            pltpu.VMEM((blocks, cells * width, nodes), F32),
            pltpu.VMEM((blocks, cells * width, nodes), BF16),
            pltpu.VMEM((blocks, cells, total_states, nodes), BF16),
            pltpu.VMEM((blocks, doms * rows, total_states), F32),
            pltpu.VMEM((blocks, doms * rows, total_states), WIRE),
            pltpu.VMEM((blocks, doms, rows, total_states), WIRE),
            pltpu.VMEM((blocks, doms * rows, total_states), WIRE),
            pltpu.VMEM((blocks, total_states, total_states), BF16),
            pltpu.VMEM((blocks, total_states, res), BF16),
            pltpu.VMEM((blocks, sts, cells, width, nodes), BF16),
            pltpu.VMEM((2, blocks, sts, cells, width, nodes), BF16),
            pltpu.VMEM((nodes, cells, res), BF16),
            pltpu.VMEM((res // 128, face * cells, 128), F32),
            pltpu.VMEM((cells, nodes, res), BF16),
            pltpu.VMEM((2, near, nodes, res), BF16),
            pltpu.VMEM((2, blocks, total_states, res), BF16),
            pltpu.VMEM((blocks, cells, width, nodes), F32),
            pltpu.VMEM((2, blocks, 2, width, face), F32),
            pltpu.VMEM((2, blocks, 2, width, face), F32),
            dma((2, blocks, 2)),
            dma((2, blocks, 2)),
            dma((blocks, 2, sts)),
            dma((blocks, sts, cells)),
            dma((blocks, doms)),
            dma((blocks, doms)),
            dma((blocks, doms)),
            dma((blocks, doms)),
            dma((blocks, sts)),
            dma((2, blocks, sts, cells)),
            dma,
            dma((2, near)),
            dma((2, near)),
            dma((2, blocks)),
            dma((2, blocks)),
        ],
        compiler_params=pltpu.CompilerParams(
            collective_id=0, has_side_effects=True, vmem_limit_bytes=60 * 1024 * 1024
        ),
    )(
        cell_scale,
        cell_count,
        start_block,
        jnp.transpose(resident, (2, 1, 0)),
        stiffness,
        potential,
        face_index,
    )


def solution(mesh):
    return jax.shard_map(
        on_device,
        mesh=mesh,
        in_specs=(
            P(None, "dom", "st", None),
            P("st", "dom", None),
            P(),
            P("dom"),
            P("dom", None),
            P("dom"),
            P("dom", None, None),
        ),
        out_specs=P(None, "dom", "st", None),
        check_vma=False,
    )
```

```python
from functools import partial

import jax
import jax.numpy as jnp
from jax import lax
from jax.experimental import pallas as pl
from jax.experimental.pallas import tpu as pltpu
from jax.sharding import PartitionSpec as P

CENTER = 0.5
HALF_WIDTH = 2.0
EPSILON = 1e-06
F32 = jnp.float32
BF16 = jnp.bfloat16
WIRE = BF16
RIGHT, LEFT = 0, 1
LAG = 3
MESH = pl.DeviceIdType.MESH


def dot_nn(a, b, precision=None):
    return lax.dot_general(
        a, b, (((1,), (0,)), ((), ())), precision=precision, preferred_element_type=F32
    )


def dot_nt(a, b, precision=None):
    return lax.dot_general(
        a, b, (((1,), (1,)), ((), ())), precision=precision, preferred_element_type=F32
    )


def both(*conditions):
    found = conditions[0]
    for condition in conditions[1:]:
        found = jnp.logical_and(found, condition)
    return found


def kernel(
    sizes,
    scale_ref,
    count_ref,
    start_hbm,
    res_hbm,
    stiff_hbm,
    pot_ref,
    face_ref,
    out_hbm,
    start_ref,
    stiff_ref,
    out_ref,
    local,
    inner,
    states,
    part,
    wire,
    part_recv,
    total,
    mix,
    proj,
    share,
    share_recv,
    res_in,
    res_wide,
    res_ref,
    res_near,
    proj_near,
    retained,
    face_out,
    face_in,
    face_send_sem,
    face_recv_sem,
    gather_send_sem,
    gather_recv_sem,
    one_send_sem,
    one_recv_sem,
    two_send_sem,
    two_recv_sem,
    share_send_sem,
    share_recv_sem,
    load_sem,
    start_sem,
    stiff_sem,
    out_sem,
    near_send_sem,
    near_recv_sem,
    coef_send_sem,
    coef_recv_sem,
):
    doms, sts, blocks, cells, width, nodes, face, res, rows, moved = sizes
    total_states = sts * width
    total_nodes = float(doms * cells * nodes)
    window = (nodes - face) // 128 * 128
    offset = nodes - face - window
    d = lax.axis_index("dom")
    s = lax.axis_index("st")
    has_right, has_left = s < sts - 1, s > 0
    has_next, has_prev = d < doms - 1, d > 0
    own = pl.ds(pl.multiple_of(s * width, width), width)
    steps = sts - 1
    last_step = jnp.maximum(s, steps - s)
    ends = jnp.logical_or(s == 0, s == steps)
    pending = []
    count = count_ref[0]
    scale = [scale_ref[c] for c in range(cells)]
    live = [jnp.where(c < count, 1.0, 0.0).astype(F32) for c in range(cells)]
    last = [jnp.where(c == count - 1, 1.0, 0.0).astype(F32) for c in range(cells)]

    def start_load(b):
        return pltpu.make_async_copy(start_hbm.at[b], start_ref.at[b], start_sem.at[b])

    def cuts(extent, number):
        step = -(-extent // (number * 16)) * 16
        return [pl.ds(at, min(step, extent - at)) for at in range(0, extent, step)]

    def stiff_load(i):
        at = cuts(nodes, 2)[i]
        return pltpu.make_async_copy(stiff_hbm.at[at], stiff_ref.at[at], stiff_sem.at[i])

    def res_load(i):
        at = cuts(nodes, 4)[i]
        return pltpu.make_async_copy(res_hbm.at[at], res_in.at[at], load_sem.at[i])

    start_load(0).start()
    for i in range(2):
        stiff_load(i).start()
    for b in range(1, blocks):
        start_load(b).start()
    for i in range(4):
        res_load(i).start()

    origin = {RIGHT: s == 0, LEFT: s == steps}
    lag = {RIGHT: LAG * jnp.maximum(s - 1, 0), LEFT: LAG * jnp.maximum(steps - 1 - s, 0)}
    sends = {RIGHT: has_right, LEFT: has_left}
    receives = {RIGHT: has_left, LEFT: has_right}
    near_end = {RIGHT: s == 1, LEFT: s == steps - 1}

    def to(way):
        return s + 1 if way == RIGHT else s - 1

    def dom_peer(k):
        return lax.rem(d + k, doms)

    barrier = pltpu.get_barrier_semaphore()

    def greet(k, carry):
        pl.semaphore_signal(barrier, inc=1, device_id={"dom": dom_peer(k)}, device_id_type=MESH)
        return carry

    lax.fori_loop(1, doms, greet, 0)
    for way in (RIGHT, LEFT):

        @pl.when(sends[way])
        def _():
            pl.semaphore_signal(barrier, inc=1, device_id={"st": to(way)}, device_id_type=MESH)

    neighbours = has_right.astype(jnp.int32) + has_left.astype(jnp.int32)
    pl.semaphore_wait(barrier, doms - 1 + neighbours)

    def remote(src, dst, send_sem, recv_sem, axis, peer):
        return pltpu.make_async_remote_copy(
            src_ref=src,
            dst_ref=dst,
            send_sem=send_sem,
            recv_sem=recv_sem,
            device_id={axis: peer},
            device_id_type=MESH,
        )

    def one_hot(row, first, extent):
        node = lax.broadcasted_iota(jnp.int32, (extent, face), 0) + first
        if row == 0:
            node = node + (count - 1) * nodes
        return jnp.where(face_ref[0, row : row + 1, :] == node, 1.0, 0.0).astype(F32)

    def mask(c):
        return live[c].astype(BF16)

    def relayout():
        for i in range(4):
            res_load(i).wait()
        for chunk in range(nodes // face):
            at = slice(chunk * face, (chunk + 1) * face)
            wide = res_in[at].astype(F32).reshape(face * cells, res)
            for h in range(res // 128):
                lanes = slice(h * 128, (h + 1) * 128)
                res_wide[h] = wide[:, lanes]
                for c in range(cells):
                    res_ref[c, at, lanes] = res_wide[h, pl.ds(c, face, stride=cells), :].astype(BF16)


    def rows_of(c):
        return slice(c * width, (c + 1) * width)

    def face_copy(step, b, way):
        return remote(
            face_out.at[step, b, way],
            face_in.at[step, b, way],
            face_send_sem.at[step, b, way],
            face_recv_sem.at[step, b, way],
            "dom",
            d + 1 if way == RIGHT else d - 1,
        )

    def first(b, c):
        if c is None:
            return jnp.concatenate([first(b, i) for i in range(cells)], axis=0)
        return start_ref[b, c] * mask(c)

    def second(b, c):
        return inner[b] if c is None else inner[b, rows_of(c), :]

    def operator_begin(step, b):
        field = partial(second if step else first, b)
        local[b] = dot_nn(field(None), stiff_ref[...])
        last_tail = jnp.zeros((width, nodes - window), F32)
        for c in range(cells):
            value = scale[c] * local[b, rows_of(c), :] + pot_ref[c : c + 1, :] * field(c).astype(F32)
            local[b, rows_of(c), :] = value
            last_tail = last_tail + last[c] * value[:, window:]
        face_out[step, b, RIGHT] = dot_nn(
            last_tail, one_hot(0, window, nodes - window), lax.Precision.HIGHEST
        )
        face_out[step, b, LEFT] = dot_nn(
            local[b, rows_of(0), :face], one_hot(1, 0, face), lax.Precision.HIGHEST
        )
        for way, there in ((RIGHT, has_next), (LEFT, has_prev)):

            @pl.when(there)
            def _():
                face_copy(step, b, way).start()

            pending.append((there, partial(face_copy, step, b, way)))
        for c in range(cells - 1):
            pair = live[c + 1]
            tail = local[b, rows_of(c), window:]
            head = local[b, rows_of(c + 1), :face]
            padded = head
            if offset:
                padded = jnp.concatenate([jnp.zeros((width, offset), F32), head], axis=1)
            local[b, rows_of(c), window:] = tail + pair * padded
            local[b, rows_of(c + 1), :face] = head + pair * tail[:, offset:]

    def operator_end(step, b):
        for way, source in ((RIGHT, has_prev), (LEFT, has_next)):

            @pl.when(source)
            def _():
                face_copy(step, b, way).wait_recv()

            @pl.when(jnp.logical_not(source))
            def _():
                face_in[step, b, way] = jnp.zeros((width, face), F32)

        local[b, rows_of(0), :face] += dot_nt(
            face_in[step, b, RIGHT], one_hot(1, 0, face), lax.Precision.HIGHEST
        )
        tail_add = dot_nt(
            face_in[step, b, LEFT], one_hot(0, window, nodes - window), lax.Precision.HIGHEST
        )
        for c in range(cells):
            local[b, rows_of(c), window:] += last[c] * tail_add
        for c in range(cells):
            value = live[c] * local[b, rows_of(c), :]
            if step == 0:
                inner[b, rows_of(c), :] = (
                    (value - CENTER * first(b, c).astype(F32)) / HALF_WIDTH
                ).astype(BF16)
            else:
                states[b, c, own, :] = (
                    2.0 * (value - CENTER * second(b, c).astype(F32)) / HALF_WIDTH
                    - first(b, c).astype(F32)
                ).astype(BF16)


    def of_shard(shard):
        return pl.ds(pl.multiple_of(shard * width, width), width)

    def gather_copy(b, way, shard, c):
        at = states.at[b, c, of_shard(shard), :]
        return remote(
            at, at, gather_send_sem.at[b, way, shard], gather_recv_sem.at[b, shard, c], "st", to(way)
        )

    def gather_whole(b, way, shard):
        at = states.at[b, :, of_shard(shard), :]
        return remote(
            at, at, gather_send_sem.at[b, way, shard], gather_recv_sem.at[b, shard, 0], "st", to(way)
        )

    def gather_own(b, way, there):
        @pl.when(both(there, sends[way]))
        def _():
            def one(c, carry):
                gather_copy(b, way, s, c).start()
                return carry

            lax.fori_loop(0, cells, one, 0)

    def gather_start(b, k):
        gather_own(b, RIGHT, s == k)
        gather_own(b, LEFT, s + k == steps)

    def gather_flat(b, begin, end):
        def one(i, carry):
            k = lax.div(i, cells) + 1
            c = lax.rem(i, cells)
            for way, shard, here in ((LEFT, s + k, s + k < sts), (RIGHT, s - k, s >= k)):

                @pl.when(here)
                def _():
                    gather_copy(b, way, shard, c).wait_recv()

                    @pl.when(sends[way])
                    def _():
                        gather_copy(b, way, shard, c).start()

            @pl.when(k == last_step)
            def _():
                contract(b, c)

            if b + 1 < blocks:

                @pl.when(c == cells - 1)
                def _():
                    gather_start(b + 1, k)

            return carry

        lax.fori_loop(begin, end, one, 0)

    def gather_drain(b):
        def one(shard, carry):
            for way, passed in ((RIGHT, shard <= s), (LEFT, shard >= s)):

                @pl.when(both(passed, sends[way]))
                def _():
                    gather_whole(b, way, shard).wait_send()

            return carry

        lax.fori_loop(0, sts, one, 0)


    def contract(b, c):
        block = states[b, c]
        found = dot_nn(block, res_ref[c])
        for h in range(res // total_states):
            at = slice(h * total_states, (h + 1) * total_states)
            part[b, at, :] += found[:, at]
        part[b, res : res + total_states, :] += dot_nt(block, block)

    def slice_of(peer):
        return pl.ds(pl.multiple_of(peer * rows, 16), rows)

    def one_copy(b, k):
        peer = dom_peer(k)
        return remote(
            wire.at[b, slice_of(peer)],
            part_recv.at[b, k],
            one_send_sem.at[b, k],
            one_recv_sem.at[b, k],
            "dom",
            peer,
        )

    def two_copy(b, k):
        at = total.at[b, slice_of(d)]
        return remote(at, at, two_send_sem.at[b, k], two_recv_sem.at[b, k], "dom", dom_peer(k))

    def from_peer(b, k):
        peer = dom_peer(doms - k)
        at = total.at[b, slice_of(peer)]
        return remote(at, at, two_send_sem.at[b, k], two_recv_sem.at[b, k], "dom", peer)

    def peers(body):
        def step(k, carry):
            body(k)
            return carry

        lax.fori_loop(1, doms, step, 0)

    def reduce_start(b):
        wire[b] = part[b].astype(WIRE)
        peers(lambda k: one_copy(b, k).start())

    def reduce_middle(b):
        def add(k, found):
            one_copy(b, k).wait_recv()
            return found + part_recv[b, k].astype(F32)

        found = lax.fori_loop(1, doms, add, part[b, slice_of(d), :])
        total[b, slice_of(d), :] = found.astype(WIRE)
        peers(lambda k: two_copy(b, k).start())

    def reduce_end(b):
        peers(lambda k: from_peer(b, k).wait_recv())

    def reduce_drain(b):
        def one(k):
            one_copy(b, k).wait_send()
            two_copy(b, k).wait_send()

        peers(one)

    def coefficients(b):
        gram = total[b, res : res + total_states, :].astype(F32)
        shape = (total_states, total_states)
        eye = (
            lax.broadcasted_iota(jnp.int32, shape, 0) == lax.broadcasted_iota(jnp.int32, shape, 1)
        ).astype(F32)
        along = jnp.sum(gram * eye, axis=0, keepdims=True) / total_nodes + EPSILON
        down = jnp.sum(gram * eye, axis=1, keepdims=True) / total_nodes + EPSILON
        root_i, root_j = lax.rsqrt(along), lax.rsqrt(down)
        mixing = root_i * (1.5 * eye - 0.5 * (gram * root_i * root_j / total_nodes))
        mix[b] = mixing.astype(BF16)
        for h in range(res // total_states):
            at = slice(h * total_states, (h + 1) * total_states)
            proj[b, :, at] = dot_nn(
                mixing, total[b, at, :].astype(F32), lax.Precision.HIGHEST
            ).astype(BF16)


    def near_copy(way, c):
        return remote(
            res_ref.at[c],
            res_near.at[way, c],
            near_send_sem.at[way, c],
            near_recv_sem.at[way, c],
            "st",
            to(way),
        )

    def near_start(c):
        if c >= moved:
            return
        for way in (RIGHT, LEFT):
            there = both(origin[way], sends[way])

            @pl.when(there)
            def _():
                near_copy(way, c).start()

            pending.append((there, partial(near_copy, way, c)))

    def coef_copy(b, way):
        return remote(
            proj.at[b],
            proj_near.at[way, b],
            coef_send_sem.at[way, b],
            coef_recv_sem.at[way, b],
            "st",
            to(way),
        )

    def coef_start(b):
        if not moved:
            return
        for way in (RIGHT, LEFT):
            there = both(origin[way], sends[way])

            @pl.when(there)
            def _():
                coef_copy(b, way).start()

            pending.append((there, partial(coef_copy, b, way)))


    def share_copy(b, t, way, c):
        return remote(
            share.at[b, t, c],
            share_recv.at[way, b, t, c],
            share_send_sem.at[b, t],
            share_recv_sem.at[way, b, t, c],
            "st",
            to(way),
        )

    def share_whole(b, t, way, begin):
        at = pl.ds(begin, cells - begin)
        return remote(
            share.at[b, t, at],
            share_recv.at[way, b, t, at],
            share_send_sem.at[b, t],
            share_recv_sem.at[way, b, t, 0],
            "st",
            to(way),
        )

    def ahead(way):
        if way == RIGHT:
            return steps - s, lambda i: steps - i
        return s, lambda i: i

    def share_cell(b, c):
        found = dot_nt(proj[b], res_ref[c])
        for t in range(sts):
            piece = found[t * width : (t + 1) * width, :]
            share[b, t, c] = piece.astype(BF16)

            @pl.when(t == s)
            def _():
                retained[b, c] = -piece

    def retain(b, c):
        retained[b, c] += dot_nn(mix[b, own, :], states[b, c])

    def share_start(b):
        def one(i, carry):
            c = lax.rem(i + moved, cells)
            share_cell(b, c)
            for way in (RIGHT, LEFT):

                @pl.when(both(origin[way], c >= moved))
                def _():
                    number, target = ahead(way)

                    def send(i, carry):
                        share_copy(b, target(i), way, c).start()
                        return carry

                    lax.fori_loop(0, number, send, 0)

            retain(b, c)
            return carry

        @pl.when(ends)
        def _():
            lax.fori_loop(0, cells, one, 0)

    def share_drain(b):
        def one(t, carry):
            for way, passed in ((RIGHT, t > s), (LEFT, t < s)):

                @pl.when(both(passed, origin[way]))
                def _():
                    share_whole(b, t, way, moved).wait_send()

                @pl.when(both(passed, jnp.logical_not(origin[way])))
                def _():
                    share_whole(b, t, way, 0).wait_send()

            return carry

        lax.fori_loop(0, sts, one, 0)

    def absorb(b, way, c):
        number, target = ahead(way)

        def one(i, carry):
            t = target(i)
            share_copy(b, t, way, c).wait_recv()
            share[b, t, c] = (
                share[b, t, c].astype(F32) + share_recv[way, b, t, c].astype(F32)
            ).astype(BF16)
            share_copy(b, t, way, c).start()
            return carry

        lax.fori_loop(0, number, one, 0)
        share_copy(b, s, way, c).wait_recv()
        retained[b, c] -= share_recv[way, b, s, c].astype(F32)

    def absorb_near(b, way, c):
        if b == 0:
            near_copy(way, c).wait_recv()

        @pl.when(c == 0)
        def _():
            coef_copy(b, way).wait_recv()

        found = dot_nt(proj_near[way, b], res_near[way, c])
        for t in reversed(range(sts)) if way == RIGHT else range(sts):
            piece = found[t * width : (t + 1) * width, :]

            @pl.when(t > s if way == RIGHT else t < s)
            def _():
                share[b, t, c] = (share[b, t, c].astype(F32) + piece).astype(BF16)
                share_copy(b, t, way, c).start()

            @pl.when(t == s)
            def _():
                retained[b, c] -= piece

    def chain(b, begin, end):
        def one(j, carry):
            c = j

            @pl.when(both(jnp.logical_not(ends), c >= 0, c < cells))
            def _():
                share_cell(b, c)
                retain(b, c)

            for way in (RIGHT, LEFT):
                c = j - lag[way]
                here = both(receives[way], c >= 0, c < cells)
                near = both(near_end[way], c < moved)
                if moved:

                    @pl.when(both(here, near))
                    def _():
                        absorb_near(b, way, c)

                @pl.when(both(here, jnp.logical_not(near)))
                def _():
                    absorb(b, way, c)

            c = j - jnp.maximum(lag[RIGHT], lag[LEFT])

            @pl.when(both(c >= 0, c < cells))
            def _():
                alive = jnp.where(c < count, 1.0, 0.0).astype(BF16)
                out_ref[b, c] = retained[b, c].astype(BF16) * alive
                pltpu.make_async_copy(out_ref.at[b, c], out_hbm.at[b, c], out_sem.at[b]).start()

            return carry

        lax.fori_loop(begin, end, one, 0)


    for b in range(blocks):
        part[b] = jnp.zeros(part.shape[1:], F32)
    start_load(0).wait()
    for i in range(2):
        stiff_load(i).wait()
    for b in range(blocks):
        if b:
            start_load(b).wait()
        operator_begin(0, b)
        if b == 0:
            relayout()
            near_start(0)
    for b in range(blocks):
        operator_end(0, b)
        operator_begin(1, b)
    for b in range(blocks):
        operator_end(1, b)
        if b == 0:
            for k in range(sts):
                gather_start(0, k)
            near_start(1)
        if b == 1:
            gather_start(1, 0)
    for c in range(2, moved):
        near_start(c)

    half = cells // 2
    whole = steps * cells
    furthest = LAG * max(steps - 1, 0)
    links = cells + furthest
    cut_one, cut_two = furthest + 2, furthest + 6
    gather_flat(0, 0, whole)
    reduce_start(0)
    for b in range(blocks):
        following, previous = b + 1 < blocks, b > 0
        if following:
            gather_flat(b + 1, 0, half)
        if previous:
            chain(b - 1, 0, cut_one)
        reduce_middle(b)
        if following:
            gather_flat(b + 1, half, cells)
        if previous:
            chain(b - 1, cut_one, cut_two)
        reduce_end(b)
        coefficients(b)
        coef_start(b)
        share_start(b)
        if previous:
            chain(b - 1, cut_two, links)
        if following:
            gather_flat(b + 1, cells, whole)
            reduce_start(b + 1)
    chain(blocks - 1, 0, links)

    for there, make in pending:

        @pl.when(there)
        def _():
            make().wait_send()

    for b in range(blocks):
        gather_drain(b)
        reduce_drain(b)
        share_drain(b)
        pltpu.make_async_copy(out_ref.at[b], out_hbm.at[b], out_sem.at[b]).wait()


def on_device(start_block, resident, stiffness, cell_scale, potential, cell_count, face_index):
    blocks, cells, width, nodes = start_block.shape
    res = resident.shape[0]
    face = face_index.shape[2]
    doms, sts = lax.axis_size("dom"), lax.axis_size("st")
    total_states = sts * width
    rows = -(-(res + total_states) // (16 * doms)) * 16
    moved = 3 * cells // 8 if sts > 3 else 0
    sizes = (doms, sts, blocks, cells, width, nodes, face, res, rows, moved)
    near = max(moved, 1)
    dma = pltpu.SemaphoreType.DMA
    vmem = pl.BlockSpec(memory_space=pltpu.VMEM)
    smem = pl.BlockSpec(memory_space=pltpu.SMEM)
    anywhere = pl.BlockSpec(memory_space=pl.ANY)
    return pl.pallas_call(
        partial(kernel, sizes),
        out_shape=jax.ShapeDtypeStruct((blocks, cells, width, nodes), BF16),
        in_specs=[smem, smem, anywhere, anywhere, anywhere, vmem, vmem],
        out_specs=anywhere,
        scratch_shapes=[
            pltpu.VMEM((blocks, cells, width, nodes), BF16),
            pltpu.VMEM((nodes, nodes), BF16),
            pltpu.VMEM((blocks, cells, width, nodes), BF16),
            pltpu.VMEM((blocks, cells * width, nodes), F32),
            pltpu.VMEM((blocks, cells * width, nodes), BF16),
            pltpu.VMEM((blocks, cells, total_states, nodes), BF16),
            pltpu.VMEM((blocks, doms * rows, total_states), F32),
            pltpu.VMEM((blocks, doms * rows, total_states), WIRE),
            pltpu.VMEM((blocks, doms, rows, total_states), WIRE),
            pltpu.VMEM((blocks, doms * rows, total_states), WIRE),
            pltpu.VMEM((blocks, total_states, total_states), BF16),
            pltpu.VMEM((blocks, total_states, res), BF16),
            pltpu.VMEM((blocks, sts, cells, width, nodes), BF16),
            pltpu.VMEM((2, blocks, sts, cells, width, nodes), BF16),
            pltpu.VMEM((nodes, cells, res), BF16),
            pltpu.VMEM((res // 128, face * cells, 128), F32),
            pltpu.VMEM((cells, nodes, res), BF16),
            pltpu.VMEM((2, near, nodes, res), BF16),
            pltpu.VMEM((2, blocks, total_states, res), BF16),
            pltpu.VMEM((blocks, cells, width, nodes), F32),
            pltpu.VMEM((2, blocks, 2, width, face), F32),
            pltpu.VMEM((2, blocks, 2, width, face), F32),
            dma((2, blocks, 2)),
            dma((2, blocks, 2)),
            dma((blocks, 2, sts)),
            dma((blocks, sts, cells)),
            dma((blocks, doms)),
            dma((blocks, doms)),
            dma((blocks, doms)),
            dma((blocks, doms)),
            dma((blocks, sts)),
            dma((2, blocks, sts, cells)),
            dma((4,)),
            dma((blocks,)),
            dma((2,)),
            dma((blocks,)),
            dma((2, near)),
            dma((2, near)),
            dma((2, blocks)),
            dma((2, blocks)),
        ],
        compiler_params=pltpu.CompilerParams(
            collective_id=0, has_side_effects=True, vmem_limit_bytes=60 * 1024 * 1024
        ),
    )(
        cell_scale,
        cell_count,
        start_block,
        jnp.transpose(resident, (2, 1, 0)),
        stiffness,
        potential,
        face_index,
    )


def solution(mesh):
    return jax.shard_map(
        on_device,
        mesh=mesh,
        in_specs=(
            P(None, "dom", "st", None),
            P("st", "dom", None),
            P(),
            P("dom"),
            P("dom", None),
            P("dom"),
            P("dom", None, None),
        ),
        out_specs=P(None, "dom", "st", None),
        check_vma=False,
    )
```

```python
from functools import partial

import jax
import jax.numpy as jnp
from jax import lax
from jax.experimental import pallas as pl
from jax.experimental.pallas import tpu as pltpu
from jax.sharding import PartitionSpec as P

CENTER = 0.5
HALF_WIDTH = 2.0
EPSILON = 1e-06
F32 = jnp.float32
BF16 = jnp.bfloat16
WIRE = BF16
RIGHT, LEFT = 0, 1
LAG = 6
MESH = pl.DeviceIdType.MESH


def dot_nn(a, b, precision=None):
    return lax.dot_general(
        a, b, (((1,), (0,)), ((), ())), precision=precision, preferred_element_type=F32
    )


def dot_nt(a, b, precision=None):
    return lax.dot_general(
        a, b, (((1,), (1,)), ((), ())), precision=precision, preferred_element_type=F32
    )


def both(*conditions):
    found = conditions[0]
    for condition in conditions[1:]:
        found = jnp.logical_and(found, condition)
    return found


def kernel(
    sizes,
    scale_ref,
    count_ref,
    start_hbm,
    res_hbm,
    stiff_hbm,
    pot_ref,
    face_ref,
    out_hbm,
    start_ref,
    stiff_ref,
    out_ref,
    local,
    inner,
    states,
    part,
    wire,
    part_recv,
    total,
    mix,
    proj,
    share,
    share_recv,
    res_in,
    res_wide,
    res_ref,
    res_near,
    proj_near,
    retained,
    near_part,
    near_wire,
    near_got,
    near_term,
    face_out,
    face_in,
    face_send_sem,
    face_recv_sem,
    gather_send_sem,
    gather_recv_sem,
    one_send_sem,
    one_recv_sem,
    two_send_sem,
    two_recv_sem,
    share_send_sem,
    share_recv_sem,
    load_sem,
    start_sem,
    stiff_sem,
    out_sem,
    near_send_sem,
    near_recv_sem,
    coef_send_sem,
    coef_recv_sem,
    give_send_sem,
    give_recv_sem,
):
    doms, sts, blocks, cells, width, nodes, face, res, rows, moved, given = sizes
    total_states = sts * width
    total_nodes = float(doms * cells * nodes)
    window = (nodes - face) // 128 * 128
    offset = nodes - face - window
    d = lax.axis_index("dom")
    s = lax.axis_index("st")
    has_right, has_left = s < sts - 1, s > 0
    has_next, has_prev = d < doms - 1, d > 0
    own = pl.ds(pl.multiple_of(s * width, width), width)
    steps = sts - 1
    last_step = jnp.maximum(s, steps - s)
    ends = jnp.logical_or(s == 0, s == steps)
    pending = []
    count = count_ref[0]
    scale = [scale_ref[c] for c in range(cells)]
    live = [jnp.where(c < count, 1.0, 0.0).astype(F32) for c in range(cells)]
    last = [jnp.where(c == count - 1, 1.0, 0.0).astype(F32) for c in range(cells)]

    def start_load(b):
        return pltpu.make_async_copy(start_hbm.at[b], start_ref.at[b], start_sem.at[b])

    def cuts(extent, number):
        step = -(-extent // (number * 16)) * 16
        return [pl.ds(at, min(step, extent - at)) for at in range(0, extent, step)]

    def stiff_load(i):
        at = cuts(nodes, 2)[i]
        return pltpu.make_async_copy(stiff_hbm.at[at], stiff_ref.at[at], stiff_sem.at[i])

    def res_load(i):
        at = cuts(nodes, 4)[i]
        return pltpu.make_async_copy(res_hbm.at[at], res_in.at[at], load_sem.at[i])

    start_load(0).start()
    for i in range(2):
        stiff_load(i).start()
    for b in range(1, blocks):
        start_load(b).start()
    for i in range(4):
        res_load(i).start()

    origin = {RIGHT: s == 0, LEFT: s == steps}
    lag = {RIGHT: LAG * jnp.maximum(s - 1, 0), LEFT: LAG * jnp.maximum(steps - 1 - s, 0)}
    done_at = jnp.maximum(
        jnp.where(s > 0, lag[RIGHT] + (steps - s) * cells, 0),
        jnp.where(s < steps, lag[LEFT] + s * cells, 0),
    )
    sends = {RIGHT: has_right, LEFT: has_left}
    receives = {RIGHT: has_left, LEFT: has_right}
    near_end = {RIGHT: s == 1, LEFT: s == steps - 1}
    to_end = {RIGHT: s == steps - 1, LEFT: s == 1}

    def to(way):
        return s + 1 if way == RIGHT else s - 1

    def dom_peer(k):
        return lax.rem(d + k, doms)

    barrier = pltpu.get_barrier_semaphore()

    def greet(k, carry):
        pl.semaphore_signal(barrier, inc=1, device_id={"dom": dom_peer(k)}, device_id_type=MESH)
        return carry

    lax.fori_loop(1, doms, greet, 0)
    for way in (RIGHT, LEFT):

        @pl.when(sends[way])
        def _():
            pl.semaphore_signal(barrier, inc=1, device_id={"st": to(way)}, device_id_type=MESH)

    neighbours = has_right.astype(jnp.int32) + has_left.astype(jnp.int32)
    pl.semaphore_wait(barrier, doms - 1 + neighbours)

    def remote(src, dst, send_sem, recv_sem, axis, peer):
        return pltpu.make_async_remote_copy(
            src_ref=src,
            dst_ref=dst,
            send_sem=send_sem,
            recv_sem=recv_sem,
            device_id={axis: peer},
            device_id_type=MESH,
        )

    def one_hot(row, first, extent):
        node = lax.broadcasted_iota(jnp.int32, (extent, face), 0) + first
        if row == 0:
            node = node + (count - 1) * nodes
        return jnp.where(face_ref[0, row : row + 1, :] == node, 1.0, 0.0).astype(F32)

    def mask(c):
        return live[c].astype(BF16)

    def relayout():
        for i in range(4):
            res_load(i).wait()
        for chunk in range(nodes // face):
            at = slice(chunk * face, (chunk + 1) * face)
            wide = res_in[at].astype(F32).reshape(face * cells, res)
            for h in range(res // 128):
                lanes = slice(h * 128, (h + 1) * 128)
                res_wide[h] = wide[:, lanes]
                for c in range(cells):
                    res_ref[c, at, lanes] = res_wide[h, pl.ds(c, face, stride=cells), :].astype(BF16)


    def rows_of(c):
        return slice(c * width, (c + 1) * width)

    def face_copy(step, b, way):
        return remote(
            face_out.at[step, b, way],
            face_in.at[step, b, way],
            face_send_sem.at[step, b, way],
            face_recv_sem.at[step, b, way],
            "dom",
            d + 1 if way == RIGHT else d - 1,
        )

    def first(b, c):
        if c is None:
            return jnp.concatenate([first(b, i) for i in range(cells)], axis=0)
        return start_ref[b, c] * mask(c)

    def second(b, c):
        return inner[b] if c is None else inner[b, rows_of(c), :]

    def operator_begin(step, b):
        field = partial(second if step else first, b)
        local[b] = dot_nn(field(None), stiff_ref[...])
        last_tail = jnp.zeros((width, nodes - window), F32)
        for c in range(cells):
            value = scale[c] * local[b, rows_of(c), :] + pot_ref[c : c + 1, :] * field(c).astype(F32)
            local[b, rows_of(c), :] = value
            last_tail = last_tail + last[c] * value[:, window:]
        face_out[step, b, RIGHT] = dot_nn(
            last_tail, one_hot(0, window, nodes - window), lax.Precision.HIGHEST
        )
        face_out[step, b, LEFT] = dot_nn(
            local[b, rows_of(0), :face], one_hot(1, 0, face), lax.Precision.HIGHEST
        )
        for way, there in ((RIGHT, has_next), (LEFT, has_prev)):

            @pl.when(there)
            def _():
                face_copy(step, b, way).start()

            pending.append((there, partial(face_copy, step, b, way)))
        for c in range(cells - 1):
            pair = live[c + 1]
            tail = local[b, rows_of(c), window:]
            head = local[b, rows_of(c + 1), :face]
            padded = head
            if offset:
                padded = jnp.concatenate([jnp.zeros((width, offset), F32), head], axis=1)
            local[b, rows_of(c), window:] = tail + pair * padded
            local[b, rows_of(c + 1), :face] = head + pair * tail[:, offset:]

    def operator_end(step, b):
        for way, source in ((RIGHT, has_prev), (LEFT, has_next)):

            @pl.when(source)
            def _():
                face_copy(step, b, way).wait_recv()

            @pl.when(jnp.logical_not(source))
            def _():
                face_in[step, b, way] = jnp.zeros((width, face), F32)

        local[b, rows_of(0), :face] += dot_nt(
            face_in[step, b, RIGHT], one_hot(1, 0, face), lax.Precision.HIGHEST
        )
        tail_add = dot_nt(
            face_in[step, b, LEFT], one_hot(0, window, nodes - window), lax.Precision.HIGHEST
        )
        for c in range(cells):
            local[b, rows_of(c), window:] += last[c] * tail_add
        for c in range(cells):
            value = live[c] * local[b, rows_of(c), :]
            if step == 0:
                inner[b, rows_of(c), :] = (
                    (value - CENTER * first(b, c).astype(F32)) / HALF_WIDTH
                ).astype(BF16)
            else:
                states[b, c, own, :] = (
                    2.0 * (value - CENTER * second(b, c).astype(F32)) / HALF_WIDTH
                    - first(b, c).astype(F32)
                ).astype(BF16)


    def of_shard(shard):
        return pl.ds(pl.multiple_of(shard * width, width), width)

    def gather_copy(b, way, shard, c):
        at = states.at[b, c, of_shard(shard), :]
        return remote(
            at, at, gather_send_sem.at[b, way, shard], gather_recv_sem.at[b, shard, c], "st", to(way)
        )

    def gather_whole(b, way, shard, begin):
        at = states.at[b, pl.ds(begin, cells - begin), of_shard(shard), :]
        return remote(
            at, at, gather_send_sem.at[b, way, shard], gather_recv_sem.at[b, shard, 0], "st", to(way)
        )

    def gather_own(b, way, there):
        @pl.when(both(there, sends[way]))
        def _():
            def one(c, carry):
                gather_copy(b, way, s, c).start()
                return carry

            lax.fori_loop(jnp.where(to_end[way], given[b], 0), cells, one, 0)

    def gather_start(b, k):
        gather_own(b, RIGHT, s == k)
        gather_own(b, LEFT, s + k == steps)

    def gather_flat(b, begin, end):
        wait = min(5, cells - given[b])

        def one(i, carry):
            k = lax.div(i, cells) + 1
            c = lax.rem(i, cells)
            whole = both(c >= given[b])
            held = jnp.logical_or(whole, jnp.logical_not(ends))
            for way, shard, here in ((LEFT, s + k, s + k < sts), (RIGHT, s - k, s >= k)):
                passed = jnp.logical_or(whole, jnp.logical_not(to_end[way]))

                @pl.when(both(here, held))
                def _():
                    gather_copy(b, way, shard, c).wait_recv()

                    @pl.when(both(sends[way], passed))
                    def _():
                        gather_copy(b, way, shard, c).start()

            @pl.when(both(k == last_step, held))
            def _():
                contract(b, c)

            if given[b]:
                for way in (RIGHT, LEFT):

                    @pl.when(both(k == last_step, near_end[way], c >= wait, c < wait + given[b]))
                    def _():
                        contract_near(b, way, c - wait)

            if b + 1 < blocks:

                @pl.when(c == cells - 1)
                def _():
                    gather_start(b + 1, k)

            return carry

        lax.fori_loop(begin, end, one, 0)

    def gather_drain(b):
        def one(shard, carry):
            for way, passed in ((RIGHT, shard <= s), (LEFT, shard >= s)):

                @pl.when(both(passed, sends[way], to_end[way]))
                def _():
                    gather_whole(b, way, shard, given[b]).wait_send()

                @pl.when(both(passed, sends[way], jnp.logical_not(to_end[way])))
                def _():
                    gather_whole(b, way, shard, 0).wait_send()

            return carry

        lax.fori_loop(0, sts, one, 0)


    def contract(b, c):
        block = states[b, c]
        found = dot_nn(block, res_ref[c])
        for h in range(res // total_states):
            at = slice(h * total_states, (h + 1) * total_states)
            part[b, at, :] += found[:, at]
        part[b, res : res + total_states, :] += dot_nt(block, block)

    def give_copy(b, way):
        return remote(
            near_wire.at[b],
            near_got.at[b],
            give_send_sem.at[b],
            give_recv_sem.at[b],
            "st",
            to(1 - way),
        )

    def contract_near(b, way, c):
        @pl.when(c >= (given[b - 1] if b else 0))
        def _():
            near_wait(way, c)

        @pl.when(c == 0)
        def _():
            near_part[b] = jnp.zeros(near_part.shape[1:], F32)

        block = states[b, c]
        found = dot_nn(block, res_near[way, c])
        for h in range(res // total_states):
            at = slice(h * total_states, (h + 1) * total_states)
            near_part[b, at, :] += found[:, at]
        near_part[b, res : res + total_states, :] += dot_nt(block, block)

        @pl.when(c == given[b] - 1)
        def _():
            near_wire[b] = near_part[b].astype(WIRE)
            give_copy(b, way).start()

    def give_end(b):
        if not given[b]:
            return
        at = slice(0, res + total_states)

        @pl.when(ends)
        def _():
            give_copy(b, RIGHT).wait_recv()
            part[b, at, :] += near_got[b].astype(F32)

    def give_drain(b):
        if not given[b]:
            return

        @pl.when(jnp.logical_or(near_end[RIGHT], near_end[LEFT]))
        def _():
            give_copy(b, RIGHT).wait_send()

    def slice_of(peer):
        return pl.ds(pl.multiple_of(peer * rows, 16), rows)

    def one_copy(b, k):
        peer = dom_peer(k)
        return remote(
            wire.at[b, slice_of(peer)],
            part_recv.at[b, k],
            one_send_sem.at[b, k],
            one_recv_sem.at[b, k],
            "dom",
            peer,
        )

    def two_copy(b, k):
        at = total.at[b, slice_of(d)]
        return remote(at, at, two_send_sem.at[b, k], two_recv_sem.at[b, k], "dom", dom_peer(k))

    def from_peer(b, k):
        peer = dom_peer(doms - k)
        at = total.at[b, slice_of(peer)]
        return remote(at, at, two_send_sem.at[b, k], two_recv_sem.at[b, k], "dom", peer)

    def peers(body):
        def step(k, carry):
            body(k)
            return carry

        lax.fori_loop(1, doms, step, 0)

    def reduce_start(b):
        give_end(b)
        wire[b] = part[b].astype(WIRE)
        peers(lambda k: one_copy(b, k).start())

    def reduce_middle(b):
        def add(k, found):
            one_copy(b, k).wait_recv()
            return found + part_recv[b, k].astype(F32)

        found = lax.fori_loop(1, doms, add, part[b, slice_of(d), :])
        total[b, slice_of(d), :] = found.astype(WIRE)
        peers(lambda k: two_copy(b, k).start())

    def reduce_end(b):
        peers(lambda k: from_peer(b, k).wait_recv())

    def reduce_drain(b):
        def one(k):
            one_copy(b, k).wait_send()
            two_copy(b, k).wait_send()

        peers(one)

    def coefficients(b):
        gram = total[b, res : res + total_states, :].astype(F32)
        shape = (total_states, total_states)
        eye = (
            lax.broadcasted_iota(jnp.int32, shape, 0) == lax.broadcasted_iota(jnp.int32, shape, 1)
        ).astype(F32)
        along = jnp.sum(gram * eye, axis=0, keepdims=True) / total_nodes + EPSILON
        down = jnp.sum(gram * eye, axis=1, keepdims=True) / total_nodes + EPSILON
        root_i, root_j = lax.rsqrt(along), lax.rsqrt(down)
        mixing = root_i * (1.5 * eye - 0.5 * (gram * root_i * root_j / total_nodes))
        mix[b] = mixing.astype(BF16)
        for h in range(res // total_states):
            at = slice(h * total_states, (h + 1) * total_states)
            proj[b, :, at] = dot_nn(
                mixing, total[b, at, :].astype(F32), lax.Precision.HIGHEST
            ).astype(BF16)


    def near_copy(way, c, i):
        at = cuts(nodes, 2)[i]
        return remote(
            res_ref.at[c, at],
            res_near.at[way, c, at],
            near_send_sem.at[way, c, i],
            near_recv_sem.at[way, c, i],
            "st",
            to(way),
        )

    def near_start(c, i):
        if c >= moved:
            return
        for way in (RIGHT, LEFT):
            there = both(origin[way], sends[way])

            @pl.when(there)
            def _():
                near_copy(way, c, i).start()

            pending.append((there, partial(near_copy, way, c, i)))

    def near_wait(way, c):
        for i in range(2):
            near_copy(way, c, i).wait_recv()

    def coef_copy(b, way):
        return remote(
            proj.at[b],
            proj_near.at[way, b],
            coef_send_sem.at[way, b],
            coef_recv_sem.at[way, b],
            "st",
            to(way),
        )

    def coef_start(b):
        if not moved:
            return
        for way in (RIGHT, LEFT):
            there = both(origin[way], sends[way])

            @pl.when(there)
            def _():
                coef_copy(b, way).start()

            pending.append((there, partial(coef_copy, b, way)))


    def share_copy(b, t, way, c):
        return remote(
            share.at[b, t, c],
            share_recv.at[way, b, t, c],
            share_send_sem.at[b, t],
            share_recv_sem.at[way, b, t, c],
            "st",
            to(way),
        )

    def share_whole(b, t, way, begin):
        at = pl.ds(begin, cells - begin)
        return remote(
            share.at[b, t, at],
            share_recv.at[way, b, t, at],
            share_send_sem.at[b, t],
            share_recv_sem.at[way, b, t, 0],
            "st",
            to(way),
        )

    def ahead(way):
        if way == RIGHT:
            return steps - s, lambda i: steps - i
        return s, lambda i: i

    def share_cell(b, c):
        found = dot_nt(proj[b], res_ref[c])
        for t in range(sts):
            piece = found[t * width : (t + 1) * width, :]
            share[b, t, c] = piece.astype(BF16)

            @pl.when(t == s)
            def _():
                retained[b, c] = -piece

    def retain(b, c):
        retained[b, c] += dot_nn(mix[b, own, :], states[b, c])

    def share_start(b):
        def one(i, carry):
            c = lax.rem(i + moved, cells)

            @pl.when(c < given[b])
            def _():
                retained[b, c] = jnp.zeros(retained.shape[2:], F32)

            @pl.when(c >= given[b])
            def _():
                share_cell(b, c)

            for way in (RIGHT, LEFT):

                @pl.when(both(origin[way], c >= moved))
                def _():
                    share_copy(b, ahead(way)[1](0), way, c).start()

            @pl.when(c >= given[b])
            def _():
                retain(b, c)

            return carry

        def rest(i, carry):
            for way in (RIGHT, LEFT):

                @pl.when(origin[way])
                def _():
                    t = ahead(way)[1](lax.div(i, kept) + 1)
                    share_copy(b, t, way, lax.rem(i, kept) + moved).start()

            return carry

        kept = cells - moved

        @pl.when(ends)
        def _():
            lax.fori_loop(0, kept, one, 0)
            lax.fori_loop(0, (steps - 1) * kept, rest, 0)
            lax.fori_loop(kept, cells, one, 0)

    def share_drain(b):
        def one(t, carry):
            for way, passed in ((RIGHT, t > s), (LEFT, t < s)):

                @pl.when(both(passed, origin[way]))
                def _():
                    share_whole(b, t, way, moved).wait_send()

                @pl.when(both(passed, jnp.logical_not(origin[way])))
                def _():
                    share_whole(b, t, way, 0).wait_send()

            return carry

        lax.fori_loop(0, sts, one, 0)

    def absorb(b, way, t, c):
        share_copy(b, t, way, c).wait_recv()

        @pl.when(t == s)
        def _():
            retained[b, c] -= share_recv[way, b, t, c].astype(F32)

        @pl.when(t != s)
        def _():
            found = share[b, t, c].astype(F32) + share_recv[way, b, t, c].astype(F32)
            share[b, t, c] = found.astype(BF16)
            if given[b]:

                @pl.when(both(to_end[way], c < given[b]))
                def _():
                    share[b, t, c] = (found + near_term[b, c]).astype(BF16)

            share_copy(b, t, way, c).start()

    def absorb_near(b, way, c):
        if b == 0:

            @pl.when(c >= max(given))
            def _():
                near_wait(way, c)

        @pl.when(c == 0)
        def _():
            coef_copy(b, way).wait_recv()

        found = dot_nt(proj_near[way, b], res_near[way, c])
        if given[b]:

            @pl.when(c < given[b])
            def _():
                at = (0 if way == RIGHT else steps) * width
                end = slice(at, at + width)
                near_term[b, c] = found[end, :] - dot_nn(mix[b, end, :], states[b, c])

        for t in reversed(range(sts)) if way == RIGHT else range(sts):
            piece = found[t * width : (t + 1) * width, :]

            @pl.when(t > s if way == RIGHT else t < s)
            def _():
                share[b, t, c] = (share[b, t, c].astype(F32) + piece).astype(BF16)

            @pl.when(t == s)
            def _():
                retained[b, c] -= piece

    def chain(b, begin, end):
        def one(j, carry):
            @pl.when(both(jnp.logical_not(ends), j < cells))
            def _():
                share_cell(b, j)
                retain(b, j)

            for way in (RIGHT, LEFT):
                m = j - lag[way]
                i = lax.div(jnp.maximum(m, 0), cells)
                c = lax.rem(jnp.maximum(m, 0), cells)
                number, target = ahead(way)
                here = both(receives[way], m >= 0, i <= number)
                near = both(near_end[way], c < moved)
                if moved:

                    @pl.when(both(here, near, i == 0))
                    def _():
                        absorb_near(b, way, c)

                    @pl.when(both(here, near, i < number))
                    def _():
                        share_copy(b, target(i), way, c).start()

                @pl.when(both(here, jnp.logical_not(near)))
                def _():
                    absorb(b, way, target(i), c)

            c = j - done_at

            @pl.when(both(c >= 0, c < cells))
            def _():
                alive = jnp.where(c < count, 1.0, 0.0).astype(BF16)
                out_ref[b, c] = retained[b, c].astype(BF16) * alive
                pltpu.make_async_copy(out_ref.at[b, c], out_hbm.at[b, c], out_sem.at[b]).start()

            return carry

        lax.fori_loop(begin, end, one, 0)


    for b in range(blocks):
        part[b] = jnp.zeros(part.shape[1:], F32)
    start_load(0).wait()
    for i in range(2):
        stiff_load(i).wait()
    for b in range(blocks):
        if b:
            start_load(b).wait()
        operator_begin(0, b)
        if b == 0:
            relayout()
            near_start(0, 0)
    for b in range(blocks):
        operator_end(0, b)
        operator_begin(1, b)
    for b in range(blocks):
        operator_end(1, b)
        if b == 0:
            for k in range(sts):
                gather_start(0, k)
            near_start(0, 1)
            for i in range(2):
                near_start(1, i)
        if b == 1:
            gather_start(1, 0)
    for c in range(2, moved):
        for i in range(2):
            near_start(c, i)

    half = cells // 2
    whole = steps * cells
    links = done_at + cells
    cut_one = jnp.where(ends, done_at, cells // 2)
    cut_two = jnp.where(ends, done_at + 2, cells)
    gather_flat(0, 0, whole)
    reduce_start(0)
    for b in range(blocks):
        following, previous = b + 1 < blocks, b > 0
        if following:
            gather_flat(b + 1, 0, half)
        if previous:
            chain(b - 1, 0, cut_one)
        reduce_middle(b)
        if following:
            gather_flat(b + 1, half, cells)
        if previous:
            chain(b - 1, cut_one, cut_two)
        reduce_end(b)
        coefficients(b)
        coef_start(b)
        share_start(b)
        if previous:
            chain(b - 1, cut_two, links)
        if following:
            gather_flat(b + 1, cells, whole)
            reduce_start(b + 1)
    chain(blocks - 1, 0, links)

    for there, make in pending:

        @pl.when(there)
        def _():
            make().wait_send()

    for b in range(blocks):
        gather_drain(b)
        reduce_drain(b)
        share_drain(b)
        give_drain(b)
        pltpu.make_async_copy(out_ref.at[b], out_hbm.at[b], out_sem.at[b]).wait()


def on_device(start_block, resident, stiffness, cell_scale, potential, cell_count, face_index):
    blocks, cells, width, nodes = start_block.shape
    res = resident.shape[0]
    face = face_index.shape[2]
    doms, sts = lax.axis_size("dom"), lax.axis_size("st")
    total_states = sts * width
    rows = -(-(res + total_states) // (16 * doms)) * 16
    moved = 3 * cells // 8 if sts > 3 else 0
    given = tuple(min(moved, (2 * b + 1) * cells // 8) for b in range(blocks))
    sizes = (doms, sts, blocks, cells, width, nodes, face, res, rows, moved, given)
    near = max(moved, 1)
    dma = pltpu.SemaphoreType.DMA
    vmem = pl.BlockSpec(memory_space=pltpu.VMEM)
    smem = pl.BlockSpec(memory_space=pltpu.SMEM)
    anywhere = pl.BlockSpec(memory_space=pl.ANY)
    return pl.pallas_call(
        partial(kernel, sizes),
        out_shape=jax.ShapeDtypeStruct((blocks, cells, width, nodes), BF16),
        in_specs=[smem, smem, anywhere, anywhere, anywhere, vmem, vmem],
        out_specs=anywhere,
        scratch_shapes=[
            pltpu.VMEM((blocks, cells, width, nodes), BF16),
            pltpu.VMEM((nodes, nodes), BF16),
            pltpu.VMEM((blocks, cells, width, nodes), BF16),
            pltpu.VMEM((blocks, cells * width, nodes), F32),
            pltpu.VMEM((blocks, cells * width, nodes), BF16),
            pltpu.VMEM((blocks, cells, total_states, nodes), BF16),
            pltpu.VMEM((blocks, doms * rows, total_states), F32),
            pltpu.VMEM((blocks, doms * rows, total_states), WIRE),
            pltpu.VMEM((blocks, doms, rows, total_states), WIRE),
            pltpu.VMEM((blocks, doms * rows, total_states), WIRE),
            pltpu.VMEM((blocks, total_states, total_states), BF16),
            pltpu.VMEM((blocks, total_states, res), BF16),
            pltpu.VMEM((blocks, sts, cells, width, nodes), BF16),
            pltpu.VMEM((2, blocks, sts, cells, width, nodes), BF16),
            pltpu.VMEM((nodes, cells, res), BF16),
            pltpu.VMEM((res // 128, face * cells, 128), F32),
            pltpu.VMEM((cells, nodes, res), BF16),
            pltpu.VMEM((2, near, nodes, res), BF16),
            pltpu.VMEM((2, blocks, total_states, res), BF16),
            pltpu.VMEM((blocks, cells, width, nodes), F32),
            pltpu.VMEM((blocks, res + total_states, total_states), F32),
            pltpu.VMEM((blocks, res + total_states, total_states), WIRE),
            pltpu.VMEM((blocks, res + total_states, total_states), WIRE),
            pltpu.VMEM((blocks, near, width, nodes), F32),
            pltpu.VMEM((2, blocks, 2, width, face), F32),
            pltpu.VMEM((2, blocks, 2, width, face), F32),
            dma((2, blocks, 2)),
            dma((2, blocks, 2)),
            dma((blocks, 2, sts)),
            dma((blocks, sts, cells)),
            dma((blocks, doms)),
            dma((blocks, doms)),
            dma((blocks, doms)),
            dma((blocks, doms)),
            dma((blocks, sts)),
            dma((2, blocks, sts, cells)),
            dma((4,)),
            dma((blocks,)),
            dma((2,)),
            dma((blocks,)),
            dma((2, near, 2)),
            dma((2, near, 2)),
            dma((2, blocks)),
            dma((2, blocks)),
            dma((blocks,)),
            dma((blocks,)),
        ],
        compiler_params=pltpu.CompilerParams(
            collective_id=0, has_side_effects=True, vmem_limit_bytes=60 * 1024 * 1024
        ),
    )(
        cell_scale,
        cell_count,
        start_block,
        jnp.transpose(resident, (2, 1, 0)),
        stiffness,
        potential,
        face_index,
    )


def solution(mesh):
    return jax.shard_map(
        on_device,
        mesh=mesh,
        in_specs=(
            P(None, "dom", "st", None),
            P("st", "dom", None),
            P(),
            P("dom"),
            P("dom", None),
            P("dom"),
            P("dom", None, None),
        ),
        out_specs=P(None, "dom", "st", None),
        check_vma=False,
    )
```

```python
from functools import partial

import jax
import jax.numpy as jnp
from jax import lax
from jax.experimental import pallas as pl
from jax.experimental.pallas import tpu as pltpu
from jax.sharding import PartitionSpec as P

CENTER = 0.5
HALF_WIDTH = 2.0
EPSILON = 1e-06
F32 = jnp.float32
BF16 = jnp.bfloat16
WIRE = BF16
RIGHT, LEFT = 0, 1
LAG = 6
MESH = pl.DeviceIdType.MESH


def dot_nn(a, b, precision=None):
    return lax.dot_general(
        a, b, (((1,), (0,)), ((), ())), precision=precision, preferred_element_type=F32
    )


def dot_nt(a, b, precision=None):
    return lax.dot_general(
        a, b, (((1,), (1,)), ((), ())), precision=precision, preferred_element_type=F32
    )


def both(*conditions):
    found = conditions[0]
    for condition in conditions[1:]:
        found = jnp.logical_and(found, condition)
    return found


def kernel(
    sizes,
    scale_ref,
    count_ref,
    start_hbm,
    res_hbm,
    stiff_hbm,
    pot_ref,
    face_ref,
    out_hbm,
    start_ref,
    stiff_ref,
    out_ref,
    local,
    inner,
    states,
    part,
    wire,
    part_recv,
    total,
    mix,
    proj,
    share,
    share_recv,
    res_in,
    res_wide,
    res_ref,
    res_near,
    proj_near,
    retained,
    near_part,
    near_wire,
    near_got,
    near_term,
    face_out,
    face_in,
    face_send_sem,
    face_recv_sem,
    gather_send_sem,
    gather_recv_sem,
    one_send_sem,
    one_recv_sem,
    two_send_sem,
    two_recv_sem,
    share_send_sem,
    share_recv_sem,
    load_sem,
    start_sem,
    stiff_sem,
    out_sem,
    near_send_sem,
    near_recv_sem,
    coef_send_sem,
    coef_recv_sem,
    give_send_sem,
    give_recv_sem,
):
    doms, sts, blocks, cells, width, nodes, face, res, rows, moved, given = sizes
    total_states = sts * width
    total_nodes = float(doms * cells * nodes)
    window = (nodes - face) // 128 * 128
    offset = nodes - face - window
    d = lax.axis_index("dom")
    s = lax.axis_index("st")
    has_right, has_left = s < sts - 1, s > 0
    has_next, has_prev = d < doms - 1, d > 0
    own = pl.ds(pl.multiple_of(s * width, width), width)
    steps = sts - 1
    last_step = jnp.maximum(s, steps - s)
    ends = jnp.logical_or(s == 0, s == steps)
    pending = []
    count = count_ref[0]
    scale = [scale_ref[c] for c in range(cells)]
    live = [jnp.where(c < count, 1.0, 0.0).astype(F32) for c in range(cells)]
    last = [jnp.where(c == count - 1, 1.0, 0.0).astype(F32) for c in range(cells)]

    def start_load(b):
        return pltpu.make_async_copy(start_hbm.at[b], start_ref.at[b], start_sem.at[b])

    def cuts(extent, number):
        step = -(-extent // (number * 16)) * 16
        return [pl.ds(at, min(step, extent - at)) for at in range(0, extent, step)]

    def stiff_load(at):
        return pltpu.make_async_copy(stiff_hbm.at[at], stiff_ref.at[at], stiff_sem)

    def res_load(at):
        return pltpu.make_async_copy(res_hbm.at[at], res_in.at[at], load_sem)

    start_load(0).start()
    for at in cuts(nodes, 2):
        stiff_load(at).start()
    for b in range(1, blocks):
        start_load(b).start()
    for at in cuts(nodes, 4):
        res_load(at).start()

    origin = {RIGHT: s == 0, LEFT: s == steps}
    lag = {RIGHT: LAG * jnp.maximum(s - 1, 0), LEFT: LAG * jnp.maximum(steps - 1 - s, 0)}
    done_at = jnp.maximum(
        jnp.where(s > 0, lag[RIGHT] + (steps - s) * cells, 0),
        jnp.where(s < steps, lag[LEFT] + s * cells, 0),
    )
    sends = {RIGHT: has_right, LEFT: has_left}
    receives = {RIGHT: has_left, LEFT: has_right}
    near_end = {RIGHT: s == 1, LEFT: s == steps - 1}
    to_end = {RIGHT: s == steps - 1, LEFT: s == 1}

    def to(way):
        return s + 1 if way == RIGHT else s - 1

    def dom_peer(k):
        return lax.rem(d + k, doms)

    barrier = pltpu.get_barrier_semaphore()

    def greet(k, carry):
        pl.semaphore_signal(barrier, inc=1, device_id={"dom": dom_peer(k)}, device_id_type=MESH)
        return carry

    lax.fori_loop(1, doms, greet, 0)
    for way in (RIGHT, LEFT):

        @pl.when(sends[way])
        def _():
            pl.semaphore_signal(barrier, inc=1, device_id={"st": to(way)}, device_id_type=MESH)

    def meet():
        neighbours = has_right.astype(jnp.int32) + has_left.astype(jnp.int32)
        pl.semaphore_wait(barrier, doms - 1 + neighbours)

    def remote(src, dst, send_sem, recv_sem, axis, peer):
        return pltpu.make_async_remote_copy(
            src_ref=src,
            dst_ref=dst,
            send_sem=send_sem,
            recv_sem=recv_sem,
            device_id={axis: peer},
            device_id_type=MESH,
        )

    def one_hot(row, first, extent):
        node = lax.broadcasted_iota(jnp.int32, (extent, face), 0) + first
        if row == 0:
            node = node + (count - 1) * nodes
        return jnp.where(face_ref[0, row : row + 1, :] == node, 1.0, 0.0).astype(F32)

    def mask(c):
        return live[c].astype(BF16)

    def relayout():
        res_load(pl.ds(0, nodes)).wait()
        for chunk in range(nodes // face):
            at = slice(chunk * face, (chunk + 1) * face)
            wide = res_in[at].astype(F32).reshape(face * cells, res)
            for h in range(res // 128):
                lanes = slice(h * 128, (h + 1) * 128)
                res_wide[h] = wide[:, lanes]
                for c in range(cells):
                    res_ref[c, at, lanes] = res_wide[h, pl.ds(c, face, stride=cells), :].astype(BF16)


    def rows_of(c):
        return slice(c * width, (c + 1) * width)

    def face_copy(step, b, way):
        return remote(
            face_out.at[step, b, way],
            face_in.at[step, b, way],
            face_send_sem.at[step, b, way],
            face_recv_sem.at[step, b, way],
            "dom",
            d + 1 if way == RIGHT else d - 1,
        )

    def first(b, c):
        if c is None:
            return jnp.concatenate([first(b, i) for i in range(cells)], axis=0)
        return start_ref[b, c] * mask(c)

    def second(b, c):
        return inner[b] if c is None else inner[b, rows_of(c), :]

    def operator_begin(step, b, meanwhile=None):
        field = partial(second if step else first, b)
        local[b] = dot_nn(field(None), stiff_ref[...])
        last_tail = jnp.zeros((width, nodes - window), F32)
        for c in range(cells):
            value = scale[c] * local[b, rows_of(c), :] + pot_ref[c : c + 1, :] * field(c).astype(F32)
            local[b, rows_of(c), :] = value
            last_tail = last_tail + last[c] * value[:, window:]
        face_out[step, b, RIGHT] = dot_nn(
            last_tail, one_hot(0, window, nodes - window), lax.Precision.HIGHEST
        )
        face_out[step, b, LEFT] = dot_nn(
            local[b, rows_of(0), :face], one_hot(1, 0, face), lax.Precision.HIGHEST
        )
        if meanwhile is not None:
            meanwhile()
        for way, there in ((RIGHT, has_next), (LEFT, has_prev)):

            @pl.when(there)
            def _():
                face_copy(step, b, way).start()

            pending.append((there, partial(face_copy, step, b, way)))
        for c in range(cells - 1):
            pair = live[c + 1]
            tail = local[b, rows_of(c), window:]
            head = local[b, rows_of(c + 1), :face]
            padded = head
            if offset:
                padded = jnp.concatenate([jnp.zeros((width, offset), F32), head], axis=1)
            local[b, rows_of(c), window:] = tail + pair * padded
            local[b, rows_of(c + 1), :face] = head + pair * tail[:, offset:]

    def operator_end(step, b):
        for way, source in ((RIGHT, has_prev), (LEFT, has_next)):

            @pl.when(source)
            def _():
                face_copy(step, b, way).wait_recv()

            @pl.when(jnp.logical_not(source))
            def _():
                face_in[step, b, way] = jnp.zeros((width, face), F32)

        local[b, rows_of(0), :face] += dot_nt(
            face_in[step, b, RIGHT], one_hot(1, 0, face), lax.Precision.HIGHEST
        )
        tail_add = dot_nt(
            face_in[step, b, LEFT], one_hot(0, window, nodes - window), lax.Precision.HIGHEST
        )
        for c in range(cells):
            local[b, rows_of(c), window:] += last[c] * tail_add
        for c in range(cells):
            value = live[c] * local[b, rows_of(c), :]
            if step == 0:
                inner[b, rows_of(c), :] = (
                    (value - CENTER * first(b, c).astype(F32)) / HALF_WIDTH
                ).astype(BF16)
            else:
                states[b, c, own, :] = (
                    2.0 * (value - CENTER * second(b, c).astype(F32)) / HALF_WIDTH
                    - first(b, c).astype(F32)
                ).astype(BF16)


    def of_shard(shard):
        return pl.ds(pl.multiple_of(shard * width, width), width)

    def gather_copy(b, way, shard, c, here):
        at = states.at[b, c, of_shard(shard), :]
        slot = jnp.where(shard > here, shard - 1, shard)
        return remote(
            at, at, gather_send_sem.at[b, way, shard], gather_recv_sem.at[b, slot, c], "st", to(way)
        )

    def gather_whole(b, way, shard, begin):
        at = states.at[b, pl.ds(begin, cells - begin), of_shard(shard), :]
        return remote(
            at, at, gather_send_sem.at[b, way, shard], gather_recv_sem.at[b, 0, 0], "st", to(way)
        )

    def gather_own(b, way, there):
        @pl.when(both(there, sends[way]))
        def _():
            def one(c, carry):
                gather_copy(b, way, s, c, to(way)).start()
                return carry

            lax.fori_loop(jnp.where(to_end[way], given[b], 0), cells, one, 0)

    def gather_start(b, k):
        gather_own(b, RIGHT, s == k)
        gather_own(b, LEFT, s + k == steps)

    def gather_flat(b, begin, end):
        wait = min(5, cells - given[b])

        def one(i, carry):
            k = lax.div(i, cells) + 1
            c = lax.rem(i, cells)
            whole = both(c >= given[b])
            held = jnp.logical_or(whole, jnp.logical_not(ends))
            for way, shard, here in ((LEFT, s + k, s + k < sts), (RIGHT, s - k, s >= k)):
                passed = jnp.logical_or(whole, jnp.logical_not(to_end[way]))

                @pl.when(both(here, held))
                def _():
                    gather_copy(b, way, shard, c, s).wait_recv()

                    @pl.when(both(sends[way], passed))
                    def _():
                        gather_copy(b, way, shard, c, to(way)).start()

            @pl.when(both(k == last_step, held))
            def _():
                contract(b, c)

            if given[b]:
                for way in (RIGHT, LEFT):

                    @pl.when(both(k == last_step, near_end[way], c >= wait, c < wait + given[b]))
                    def _():
                        contract_near(b, way, c - wait)

            if b + 1 < blocks:

                @pl.when(c == cells - 1)
                def _():
                    gather_start(b + 1, k)

            return carry

        lax.fori_loop(begin, end, one, 0)

    def gather_drain(b):
        def one(shard, carry):
            for way, passed in ((RIGHT, shard <= s), (LEFT, shard >= s)):

                @pl.when(both(passed, sends[way], to_end[way]))
                def _():
                    gather_whole(b, way, shard, given[b]).wait_send()

                @pl.when(both(passed, sends[way], jnp.logical_not(to_end[way])))
                def _():
                    gather_whole(b, way, shard, 0).wait_send()

            return carry

        lax.fori_loop(0, sts, one, 0)


    def contract(b, c):
        block = states[b, c]
        found = dot_nn(block, res_ref[c])
        for h in range(res // total_states):
            at = slice(h * total_states, (h + 1) * total_states)
            part[b, at, :] += found[:, at]
        part[b, res : res + total_states, :] += dot_nt(block, block)

    def give_copy(b, way):
        return remote(
            near_wire.at[b],
            near_got.at[b],
            give_send_sem.at[b],
            give_recv_sem.at[b],
            "st",
            to(1 - way),
        )

    def contract_near(b, way, c):
        @pl.when(c >= (given[b - 1] if b else 0))
        def _():
            near_wait(way, c)

        @pl.when(c == 0)
        def _():
            near_part[b] = jnp.zeros(near_part.shape[1:], F32)

        block = states[b, c]
        found = dot_nn(block, res_near[way, c])
        for h in range(res // total_states):
            at = slice(h * total_states, (h + 1) * total_states)
            near_part[b, at, :] += found[:, at]
        near_part[b, res : res + total_states, :] += dot_nt(block, block)

        @pl.when(c == given[b] - 1)
        def _():
            near_wire[b] = near_part[b].astype(WIRE)
            give_copy(b, way).start()

    def give_end(b):
        if not given[b]:
            return
        at = slice(0, res + total_states)

        @pl.when(ends)
        def _():
            give_copy(b, RIGHT).wait_recv()
            part[b, at, :] += near_got[b].astype(F32)

    def give_drain(b):
        if not given[b]:
            return

        @pl.when(jnp.logical_or(near_end[RIGHT], near_end[LEFT]))
        def _():
            give_copy(b, RIGHT).wait_send()

    def slice_of(peer):
        return pl.ds(pl.multiple_of(peer * rows, 16), rows)

    def one_copy(b, k):
        peer = dom_peer(k)
        return remote(
            wire.at[b, slice_of(peer)],
            part_recv.at[b, k],
            one_send_sem.at[b],
            one_recv_sem.at[b],
            "dom",
            peer,
        )

    def two_copy(b, k):
        at = total.at[b, slice_of(d)]
        return remote(at, at, two_send_sem.at[b], two_recv_sem.at[b], "dom", dom_peer(k))


    def one_whole(b):
        at = part_recv.at[b, pl.ds(1, doms - 1)]
        return remote(at, at, one_send_sem.at[b], one_recv_sem.at[b], "dom", dom_peer(1))

    def two_whole(b):
        at = total.at[b, pl.ds(0, (doms - 1) * rows)]
        return remote(at, at, two_send_sem.at[b], two_recv_sem.at[b], "dom", dom_peer(1))

    def peers(body):
        def step(k, carry):
            body(k)
            return carry

        lax.fori_loop(1, doms, step, 0)

    def reduce_start(b):
        give_end(b)
        wire[b] = part[b].astype(WIRE)
        peers(lambda k: one_copy(b, k).start())

    def reduce_middle(b):
        one_whole(b).wait_recv()

        def add(k, found):
            return found + part_recv[b, k].astype(F32)

        found = lax.fori_loop(1, doms, add, part[b, slice_of(d), :])
        total[b, slice_of(d), :] = found.astype(WIRE)
        peers(lambda k: two_copy(b, k).start())

    def reduce_end(b):
        two_whole(b).wait_recv()

    def reduce_drain(b):
        one_whole(b).wait_send()
        two_whole(b).wait_send()

    def coefficients(b):
        gram = total[b, res : res + total_states, :].astype(F32)
        shape = (total_states, total_states)
        eye = (
            lax.broadcasted_iota(jnp.int32, shape, 0) == lax.broadcasted_iota(jnp.int32, shape, 1)
        ).astype(F32)
        along = jnp.sum(gram * eye, axis=0, keepdims=True) / total_nodes + EPSILON
        down = jnp.sum(gram * eye, axis=1, keepdims=True) / total_nodes + EPSILON
        root_i, root_j = lax.rsqrt(along), lax.rsqrt(down)
        mixing = root_i * (1.5 * eye - 0.5 * (gram * root_i * root_j / total_nodes))
        mix[b] = mixing.astype(BF16)
        for h in range(res // total_states):
            at = slice(h * total_states, (h + 1) * total_states)
            proj[b, :, at] = dot_nn(
                mixing, total[b, at, :].astype(F32), lax.Precision.HIGHEST
            ).astype(BF16)


    def near_copy(way, c, i):
        at = cuts(nodes, 2)[i]
        return remote(
            res_ref.at[c, at],
            res_near.at[way, c, at],
            near_send_sem.at[c, i],
            near_recv_sem.at[c, i],
            "st",
            to(way),
        )

    def near_start(c, i):
        if c >= moved:
            return
        for way in (RIGHT, LEFT):
            there = both(origin[way], sends[way])

            @pl.when(there)
            def _():
                near_copy(way, c, i).start()

            pending.append((there, partial(near_copy, way, c, i)))

    def near_wait(way, c):
        for i in range(2):
            near_copy(way, c, i).wait_recv()

    def coef_copy(b, way):
        return remote(
            proj.at[b],
            proj_near.at[way, b],
            coef_send_sem.at[b],
            coef_recv_sem.at[b],
            "st",
            to(way),
        )

    def coef_start(b):
        if not moved:
            return
        for way in (RIGHT, LEFT):
            there = both(origin[way], sends[way])

            @pl.when(there)
            def _():
                coef_copy(b, way).start()

            pending.append((there, partial(coef_copy, b, way)))


    def share_copy(b, t, way, c, here):
        slot = jnp.where(jnp.logical_and(t == here, way == LEFT), sts, t)
        return remote(
            share.at[b, t, c],
            share_recv.at[way, b, t, c],
            share_send_sem.at[b, t],
            share_recv_sem.at[b, slot, c],
            "st",
            to(way),
        )

    def share_whole(b, t, way, begin):
        at = pl.ds(begin, cells - begin)
        return remote(
            share.at[b, t, at],
            share_recv.at[way, b, t, at],
            share_send_sem.at[b, t],
            share_recv_sem.at[b, t, 0],
            "st",
            to(way),
        )

    def ahead(way):
        if way == RIGHT:
            return steps - s, lambda i: steps - i
        return s, lambda i: i

    def share_cell(b, c):
        found = dot_nt(proj[b], res_ref[c])
        for t in range(sts):
            piece = found[t * width : (t + 1) * width, :]
            share[b, t, c] = piece.astype(BF16)

            @pl.when(t == s)
            def _():
                retained[b, c] = -piece

    def retain(b, c):
        retained[b, c] += dot_nn(mix[b, own, :], states[b, c])

    def share_start(b):
        def one(i, carry):
            c = lax.rem(i + moved, cells)

            @pl.when(c < given[b])
            def _():
                retained[b, c] = jnp.zeros(retained.shape[2:], F32)

            @pl.when(c >= given[b])
            def _():
                share_cell(b, c)

            for way in (RIGHT, LEFT):

                @pl.when(both(origin[way], c >= moved))
                def _():
                    share_copy(b, ahead(way)[1](0), way, c, to(way)).start()

            @pl.when(c >= given[b])
            def _():
                retain(b, c)

            return carry

        def rest(i, carry):
            for way in (RIGHT, LEFT):

                @pl.when(origin[way])
                def _():
                    t = ahead(way)[1](lax.div(i, kept) + 1)
                    share_copy(b, t, way, lax.rem(i, kept) + moved, to(way)).start()

            return carry

        kept = cells - moved

        @pl.when(ends)
        def _():
            lax.fori_loop(0, kept, one, 0)
            lax.fori_loop(0, (steps - 1) * kept, rest, 0)
            lax.fori_loop(kept, cells, one, 0)

    def share_drain(b):
        def one(t, carry):
            for way, passed in ((RIGHT, t > s), (LEFT, t < s)):

                @pl.when(both(passed, origin[way]))
                def _():
                    share_whole(b, t, way, moved).wait_send()

                @pl.when(both(passed, jnp.logical_not(origin[way])))
                def _():
                    share_whole(b, t, way, 0).wait_send()

            return carry

        lax.fori_loop(0, sts, one, 0)

    def absorb(b, way, t, c):
        share_copy(b, t, way, c, s).wait_recv()

        @pl.when(t == s)
        def _():
            retained[b, c] -= share_recv[way, b, t, c].astype(F32)

        @pl.when(t != s)
        def _():
            found = share[b, t, c].astype(F32) + share_recv[way, b, t, c].astype(F32)
            share[b, t, c] = found.astype(BF16)
            if given[b]:

                @pl.when(both(to_end[way], c < given[b]))
                def _():
                    share[b, t, c] = (found + near_term[b, c]).astype(BF16)

            share_copy(b, t, way, c, to(way)).start()

    def absorb_near(b, way, c):
        if b == 0:

            @pl.when(c >= max(given))
            def _():
                near_wait(way, c)

        @pl.when(c == 0)
        def _():
            coef_copy(b, way).wait_recv()

        found = dot_nt(proj_near[way, b], res_near[way, c])
        if given[b]:

            @pl.when(c < given[b])
            def _():
                at = (0 if way == RIGHT else steps) * width
                end = slice(at, at + width)
                near_term[b, c] = found[end, :] - dot_nn(mix[b, end, :], states[b, c])

        for t in reversed(range(sts)) if way == RIGHT else range(sts):
            piece = found[t * width : (t + 1) * width, :]

            @pl.when(t > s if way == RIGHT else t < s)
            def _():
                share[b, t, c] = (share[b, t, c].astype(F32) + piece).astype(BF16)

            @pl.when(t == s)
            def _():
                retained[b, c] -= piece

    def chain(turns, begin, end):
        def one(j, carry):
            for b, offset in turns:
                chain_step(b, j + offset)
            return carry

        lax.fori_loop(begin, end, one, 0)

    def chain_step(b, j):
        @pl.when(both(jnp.logical_not(ends), j < cells))
        def _():
            share_cell(b, j)
            retain(b, j)

        for way in (RIGHT, LEFT):
            m = j - lag[way]
            i = lax.div(jnp.maximum(m, 0), cells)
            c = lax.rem(jnp.maximum(m, 0), cells)
            number, target = ahead(way)
            here = both(receives[way], m >= 0, i <= number)
            near = both(near_end[way], c < moved)
            if moved:

                @pl.when(both(here, near, i == 0))
                def _():
                    absorb_near(b, way, c)

                @pl.when(both(here, near, i < number))
                def _():
                    share_copy(b, target(i), way, c, to(way)).start()

            @pl.when(both(here, jnp.logical_not(near)))
            def _():
                absorb(b, way, target(i), c)

        c = j - done_at

        @pl.when(both(c >= 0, c < cells))
        def _():
            alive = jnp.where(c < count, 1.0, 0.0).astype(BF16)
            out_ref[b, c] = retained[b, c].astype(BF16) * alive
            pltpu.make_async_copy(out_ref.at[b, c], out_hbm.at[b, c], out_sem.at[b]).start()


    for b in range(blocks):
        part[b] = jnp.zeros(part.shape[1:], F32)
    start_load(0).wait()
    stiff_load(pl.ds(0, nodes)).wait()
    operator_begin(0, 0, meet)
    relayout()
    for i in range(2):
        near_start(0, i)
    for b in range(1, blocks):
        start_load(b).wait()
        operator_begin(0, b)
    for b in range(blocks):
        operator_end(0, b)
        operator_begin(1, b)
    for b in range(blocks):
        operator_end(1, b)
        if b == 0:
            for k in range(sts):
                gather_start(0, k)
            for i in range(2):
                near_start(1, i)
        if b == 1:
            gather_start(1, 0)
    for c in range(2, moved):
        for i in range(2):
            near_start(c, i)

    half = cells // 2
    whole = steps * cells
    links = done_at + cells
    over = 3 * cells // 4
    cut_one = jnp.where(ends, done_at, cells // 2)
    cut_two = jnp.where(ends, done_at + 2, cells)
    gather_flat(0, 0, whole)
    reduce_start(0)
    for b in range(blocks):
        following, previous = b + 1 < blocks, b > 0
        if following:
            gather_flat(b + 1, 0, half)
        if previous:
            chain([(b - 1, 0)], over if b > 1 else 0, cut_one)
        reduce_middle(b)
        if following:
            gather_flat(b + 1, half, cells)
        if previous:
            chain([(b - 1, 0)], cut_one, cut_two)
        reduce_end(b)
        coefficients(b)
        coef_start(b)
        share_start(b)
        if previous:
            chain([(b - 1, 0)], cut_two, links - over)
            chain([(b - 1, links - over), (b, 0)], 0, over)
        if following:
            gather_flat(b + 1, cells, whole)
            reduce_start(b + 1)
    chain([(blocks - 1, 0)], over if blocks > 1 else 0, links)

    for there, make in pending:

        @pl.when(there)
        def _():
            make().wait_send()

    for b in range(blocks):
        gather_drain(b)
        reduce_drain(b)
        share_drain(b)
        give_drain(b)
        pltpu.make_async_copy(out_ref.at[b], out_hbm.at[b], out_sem.at[b]).wait()


def on_device(start_block, resident, stiffness, cell_scale, potential, cell_count, face_index):
    blocks, cells, width, nodes = start_block.shape
    res = resident.shape[0]
    face = face_index.shape[2]
    doms, sts = lax.axis_size("dom"), lax.axis_size("st")
    total_states = sts * width
    rows = -(-(res + total_states) // (16 * doms)) * 16
    moved = 3 * cells // 8 if sts > 3 else 0
    given = tuple(min(moved, (2 * b + 1) * cells // 8) for b in range(blocks))
    sizes = (doms, sts, blocks, cells, width, nodes, face, res, rows, moved, given)
    near = max(moved, 1)
    dma = pltpu.SemaphoreType.DMA
    vmem = pl.BlockSpec(memory_space=pltpu.VMEM)
    smem = pl.BlockSpec(memory_space=pltpu.SMEM)
    anywhere = pl.BlockSpec(memory_space=pl.ANY)
    return pl.pallas_call(
        partial(kernel, sizes),
        out_shape=jax.ShapeDtypeStruct((blocks, cells, width, nodes), BF16),
        in_specs=[smem, smem, anywhere, anywhere, anywhere, vmem, vmem],
        out_specs=anywhere,
        scratch_shapes=[
            pltpu.VMEM((blocks, cells, width, nodes), BF16),
            pltpu.VMEM((nodes, nodes), BF16),
            pltpu.VMEM((blocks, cells, width, nodes), BF16),
            pltpu.VMEM((blocks, cells * width, nodes), F32),
            pltpu.VMEM((blocks, cells * width, nodes), BF16),
            pltpu.VMEM((blocks, cells, total_states, nodes), BF16),
            pltpu.VMEM((blocks, doms * rows, total_states), F32),
            pltpu.VMEM((blocks, doms * rows, total_states), WIRE),
            pltpu.VMEM((blocks, doms, rows, total_states), WIRE),
            pltpu.VMEM((blocks, doms * rows, total_states), WIRE),
            pltpu.VMEM((blocks, total_states, total_states), BF16),
            pltpu.VMEM((blocks, total_states, res), BF16),
            pltpu.VMEM((blocks, sts, cells, width, nodes), BF16),
            pltpu.VMEM((2, blocks, sts, cells, width, nodes), BF16),
            pltpu.VMEM((nodes, cells, res), BF16),
            pltpu.VMEM((res // 128, face * cells, 128), F32),
            pltpu.VMEM((cells, nodes, res), BF16),
            pltpu.VMEM((2, near, nodes, res), BF16),
            pltpu.VMEM((2, blocks, total_states, res), BF16),
            pltpu.VMEM((blocks, cells, width, nodes), F32),
            pltpu.VMEM((blocks, res + total_states, total_states), F32),
            pltpu.VMEM((blocks, res + total_states, total_states), WIRE),
            pltpu.VMEM((blocks, res + total_states, total_states), WIRE),
            pltpu.VMEM((blocks, near, width, nodes), F32),
            pltpu.VMEM((2, blocks, 2, width, face), F32),
            pltpu.VMEM((2, blocks, 2, width, face), F32),
            dma((2, blocks, 2)),
            dma((2, blocks, 2)),
            dma((blocks, 2, sts)),
            dma((blocks, max(sts - 1, 1), cells)),
            dma((blocks,)),
            dma((blocks,)),
            dma((blocks,)),
            dma((blocks,)),
            dma((blocks, sts)),
            dma((blocks, sts + 1, cells)),
            dma,
            dma((blocks,)),
            dma,
            dma((blocks,)),
            dma((near, 2)),
            dma((near, 2)),
            dma((blocks,)),
            dma((blocks,)),
            dma((blocks,)),
            dma((blocks,)),
        ],
        compiler_params=pltpu.CompilerParams(
            collective_id=0, has_side_effects=True, vmem_limit_bytes=60 * 1024 * 1024
        ),
    )(
        cell_scale,
        cell_count,
        start_block,
        jnp.transpose(resident, (2, 1, 0)),
        stiffness,
        potential,
        face_index,
    )


def solution(mesh):
    return jax.shard_map(
        on_device,
        mesh=mesh,
        in_specs=(
            P(None, "dom", "st", None),
            P("st", "dom", None),
            P(),
            P("dom"),
            P("dom", None),
            P("dom"),
            P("dom", None, None),
        ),
        out_specs=P(None, "dom", "st", None),
        check_vma=False,
    )
```

```python
from functools import partial

import jax
import jax.numpy as jnp
from jax import lax
from jax.experimental import pallas as pl
from jax.experimental.pallas import tpu as pltpu
from jax.sharding import PartitionSpec as P

CENTER = 0.5
HALF_WIDTH = 2.0
EPSILON = 1e-06
F32 = jnp.float32
BF16 = jnp.bfloat16
WIRE = BF16
RIGHT, LEFT = 0, 1
LAG = 6
GAP = 4
MESH = pl.DeviceIdType.MESH


def dot_nn(a, b, precision=None):
    return lax.dot_general(
        a, b, (((1,), (0,)), ((), ())), precision=precision, preferred_element_type=F32
    )


def dot_nt(a, b, precision=None):
    return lax.dot_general(
        a, b, (((1,), (1,)), ((), ())), precision=precision, preferred_element_type=F32
    )


def both(*conditions):
    found = conditions[0]
    for condition in conditions[1:]:
        found = jnp.logical_and(found, condition)
    return found


def kernel(
    sizes,
    scale_ref,
    count_ref,
    start_hbm,
    res_hbm,
    stiff_hbm,
    pot_ref,
    face_ref,
    out_hbm,
    start_ref,
    stiff_ref,
    out_ref,
    local,
    inner,
    states,
    part,
    wire,
    part_recv,
    total,
    mix,
    proj,
    share,
    share_recv,
    res_in,
    res_wide,
    res_ref,
    res_near,
    proj_near,
    retained,
    near_part,
    near_wire,
    near_got,
    near_term,
    face_out,
    face_in,
    face_send_sem,
    face_recv_sem,
    gather_send_sem,
    gather_recv_sem,
    one_send_sem,
    one_recv_sem,
    two_send_sem,
    two_recv_sem,
    share_send_sem,
    share_recv_sem,
    load_sem,
    start_sem,
    stiff_sem,
    out_sem,
    near_send_sem,
    near_recv_sem,
    coef_send_sem,
    coef_recv_sem,
    give_send_sem,
    give_recv_sem,
):
    doms, sts, blocks, cells, width, nodes, face, res, rows, moved, given = sizes
    total_states = sts * width
    total_nodes = float(doms * cells * nodes)
    window = (nodes - face) // 128 * 128
    offset = nodes - face - window
    d = lax.axis_index("dom")
    s = lax.axis_index("st")
    has_right, has_left = s < sts - 1, s > 0
    has_next, has_prev = d < doms - 1, d > 0
    own = pl.ds(pl.multiple_of(s * width, width), width)
    steps = sts - 1
    last_step = jnp.maximum(s, steps - s)
    ends = jnp.logical_or(s == 0, s == steps)
    pending = []
    count = count_ref[0]
    scale = [scale_ref[c] for c in range(cells)]
    live = [jnp.where(c < count, 1.0, 0.0).astype(F32) for c in range(cells)]
    last = [jnp.where(c == count - 1, 1.0, 0.0).astype(F32) for c in range(cells)]

    def start_load(b):
        return pltpu.make_async_copy(start_hbm.at[b], start_ref.at[b], start_sem.at[b])

    def cuts(extent, number):
        step = -(-extent // (number * 16)) * 16
        return [pl.ds(at, min(step, extent - at)) for at in range(0, extent, step)]

    def stiff_load(at):
        return pltpu.make_async_copy(stiff_hbm.at[at], stiff_ref.at[at], stiff_sem)

    def res_load(at):
        return pltpu.make_async_copy(res_hbm.at[at], res_in.at[at], load_sem)

    start_load(0).start()
    for at in cuts(nodes, 2):
        stiff_load(at).start()
    for b in range(1, blocks):
        start_load(b).start()
    for at in cuts(nodes, 4):
        res_load(at).start()

    origin = {RIGHT: s == 0, LEFT: s == steps}
    lag = {RIGHT: LAG * jnp.maximum(s - 1, 0), LEFT: LAG * jnp.maximum(steps - 1 - s, 0)}
    done_at = jnp.maximum(
        jnp.where(s > 0, lag[RIGHT] + (steps - s) * cells, 0),
        jnp.where(s < steps, lag[LEFT] + s * cells, 0),
    )
    sends = {RIGHT: has_right, LEFT: has_left}
    receives = {RIGHT: has_left, LEFT: has_right}
    near_end = {RIGHT: s == 1, LEFT: s == steps - 1}
    to_end = {RIGHT: s == steps - 1, LEFT: s == 1}
    gap = {way: jnp.where(near_end[way], GAP if moved else 0, 0) for way in (RIGHT, LEFT)}
    gathered_at = jnp.maximum(
        jnp.where(s > 0, gap[RIGHT] + (s - 1) * cells, 0),
        jnp.where(s < steps, gap[LEFT] + (steps - s - 1) * cells, 0),
    )

    def to(way):
        return s + 1 if way == RIGHT else s - 1

    def dom_peer(k):
        return lax.rem(d + k, doms)

    barrier = pltpu.get_barrier_semaphore()

    def greet(k, carry):
        pl.semaphore_signal(barrier, inc=1, device_id={"dom": dom_peer(k)}, device_id_type=MESH)
        return carry

    lax.fori_loop(1, doms, greet, 0)
    for way in (RIGHT, LEFT):

        @pl.when(sends[way])
        def _():
            pl.semaphore_signal(barrier, inc=1, device_id={"st": to(way)}, device_id_type=MESH)

    def meet():
        neighbours = has_right.astype(jnp.int32) + has_left.astype(jnp.int32)
        pl.semaphore_wait(barrier, doms - 1 + neighbours)

    def remote(src, dst, send_sem, recv_sem, axis, peer):
        return pltpu.make_async_remote_copy(
            src_ref=src,
            dst_ref=dst,
            send_sem=send_sem,
            recv_sem=recv_sem,
            device_id={axis: peer},
            device_id_type=MESH,
        )

    def one_hot(row, first, extent):
        node = lax.broadcasted_iota(jnp.int32, (extent, face), 0) + first
        if row == 0:
            node = node + (count - 1) * nodes
        return jnp.where(face_ref[0, row : row + 1, :] == node, 1.0, 0.0).astype(F32)

    def mask(c):
        return live[c].astype(BF16)

    def relayout():
        res_load(pl.ds(0, nodes)).wait()
        for chunk in range(nodes // face):
            at = slice(chunk * face, (chunk + 1) * face)
            wide = res_in[at].astype(F32).reshape(face * cells, res)
            for h in range(res // 128):
                lanes = slice(h * 128, (h + 1) * 128)
                res_wide[h] = wide[:, lanes]
                for c in range(cells):
                    res_ref[c, at, lanes] = res_wide[h, pl.ds(c, face, stride=cells), :].astype(BF16)


    def rows_of(c):
        return slice(c * width, (c + 1) * width)

    def face_copy(step, b, way):
        return remote(
            face_out.at[step, b, way],
            face_in.at[step, b, way],
            face_send_sem.at[step, b, way],
            face_recv_sem.at[step, b, way],
            "dom",
            d + 1 if way == RIGHT else d - 1,
        )

    def first(b, c):
        if c is None:
            return jnp.concatenate([first(b, i) for i in range(cells)], axis=0)
        return start_ref[b, c] * mask(c)

    def second(b, c):
        return inner[b] if c is None else inner[b, rows_of(c), :]

    def operator_begin(step, b, meanwhile=None):
        field = partial(second if step else first, b)
        local[b] = dot_nn(field(None), stiff_ref[...])
        last_tail = jnp.zeros((width, nodes - window), F32)
        for c in range(cells):
            value = scale[c] * local[b, rows_of(c), :] + pot_ref[c : c + 1, :] * field(c).astype(F32)
            local[b, rows_of(c), :] = value
            last_tail = last_tail + last[c] * value[:, window:]
        face_out[step, b, RIGHT] = dot_nn(
            last_tail, one_hot(0, window, nodes - window), lax.Precision.HIGHEST
        )
        face_out[step, b, LEFT] = dot_nn(
            local[b, rows_of(0), :face], one_hot(1, 0, face), lax.Precision.HIGHEST
        )
        if meanwhile is not None:
            meanwhile()
        for way, there in ((RIGHT, has_next), (LEFT, has_prev)):

            @pl.when(there)
            def _():
                face_copy(step, b, way).start()

            pending.append((there, partial(face_copy, step, b, way)))
        for c in range(cells - 1):
            pair = live[c + 1]
            tail = local[b, rows_of(c), window:]
            head = local[b, rows_of(c + 1), :face]
            padded = head
            if offset:
                padded = jnp.concatenate([jnp.zeros((width, offset), F32), head], axis=1)
            local[b, rows_of(c), window:] = tail + pair * padded
            local[b, rows_of(c + 1), :face] = head + pair * tail[:, offset:]

    def operator_end(step, b):
        for way, source in ((RIGHT, has_prev), (LEFT, has_next)):

            @pl.when(source)
            def _():
                face_copy(step, b, way).wait_recv()

            @pl.when(jnp.logical_not(source))
            def _():
                face_in[step, b, way] = jnp.zeros((width, face), F32)

        local[b, rows_of(0), :face] += dot_nt(
            face_in[step, b, RIGHT], one_hot(1, 0, face), lax.Precision.HIGHEST
        )
        tail_add = dot_nt(
            face_in[step, b, LEFT], one_hot(0, window, nodes - window), lax.Precision.HIGHEST
        )
        for c in range(cells):
            local[b, rows_of(c), window:] += last[c] * tail_add
        for c in range(cells):
            value = live[c] * local[b, rows_of(c), :]
            if step == 0:
                inner[b, rows_of(c), :] = (
                    (value - CENTER * first(b, c).astype(F32)) / HALF_WIDTH
                ).astype(BF16)
            else:
                states[b, c, own, :] = (
                    2.0 * (value - CENTER * second(b, c).astype(F32)) / HALF_WIDTH
                    - first(b, c).astype(F32)
                ).astype(BF16)


    def of_shard(shard):
        return pl.ds(pl.multiple_of(shard * width, width), width)

    def gather_copy(b, way, shard, c, here):
        at = states.at[b, c, of_shard(shard), :]
        slot = jnp.where(shard > here, shard - 1, shard)
        return remote(
            at, at, gather_send_sem.at[b, way, shard], gather_recv_sem.at[b, slot, c], "st", to(way)
        )

    def gather_whole(b, way, shard, begin):
        at = states.at[b, pl.ds(begin, cells - begin), of_shard(shard), :]
        return remote(
            at, at, gather_send_sem.at[b, way, shard], gather_recv_sem.at[b, 0, 0], "st", to(way)
        )

    def gather_own(b, way, there):
        @pl.when(jnp.logical_and(there, sends[way]))
        def _():
            def one(c, carry):
                gather_copy(b, way, s, c, to(way)).start()
                return carry

            lax.fori_loop(jnp.where(to_end[way], given[b], 0), cells, one, 0)

    def gather_flat(b, begin, end):
        wait = min(5, cells - given[b])

        def one(i, carry):
            for way in (LEFT, RIGHT):
                m = i - gap[way]
                k = lax.div(jnp.maximum(m, 0), cells) + 1
                c = lax.rem(jnp.maximum(m, 0), cells)
                shard = s - k if way == RIGHT else s + k
                here = both(m >= 0, shard >= 0, shard < sts)
                whole = c >= given[b]
                held = jnp.logical_or(whole, jnp.logical_not(ends))
                passed = jnp.logical_or(whole, jnp.logical_not(to_end[way]))

                @pl.when(both(here, held))
                def _():
                    gather_copy(b, way, shard, c, s).wait_recv()

                    @pl.when(both(sends[way], passed))
                    def _():
                        gather_copy(b, way, shard, c, to(way)).start()

                if b + 1 < blocks:
                    final = shard == (0 if way == RIGHT else steps)

                    @pl.when(both(here, final, c == cells - 1))
                    def _():
                        gather_own(b + 1, way, True)

            c = i - gathered_at

            @pl.when(both(c >= jnp.where(ends, given[b], 0), c < cells))
            def _():
                contract(b, c)

            if given[b]:
                for way in (RIGHT, LEFT):

                    @pl.when(both(near_end[way], c >= wait, c < wait + given[b]))
                    def _():
                        contract_near(b, way, c - wait)

            return carry

        lax.fori_loop(begin, end, one, 0)

    def gather_drain(b):
        def one(shard, carry):
            for way, passed in ((RIGHT, shard <= s), (LEFT, shard >= s)):

                @pl.when(both(passed, sends[way], to_end[way]))
                def _():
                    gather_whole(b, way, shard, given[b]).wait_send()

                @pl.when(both(passed, sends[way], jnp.logical_not(to_end[way])))
                def _():
                    gather_whole(b, way, shard, 0).wait_send()

            return carry

        lax.fori_loop(0, sts, one, 0)


    def contract(b, c):
        block = states[b, c]
        found = dot_nn(block, res_ref[c])
        for h in range(res // total_states):
            at = slice(h * total_states, (h + 1) * total_states)
            part[b, at, :] += found[:, at]
        part[b, res : res + total_states, :] += dot_nt(block, block)

    def give_copy(b, way):
        return remote(
            near_wire.at[b],
            near_got.at[b],
            give_send_sem.at[b],
            give_recv_sem.at[b],
            "st",
            to(1 - way),
        )

    def contract_near(b, way, c):
        @pl.when(c >= (given[b - 1] if b else 0))
        def _():
            near_wait(way, c)

        @pl.when(c == 0)
        def _():
            near_part[b] = jnp.zeros(near_part.shape[1:], F32)

        block = states[b, c]
        found = dot_nn(block, res_near[way, c])
        for h in range(res // total_states):
            at = slice(h * total_states, (h + 1) * total_states)
            near_part[b, at, :] += found[:, at]
        near_part[b, res : res + total_states, :] += dot_nt(block, block)

        @pl.when(c == given[b] - 1)
        def _():
            near_wire[b] = near_part[b].astype(WIRE)
            give_copy(b, way).start()

    def give_end(b):
        if not given[b]:
            return
        at = slice(0, res + total_states)

        @pl.when(ends)
        def _():
            give_copy(b, RIGHT).wait_recv()
            part[b, at, :] += near_got[b].astype(F32)

    def give_drain(b):
        if not given[b]:
            return

        @pl.when(jnp.logical_or(near_end[RIGHT], near_end[LEFT]))
        def _():
            give_copy(b, RIGHT).wait_send()

    def slice_of(peer):
        return pl.ds(pl.multiple_of(peer * rows, 16), rows)

    def one_copy(b, k):
        peer = dom_peer(k)
        return remote(
            wire.at[b, slice_of(peer)],
            part_recv.at[b, k],
            one_send_sem.at[b],
            one_recv_sem.at[b],
            "dom",
            peer,
        )

    def two_copy(b, k):
        at = total.at[b, slice_of(d)]
        return remote(at, at, two_send_sem.at[b], two_recv_sem.at[b], "dom", dom_peer(k))


    def one_whole(b):
        at = part_recv.at[b, pl.ds(1, doms - 1)]
        return remote(at, at, one_send_sem.at[b], one_recv_sem.at[b], "dom", dom_peer(1))

    def two_whole(b):
        at = total.at[b, pl.ds(0, (doms - 1) * rows)]
        return remote(at, at, two_send_sem.at[b], two_recv_sem.at[b], "dom", dom_peer(1))

    def peers(body):
        def step(k, carry):
            body(k)
            return carry

        lax.fori_loop(1, doms, step, 0)

    def reduce_start(b):
        give_end(b)
        wire[b] = part[b].astype(WIRE)
        peers(lambda k: one_copy(b, k).start())

    def reduce_middle(b):
        one_whole(b).wait_recv()

        def add(k, found):
            return found + part_recv[b, k].astype(F32)

        found = lax.fori_loop(1, doms, add, part[b, slice_of(d), :])
        total[b, slice_of(d), :] = found.astype(WIRE)
        peers(lambda k: two_copy(b, k).start())

    def reduce_end(b):
        two_whole(b).wait_recv()

    def reduce_drain(b):
        one_whole(b).wait_send()
        two_whole(b).wait_send()

    def coefficients(b):
        gram = total[b, res : res + total_states, :].astype(F32)
        shape = (total_states, total_states)
        eye = (
            lax.broadcasted_iota(jnp.int32, shape, 0) == lax.broadcasted_iota(jnp.int32, shape, 1)
        ).astype(F32)
        along = jnp.sum(gram * eye, axis=0, keepdims=True) / total_nodes + EPSILON
        down = jnp.sum(gram * eye, axis=1, keepdims=True) / total_nodes + EPSILON
        root_i, root_j = lax.rsqrt(along), lax.rsqrt(down)
        mixing = root_i * (1.5 * eye - 0.5 * (gram * root_i * root_j / total_nodes))
        mix[b] = mixing.astype(BF16)
        for h in range(res // total_states):
            at = slice(h * total_states, (h + 1) * total_states)
            proj[b, :, at] = dot_nn(
                mixing, total[b, at, :].astype(F32), lax.Precision.HIGHEST
            ).astype(BF16)


    def near_copy(way, c, i):
        at = cuts(nodes, 2)[i]
        return remote(
            res_ref.at[c, at],
            res_near.at[way, c, at],
            near_send_sem.at[c, i],
            near_recv_sem.at[c, i],
            "st",
            to(way),
        )

    def near_start(c, i):
        if c >= moved:
            return
        for way in (RIGHT, LEFT):
            there = both(origin[way], sends[way])

            @pl.when(there)
            def _():
                near_copy(way, c, i).start()

            pending.append((there, partial(near_copy, way, c, i)))

    def near_wait(way, c):
        for i in range(2):
            near_copy(way, c, i).wait_recv()

    def coef_copy(b, way):
        return remote(
            proj.at[b],
            proj_near.at[way, b],
            coef_send_sem.at[b],
            coef_recv_sem.at[b],
            "st",
            to(way),
        )

    def coef_start(b):
        if not moved:
            return
        for way in (RIGHT, LEFT):
            there = both(origin[way], sends[way])

            @pl.when(there)
            def _():
                coef_copy(b, way).start()

            pending.append((there, partial(coef_copy, b, way)))


    def share_copy(b, t, way, c, here):
        slot = jnp.where(jnp.logical_and(t == here, way == LEFT), sts, t)
        return remote(
            share.at[b, t, c],
            share_recv.at[way, b, t, c],
            share_send_sem.at[b, t],
            share_recv_sem.at[b, slot, c],
            "st",
            to(way),
        )

    def share_whole(b, t, way, begin):
        at = pl.ds(begin, cells - begin)
        return remote(
            share.at[b, t, at],
            share_recv.at[way, b, t, at],
            share_send_sem.at[b, t],
            share_recv_sem.at[b, t, 0],
            "st",
            to(way),
        )

    def ahead(way):
        if way == RIGHT:
            return steps - s, lambda i: steps - i
        return s, lambda i: i

    def share_cell(b, c):
        found = dot_nt(proj[b], res_ref[c])
        for t in range(sts):
            piece = found[t * width : (t + 1) * width, :]
            share[b, t, c] = piece.astype(BF16)

            @pl.when(t == s)
            def _():
                retained[b, c] = -piece

    def retain(b, c):
        retained[b, c] += dot_nn(mix[b, own, :], states[b, c])

    def share_start(b):
        def one(i, carry):
            c = lax.rem(i + moved, cells)

            @pl.when(c < given[b])
            def _():
                retained[b, c] = jnp.zeros(retained.shape[2:], F32)

            @pl.when(c >= given[b])
            def _():
                share_cell(b, c)

            for way in (RIGHT, LEFT):

                @pl.when(both(origin[way], c >= moved))
                def _():
                    share_copy(b, ahead(way)[1](0), way, c, to(way)).start()

            @pl.when(c >= given[b])
            def _():
                retain(b, c)

            return carry

        def rest(i, carry):
            for way in (RIGHT, LEFT):

                @pl.when(origin[way])
                def _():
                    t = ahead(way)[1](lax.div(i, kept) + 1)
                    share_copy(b, t, way, lax.rem(i, kept) + moved, to(way)).start()

            return carry

        kept = cells - moved

        @pl.when(ends)
        def _():
            lax.fori_loop(0, kept, one, 0)
            lax.fori_loop(0, (steps - 1) * kept, rest, 0)
            lax.fori_loop(kept, cells, one, 0)

    def share_drain(b):
        def one(t, carry):
            for way, passed in ((RIGHT, t > s), (LEFT, t < s)):

                @pl.when(both(passed, origin[way]))
                def _():
                    share_whole(b, t, way, moved).wait_send()

                @pl.when(both(passed, jnp.logical_not(origin[way])))
                def _():
                    share_whole(b, t, way, 0).wait_send()

            return carry

        lax.fori_loop(0, sts, one, 0)

    def absorb(b, way, t, c):
        share_copy(b, t, way, c, s).wait_recv()

        @pl.when(t == s)
        def _():
            retained[b, c] -= share_recv[way, b, t, c].astype(F32)

        @pl.when(t != s)
        def _():
            found = share[b, t, c].astype(F32) + share_recv[way, b, t, c].astype(F32)
            share[b, t, c] = found.astype(BF16)
            if given[b]:

                @pl.when(both(to_end[way], c < given[b]))
                def _():
                    share[b, t, c] = (found + near_term[b, c]).astype(BF16)

            share_copy(b, t, way, c, to(way)).start()

    def absorb_near(b, way, c):
        if b == 0:

            @pl.when(c >= max(given))
            def _():
                near_wait(way, c)

        @pl.when(c == 0)
        def _():
            coef_copy(b, way).wait_recv()

        found = dot_nt(proj_near[way, b], res_near[way, c])
        if given[b]:

            @pl.when(c < given[b])
            def _():
                at = (0 if way == RIGHT else steps) * width
                end = slice(at, at + width)
                near_term[b, c] = found[end, :] - dot_nn(mix[b, end, :], states[b, c])

        for t in reversed(range(sts)) if way == RIGHT else range(sts):
            piece = found[t * width : (t + 1) * width, :]

            @pl.when(t > s if way == RIGHT else t < s)
            def _():
                share[b, t, c] = (share[b, t, c].astype(F32) + piece).astype(BF16)

            @pl.when(t == s)
            def _():
                retained[b, c] -= piece

    def chain(turns, begin, end):
        def one(j, carry):
            for b, offset in turns:
                chain_step(b, j + offset)
            return carry

        lax.fori_loop(begin, end, one, 0)

    def chain_step(b, j):
        @pl.when(both(jnp.logical_not(ends), j < cells))
        def _():
            share_cell(b, j)
            retain(b, j)

        for way in (RIGHT, LEFT):
            m = j - lag[way]
            i = lax.div(jnp.maximum(m, 0), cells)
            c = lax.rem(jnp.maximum(m, 0), cells)
            number, target = ahead(way)
            here = both(receives[way], m >= 0, i <= number)
            near = both(near_end[way], c < moved)
            if moved:

                @pl.when(both(here, near, i == 0))
                def _():
                    absorb_near(b, way, c)

                @pl.when(both(here, near, i < number))
                def _():
                    share_copy(b, target(i), way, c, to(way)).start()

            @pl.when(both(here, jnp.logical_not(near)))
            def _():
                absorb(b, way, target(i), c)

        c = j - done_at

        @pl.when(both(c >= 0, c < cells))
        def _():
            alive = jnp.where(c < count, 1.0, 0.0).astype(BF16)
            out_ref[b, c] = retained[b, c].astype(BF16) * alive
            pltpu.make_async_copy(out_ref.at[b, c], out_hbm.at[b, c], out_sem.at[b]).start()


    for b in range(blocks):
        part[b] = jnp.zeros(part.shape[1:], F32)
    start_load(0).wait()
    stiff_load(pl.ds(0, nodes)).wait()
    operator_begin(0, 0, meet)
    relayout()
    for i in range(2):
        near_start(0, i)
    operator_end(0, 0)
    operator_begin(1, 0)
    for b in range(1, blocks):
        start_load(b).wait()
        operator_begin(0, b)
    for b in range(blocks):
        operator_end(1, b)
        if b == 0:
            for way in (RIGHT, LEFT):
                gather_own(0, way, True)
            for i in range(2):
                near_start(1, i)
            for later in range(1, blocks):
                operator_end(0, later)
                operator_begin(1, later)
        if b == 1:
            for way in (RIGHT, LEFT):
                gather_own(1, way, origin[way])
    for c in range(2, moved):
        for i in range(2):
            near_start(c, i)

    half = cells // 2
    whole = steps * cells
    links = done_at + cells
    over = 3 * cells // 4
    cut_one = jnp.where(ends, done_at, cells // 2)
    cut_two = jnp.where(ends, done_at + 2, cells)
    gather_flat(0, 0, whole)
    reduce_start(0)
    for b in range(blocks):
        following, previous = b + 1 < blocks, b > 0
        if following:
            gather_flat(b + 1, 0, half)
        if previous:
            chain([(b - 1, 0)], over if b > 1 else 0, cut_one)
        reduce_middle(b)
        if following:
            gather_flat(b + 1, half, cells)
        if previous:
            chain([(b - 1, 0)], cut_one, cut_two)
        reduce_end(b)
        coefficients(b)
        coef_start(b)
        share_start(b)
        if previous:
            chain([(b - 1, 0)], cut_two, links - over)
            chain([(b - 1, links - over), (b, 0)], 0, over)
        if following:
            gather_flat(b + 1, cells, whole)
            reduce_start(b + 1)
    chain([(blocks - 1, 0)], over if blocks > 1 else 0, links)

    for there, make in pending:

        @pl.when(there)
        def _():
            make().wait_send()

    for b in range(blocks):
        gather_drain(b)
        reduce_drain(b)
        share_drain(b)
        give_drain(b)
        pltpu.make_async_copy(out_ref.at[b], out_hbm.at[b], out_sem.at[b]).wait()


def on_device(start_block, resident, stiffness, cell_scale, potential, cell_count, face_index):
    blocks, cells, width, nodes = start_block.shape
    res = resident.shape[0]
    face = face_index.shape[2]
    doms, sts = lax.axis_size("dom"), lax.axis_size("st")
    total_states = sts * width
    rows = -(-(res + total_states) // (16 * doms)) * 16
    moved = 3 * cells // 8 if sts > 3 else 0
    given = tuple(min(moved, (2 * b + 1) * cells // 8) for b in range(blocks))
    sizes = (doms, sts, blocks, cells, width, nodes, face, res, rows, moved, given)
    near = max(moved, 1)
    dma = pltpu.SemaphoreType.DMA
    vmem = pl.BlockSpec(memory_space=pltpu.VMEM)
    smem = pl.BlockSpec(memory_space=pltpu.SMEM)
    anywhere = pl.BlockSpec(memory_space=pl.ANY)
    far = pl.BlockSpec(memory_space=pltpu.HBM)

    def hold(array):
        return pltpu.with_memory_space_constraint(array, pltpu.HBM)

    return pl.pallas_call(
        partial(kernel, sizes),
        out_shape=jax.ShapeDtypeStruct((blocks, cells, width, nodes), BF16),
        in_specs=[smem, smem, far, far, far, vmem, vmem],
        out_specs=anywhere,
        scratch_shapes=[
            pltpu.VMEM((blocks, cells, width, nodes), BF16),
            pltpu.VMEM((nodes, nodes), BF16),
            pltpu.VMEM((blocks, cells, width, nodes), BF16),
            pltpu.VMEM((blocks, cells * width, nodes), F32),
            pltpu.VMEM((blocks, cells * width, nodes), BF16),
            pltpu.VMEM((blocks, cells, total_states, nodes), BF16),
            pltpu.VMEM((blocks, doms * rows, total_states), F32),
            pltpu.VMEM((blocks, doms * rows, total_states), WIRE),
            pltpu.VMEM((blocks, doms, rows, total_states), WIRE),
            pltpu.VMEM((blocks, doms * rows, total_states), WIRE),
            pltpu.VMEM((blocks, total_states, total_states), BF16),
            pltpu.VMEM((blocks, total_states, res), BF16),
            pltpu.VMEM((blocks, sts, cells, width, nodes), BF16),
            pltpu.VMEM((2, blocks, sts, cells, width, nodes), BF16),
            pltpu.VMEM((nodes, cells, res), BF16),
            pltpu.VMEM((res // 128, face * cells, 128), F32),
            pltpu.VMEM((cells, nodes, res), BF16),
            pltpu.VMEM((2, near, nodes, res), BF16),
            pltpu.VMEM((2, blocks, total_states, res), BF16),
            pltpu.VMEM((blocks, cells, width, nodes), F32),
            pltpu.VMEM((blocks, res + total_states, total_states), F32),
            pltpu.VMEM((blocks, res + total_states, total_states), WIRE),
            pltpu.VMEM((blocks, res + total_states, total_states), WIRE),
            pltpu.VMEM((blocks, near, width, nodes), F32),
            pltpu.VMEM((2, blocks, 2, width, face), F32),
            pltpu.VMEM((2, blocks, 2, width, face), F32),
            dma((2, blocks, 2)),
            dma((2, blocks, 2)),
            dma((blocks, 2, sts)),
            dma((blocks, max(sts - 1, 1), cells)),
            dma((blocks,)),
            dma((blocks,)),
            dma((blocks,)),
            dma((blocks,)),
            dma((blocks, sts)),
            dma((blocks, sts + 1, cells)),
            dma,
            dma((blocks,)),
            dma,
            dma((blocks,)),
            dma((near, 2)),
            dma((near, 2)),
            dma((blocks,)),
            dma((blocks,)),
            dma((blocks,)),
            dma((blocks,)),
        ],
        compiler_params=pltpu.CompilerParams(
            collective_id=0, has_side_effects=True, vmem_limit_bytes=36 * 1024 * 1024
        ),
    )(
        hold(cell_scale),
        cell_count,
        hold(start_block),
        hold(jnp.transpose(resident, (2, 1, 0))),
        hold(stiffness),
        hold(potential),
        hold(face_index),
    )


def solution(mesh):
    return jax.shard_map(
        on_device,
        mesh=mesh,
        in_specs=(
            P(None, "dom", "st", None),
            P("st", "dom", None),
            P(),
            P("dom"),
            P("dom", None),
            P("dom"),
            P("dom", None, None),
        ),
        out_specs=P(None, "dom", "st", None),
        check_vma=False,
    )
```

```python
from functools import partial

import jax
import jax.numpy as jnp
from jax import lax
from jax.experimental import pallas as pl
from jax.experimental.pallas import tpu as pltpu
from jax.sharding import PartitionSpec as P

CENTER = 0.5
HALF_WIDTH = 2.0
EPSILON = 1e-06
F32 = jnp.float32
BF16 = jnp.bfloat16
WIRE = BF16
RIGHT, LEFT = 0, 1
LAG = 6
GAP = 4
MESH = pl.DeviceIdType.MESH


def dot_nn(a, b, precision=None):
    return lax.dot_general(
        a, b, (((1,), (0,)), ((), ())), precision=precision, preferred_element_type=F32
    )


def dot_nt(a, b, precision=None):
    return lax.dot_general(
        a, b, (((1,), (1,)), ((), ())), precision=precision, preferred_element_type=F32
    )


def both(*conditions):
    found = conditions[0]
    for condition in conditions[1:]:
        found = jnp.logical_and(found, condition)
    return found


def kernel(
    sizes,
    scale_ref,
    count_ref,
    start_hbm,
    res_hbm,
    stiff_hbm,
    pot_ref,
    face_ref,
    out_hbm,
    start_ref,
    stiff_ref,
    out_ref,
    local,
    inner,
    states,
    part,
    wire,
    part_recv,
    total,
    mix,
    proj,
    share,
    share_recv,
    res_in,
    res_wide,
    res_ref,
    res_near,
    proj_near,
    retained,
    near_part,
    near_wire,
    near_got,
    near_term,
    face_out,
    face_in,
    face_send_sem,
    face_recv_sem,
    gather_send_sem,
    gather_recv_sem,
    one_send_sem,
    one_recv_sem,
    two_send_sem,
    two_recv_sem,
    share_send_sem,
    share_recv_sem,
    load_sem,
    start_sem,
    stiff_sem,
    out_sem,
    near_send_sem,
    near_recv_sem,
    coef_send_sem,
    coef_recv_sem,
    give_send_sem,
    give_recv_sem,
):
    doms, sts, blocks, cells, width, nodes, face, res, rows, moved, given = sizes
    total_states = sts * width
    total_nodes = float(doms * cells * nodes)
    window = (nodes - face) // 128 * 128
    offset = nodes - face - window
    d = lax.axis_index("dom")
    s = lax.axis_index("st")
    has_right, has_left = s < sts - 1, s > 0
    has_next, has_prev = d < doms - 1, d > 0
    own = pl.ds(pl.multiple_of(s * width, width), width)
    steps = sts - 1
    last_step = jnp.maximum(s, steps - s)
    ends = jnp.logical_or(s == 0, s == steps)
    pending = []
    count = count_ref[0]
    scale = [scale_ref[c] for c in range(cells)]
    live = [jnp.where(c < count, 1.0, 0.0).astype(F32) for c in range(cells)]
    last = [jnp.where(c == count - 1, 1.0, 0.0).astype(F32) for c in range(cells)]

    def start_load(b):
        return pltpu.make_async_copy(start_hbm.at[b], start_ref.at[b], start_sem.at[b])

    def cuts(extent, number):
        step = -(-extent // (number * 16)) * 16
        return [pl.ds(at, min(step, extent - at)) for at in range(0, extent, step)]

    def stiff_load(at):
        return pltpu.make_async_copy(stiff_hbm.at[at], stiff_ref.at[at], stiff_sem)

    def res_load(at):
        return pltpu.make_async_copy(res_hbm.at[at], res_in.at[at], load_sem)

    def res_start():
        for at in cuts(nodes, 4):
            res_load(at).start()

    pl.when(ends)(res_start)
    start_load(0).start()
    for at in cuts(nodes, 2):
        stiff_load(at).start()
    for b in range(1, blocks):
        start_load(b).start()
    pl.when(jnp.logical_not(ends))(res_start)

    origin = {RIGHT: s == 0, LEFT: s == steps}
    lag = {RIGHT: LAG * jnp.maximum(s - 1, 0), LEFT: LAG * jnp.maximum(steps - 1 - s, 0)}
    done_at = jnp.maximum(
        jnp.where(s > 0, lag[RIGHT] + (steps - s) * cells, 0),
        jnp.where(s < steps, lag[LEFT] + s * cells, 0),
    )
    sends = {RIGHT: has_right, LEFT: has_left}
    receives = {RIGHT: has_left, LEFT: has_right}
    near_end = {RIGHT: s == 1, LEFT: s == steps - 1}
    to_end = {RIGHT: s == steps - 1, LEFT: s == 1}
    gap = {way: jnp.where(near_end[way], GAP if moved else 0, 0) for way in (RIGHT, LEFT)}
    gathered_at = jnp.maximum(
        jnp.where(s > 0, gap[RIGHT] + (s - 1) * cells, 0),
        jnp.where(s < steps, gap[LEFT] + (steps - s - 1) * cells, 0),
    )

    def to(way):
        return s + 1 if way == RIGHT else s - 1

    def dom_peer(k):
        return lax.rem(d + k, doms)

    barrier = pltpu.get_barrier_semaphore()

    def greet(k, carry):
        pl.semaphore_signal(barrier, inc=1, device_id={"dom": dom_peer(k)}, device_id_type=MESH)
        return carry

    lax.fori_loop(1, doms, greet, 0)
    for way in (RIGHT, LEFT):

        @pl.when(sends[way])
        def _():
            pl.semaphore_signal(barrier, inc=1, device_id={"st": to(way)}, device_id_type=MESH)

    def meet():
        neighbours = has_right.astype(jnp.int32) + has_left.astype(jnp.int32)
        pl.semaphore_wait(barrier, doms - 1 + neighbours)

    def remote(src, dst, send_sem, recv_sem, axis, peer):
        return pltpu.make_async_remote_copy(
            src_ref=src,
            dst_ref=dst,
            send_sem=send_sem,
            recv_sem=recv_sem,
            device_id={axis: peer},
            device_id_type=MESH,
        )

    def one_hot(row, first, extent):
        node = lax.broadcasted_iota(jnp.int32, (extent, face), 0) + first
        if row == 0:
            node = node + (count - 1) * nodes
        return jnp.where(face_ref[0, row : row + 1, :] == node, 1.0, 0.0).astype(F32)

    def mask(c):
        return live[c].astype(BF16)

    def relayout():
        res_load(pl.ds(0, nodes)).wait()
        for chunk in range(nodes // face):
            at = slice(chunk * face, (chunk + 1) * face)
            wide = res_in[at].astype(F32).reshape(face * cells, res)
            for h in range(res // 128):
                lanes = slice(h * 128, (h + 1) * 128)
                res_wide[h] = wide[:, lanes]
                for c in range(cells):
                    res_ref[c, at, lanes] = res_wide[h, pl.ds(c, face, stride=cells), :].astype(BF16)


    def rows_of(c):
        return slice(c * width, (c + 1) * width)

    def face_copy(step, b, way):
        return remote(
            face_out.at[step, b, way],
            face_in.at[step, b, way],
            face_send_sem.at[step, b, way],
            face_recv_sem.at[step, b, way],
            "dom",
            d + 1 if way == RIGHT else d - 1,
        )

    def first(b, c):
        if c is None:
            return jnp.concatenate([first(b, i) for i in range(cells)], axis=0)
        return start_ref[b, c] * mask(c)

    def second(b, c):
        return inner[b] if c is None else inner[b, rows_of(c), :]

    def operator_begin(step, b, meanwhile=None):
        field = partial(second if step else first, b)
        local[b] = dot_nn(field(None), stiff_ref[...])
        last_tail = jnp.zeros((width, nodes - window), F32)
        for c in range(cells):
            value = scale[c] * local[b, rows_of(c), :] + pot_ref[c : c + 1, :] * field(c).astype(F32)
            local[b, rows_of(c), :] = value
            last_tail = last_tail + last[c] * value[:, window:]
        face_out[step, b, RIGHT] = dot_nn(
            last_tail, one_hot(0, window, nodes - window), lax.Precision.HIGHEST
        )
        face_out[step, b, LEFT] = dot_nn(
            local[b, rows_of(0), :face], one_hot(1, 0, face), lax.Precision.HIGHEST
        )
        if meanwhile is not None:
            meanwhile()
        for way, there in ((RIGHT, has_next), (LEFT, has_prev)):

            @pl.when(there)
            def _():
                face_copy(step, b, way).start()

            pending.append((there, partial(face_copy, step, b, way)))
        for c in range(cells - 1):
            pair = live[c + 1]
            tail = local[b, rows_of(c), window:]
            head = local[b, rows_of(c + 1), :face]
            padded = head
            if offset:
                padded = jnp.concatenate([jnp.zeros((width, offset), F32), head], axis=1)
            local[b, rows_of(c), window:] = tail + pair * padded
            local[b, rows_of(c + 1), :face] = head + pair * tail[:, offset:]

    def operator_end(step, b):
        for way, source in ((RIGHT, has_prev), (LEFT, has_next)):

            @pl.when(source)
            def _():
                face_copy(step, b, way).wait_recv()

            @pl.when(jnp.logical_not(source))
            def _():
                face_in[step, b, way] = jnp.zeros((width, face), F32)

        local[b, rows_of(0), :face] += dot_nt(
            face_in[step, b, RIGHT], one_hot(1, 0, face), lax.Precision.HIGHEST
        )
        tail_add = dot_nt(
            face_in[step, b, LEFT], one_hot(0, window, nodes - window), lax.Precision.HIGHEST
        )
        for c in range(cells):
            local[b, rows_of(c), window:] += last[c] * tail_add
        for c in range(cells):
            value = live[c] * local[b, rows_of(c), :]
            if step == 0:
                inner[b, rows_of(c), :] = (
                    (value - CENTER * first(b, c).astype(F32)) / HALF_WIDTH
                ).astype(BF16)
            else:
                states[b, c, own, :] = (
                    2.0 * (value - CENTER * second(b, c).astype(F32)) / HALF_WIDTH
                    - first(b, c).astype(F32)
                ).astype(BF16)


    def of_shard(shard):
        return pl.ds(pl.multiple_of(shard * width, width), width)

    def gather_copy(b, way, shard, c, here):
        at = states.at[b, c, of_shard(shard), :]
        slot = jnp.where(shard > here, shard - 1, shard)
        return remote(
            at, at, gather_send_sem.at[b, way, shard], gather_recv_sem.at[b, slot, c], "st", to(way)
        )

    def gather_whole(b, way, shard, begin):
        at = states.at[b, pl.ds(begin, cells - begin), of_shard(shard), :]
        return remote(
            at, at, gather_send_sem.at[b, way, shard], gather_recv_sem.at[b, 0, 0], "st", to(way)
        )

    def gather_own(b, way, there):
        @pl.when(jnp.logical_and(there, sends[way]))
        def _():
            def one(c, carry):
                gather_copy(b, way, s, c, to(way)).start()
                return carry

            lax.fori_loop(jnp.where(to_end[way], given[b], 0), cells, one, 0)

    def gather_flat(b, begin, end):
        wait = min(5, cells - given[b])

        def one(i, carry):
            for way in (LEFT, RIGHT):
                m = i - gap[way]
                k = lax.div(jnp.maximum(m, 0), cells) + 1
                c = lax.rem(jnp.maximum(m, 0), cells)
                shard = s - k if way == RIGHT else s + k
                here = both(m >= 0, shard >= 0, shard < sts)
                whole = c >= given[b]
                held = jnp.logical_or(whole, jnp.logical_not(ends))
                passed = jnp.logical_or(whole, jnp.logical_not(to_end[way]))

                @pl.when(both(here, held))
                def _():
                    gather_copy(b, way, shard, c, s).wait_recv()

                    @pl.when(both(sends[way], passed))
                    def _():
                        gather_copy(b, way, shard, c, to(way)).start()

                if b + 1 < blocks:
                    final = shard == (0 if way == RIGHT else steps)

                    @pl.when(both(here, final, c == cells - 1))
                    def _():
                        gather_own(b + 1, way, True)

            c = i - gathered_at

            @pl.when(both(c >= jnp.where(ends, given[b], 0), c < cells))
            def _():
                contract(b, c)

            if given[b]:
                for way in (RIGHT, LEFT):

                    @pl.when(both(near_end[way], c >= wait, c < wait + given[b]))
                    def _():
                        contract_near(b, way, c - wait)

            return carry

        lax.fori_loop(begin, end, one, 0)

    def gather_drain(b):
        def one(shard, carry):
            for way, passed in ((RIGHT, shard <= s), (LEFT, shard >= s)):

                @pl.when(both(passed, sends[way], to_end[way]))
                def _():
                    gather_whole(b, way, shard, given[b]).wait_send()

                @pl.when(both(passed, sends[way], jnp.logical_not(to_end[way])))
                def _():
                    gather_whole(b, way, shard, 0).wait_send()

            return carry

        lax.fori_loop(0, sts, one, 0)


    def contract(b, c):
        block = states[b, c]
        found = dot_nn(block, res_ref[c])
        for h in range(res // total_states):
            at = slice(h * total_states, (h + 1) * total_states)
            part[b, at, :] += found[:, at]
        part[b, res : res + total_states, :] += dot_nt(block, block)

    def give_copy(b, way):
        return remote(
            near_wire.at[b],
            near_got.at[b],
            give_send_sem.at[b],
            give_recv_sem.at[b],
            "st",
            to(1 - way),
        )

    def contract_near(b, way, c):
        @pl.when(c >= (given[b - 1] if b else 0))
        def _():
            near_wait(way, c)

        @pl.when(c == 0)
        def _():
            near_part[b] = jnp.zeros(near_part.shape[1:], F32)

        block = states[b, c]
        found = dot_nn(block, res_near[way, c])
        for h in range(res // total_states):
            at = slice(h * total_states, (h + 1) * total_states)
            near_part[b, at, :] += found[:, at]
        near_part[b, res : res + total_states, :] += dot_nt(block, block)

        @pl.when(c == given[b] - 1)
        def _():
            near_wire[b] = near_part[b].astype(WIRE)
            give_copy(b, way).start()

    def give_end(b):
        if not given[b]:
            return
        at = slice(0, res + total_states)

        @pl.when(ends)
        def _():
            give_copy(b, RIGHT).wait_recv()
            part[b, at, :] += near_got[b].astype(F32)

    def give_drain(b):
        if not given[b]:
            return

        @pl.when(jnp.logical_or(near_end[RIGHT], near_end[LEFT]))
        def _():
            give_copy(b, RIGHT).wait_send()

    def slice_of(peer):
        return pl.ds(pl.multiple_of(peer * rows, 16), rows)

    def one_copy(b, k):
        peer = dom_peer(k)
        return remote(
            wire.at[b, slice_of(peer)],
            part_recv.at[b, k],
            one_send_sem.at[b],
            one_recv_sem.at[b],
            "dom",
            peer,
        )

    def two_copy(b, k):
        at = total.at[b, slice_of(d)]
        return remote(at, at, two_send_sem.at[b], two_recv_sem.at[b], "dom", dom_peer(k))


    def one_whole(b):
        at = part_recv.at[b, pl.ds(1, doms - 1)]
        return remote(at, at, one_send_sem.at[b], one_recv_sem.at[b], "dom", dom_peer(1))

    def two_whole(b):
        at = total.at[b, pl.ds(0, (doms - 1) * rows)]
        return remote(at, at, two_send_sem.at[b], two_recv_sem.at[b], "dom", dom_peer(1))

    def peers(body):
        def step(k, carry):
            body(k)
            return carry

        lax.fori_loop(1, doms, step, 0)

    def reduce_start(b):
        give_end(b)
        wire[b] = part[b].astype(WIRE)
        peers(lambda k: one_copy(b, k).start())

    def reduce_middle(b):
        one_whole(b).wait_recv()

        def add(k, found):
            return found + part_recv[b, k].astype(F32)

        found = lax.fori_loop(1, doms, add, part[b, slice_of(d), :])
        total[b, slice_of(d), :] = found.astype(WIRE)
        peers(lambda k: two_copy(b, k).start())

    def reduce_end(b):
        two_whole(b).wait_recv()

    def reduce_drain(b):
        one_whole(b).wait_send()
        two_whole(b).wait_send()

    def coefficients(b):
        gram = total[b, res : res + total_states, :].astype(F32)
        shape = (total_states, total_states)
        eye = (
            lax.broadcasted_iota(jnp.int32, shape, 0) == lax.broadcasted_iota(jnp.int32, shape, 1)
        ).astype(F32)
        along = jnp.sum(gram * eye, axis=0, keepdims=True) / total_nodes + EPSILON
        down = jnp.sum(gram * eye, axis=1, keepdims=True) / total_nodes + EPSILON
        root_i, root_j = lax.rsqrt(along), lax.rsqrt(down)
        mixing = root_i * (1.5 * eye - 0.5 * (gram * root_i * root_j / total_nodes))
        mix[b] = mixing.astype(BF16)
        for h in range(res // total_states):
            at = slice(h * total_states, (h + 1) * total_states)
            proj[b, :, at] = dot_nn(
                mixing, total[b, at, :].astype(F32), lax.Precision.HIGHEST
            ).astype(BF16)


    def near_copy(way, c, i):
        at = cuts(nodes, 2)[i]
        return remote(
            res_ref.at[c, at],
            res_near.at[way, c, at],
            near_send_sem.at[c, i],
            near_recv_sem.at[c, i],
            "st",
            to(way),
        )

    def near_start(c, i):
        if c >= moved:
            return
        for way in (RIGHT, LEFT):
            there = both(origin[way], sends[way])

            @pl.when(there)
            def _():
                near_copy(way, c, i).start()

            pending.append((there, partial(near_copy, way, c, i)))

    def near_wait(way, c):
        for i in range(2):
            near_copy(way, c, i).wait_recv()

    def coef_copy(b, way):
        return remote(
            proj.at[b],
            proj_near.at[way, b],
            coef_send_sem.at[b],
            coef_recv_sem.at[b],
            "st",
            to(way),
        )

    def coef_start(b):
        if not moved:
            return
        for way in (RIGHT, LEFT):
            there = both(origin[way], sends[way])

            @pl.when(there)
            def _():
                coef_copy(b, way).start()

            pending.append((there, partial(coef_copy, b, way)))


    def share_copy(b, t, way, c, here):
        slot = jnp.where(jnp.logical_and(t == here, way == LEFT), sts, t)
        return remote(
            share.at[b, t, c],
            share_recv.at[way, b, t, c],
            share_send_sem.at[b, t],
            share_recv_sem.at[b, slot, c],
            "st",
            to(way),
        )

    def share_whole(b, t, way, begin):
        at = pl.ds(begin, cells - begin)
        return remote(
            share.at[b, t, at],
            share_recv.at[way, b, t, at],
            share_send_sem.at[b, t],
            share_recv_sem.at[b, t, 0],
            "st",
            to(way),
        )

    def ahead(way):
        if way == RIGHT:
            return steps - s, lambda i: steps - i
        return s, lambda i: i

    def share_cell(b, c):
        found = dot_nt(proj[b], res_ref[c])
        for t in range(sts):
            piece = found[t * width : (t + 1) * width, :]
            share[b, t, c] = piece.astype(BF16)

            @pl.when(t == s)
            def _():
                retained[b, c] = -piece

    def retain(b, c):
        retained[b, c] += dot_nn(mix[b, own, :], states[b, c])

    def share_start(b):
        def one(i, carry):
            c = lax.rem(i + moved, cells)

            @pl.when(c < given[b])
            def _():
                retained[b, c] = jnp.zeros(retained.shape[2:], F32)

            @pl.when(c >= given[b])
            def _():
                share_cell(b, c)

            for way in (RIGHT, LEFT):

                @pl.when(both(origin[way], c >= moved))
                def _():
                    share_copy(b, ahead(way)[1](0), way, c, to(way)).start()

            @pl.when(c >= given[b])
            def _():
                retain(b, c)

            return carry

        def rest(i, carry):
            for way in (RIGHT, LEFT):

                @pl.when(origin[way])
                def _():
                    t = ahead(way)[1](lax.div(i, kept) + 1)
                    share_copy(b, t, way, lax.rem(i, kept) + moved, to(way)).start()

            return carry

        kept = cells - moved

        @pl.when(ends)
        def _():
            lax.fori_loop(0, kept, one, 0)
            lax.fori_loop(0, (steps - 1) * kept, rest, 0)
            lax.fori_loop(kept, cells, one, 0)

    def share_drain(b):
        def one(t, carry):
            for way, passed in ((RIGHT, t > s), (LEFT, t < s)):

                @pl.when(both(passed, origin[way]))
                def _():
                    share_whole(b, t, way, moved).wait_send()

                @pl.when(both(passed, jnp.logical_not(origin[way])))
                def _():
                    share_whole(b, t, way, 0).wait_send()

            return carry

        lax.fori_loop(0, sts, one, 0)

    def absorb(b, way, t, c):
        share_copy(b, t, way, c, s).wait_recv()

        @pl.when(t == s)
        def _():
            retained[b, c] -= share_recv[way, b, t, c].astype(F32)

        @pl.when(t != s)
        def _():
            found = share[b, t, c].astype(F32) + share_recv[way, b, t, c].astype(F32)
            share[b, t, c] = found.astype(BF16)
            if given[b]:

                @pl.when(both(to_end[way], c < given[b]))
                def _():
                    share[b, t, c] = (found + near_term[b, c]).astype(BF16)

            share_copy(b, t, way, c, to(way)).start()

    def absorb_near(b, way, c):
        if b == 0:

            @pl.when(c >= max(given))
            def _():
                near_wait(way, c)

        @pl.when(c == 0)
        def _():
            coef_copy(b, way).wait_recv()

        found = dot_nt(proj_near[way, b], res_near[way, c])
        if given[b]:

            @pl.when(c < given[b])
            def _():
                at = (0 if way == RIGHT else steps) * width
                end = slice(at, at + width)
                near_term[b, c] = found[end, :] - dot_nn(mix[b, end, :], states[b, c])

        for t in reversed(range(sts)) if way == RIGHT else range(sts):
            piece = found[t * width : (t + 1) * width, :]

            @pl.when(t > s if way == RIGHT else t < s)
            def _():
                share[b, t, c] = (share[b, t, c].astype(F32) + piece).astype(BF16)

            @pl.when(t == s)
            def _():
                retained[b, c] -= piece

    def chain(turns, begin, end):
        def one(j, carry):
            for b, offset in turns:
                chain_step(b, j + offset)
            return carry

        lax.fori_loop(begin, end, one, 0)

    def chain_step(b, j):
        @pl.when(both(jnp.logical_not(ends), j < cells))
        def _():
            share_cell(b, j)
            retain(b, j)

        for way in (RIGHT, LEFT):
            m = j - lag[way]
            i = lax.div(jnp.maximum(m, 0), cells)
            c = lax.rem(jnp.maximum(m, 0), cells)
            number, target = ahead(way)
            here = both(receives[way], m >= 0, i <= number)
            near = both(near_end[way], c < moved)
            if moved:

                @pl.when(both(here, near, i == 0))
                def _():
                    absorb_near(b, way, c)

                @pl.when(both(here, near, i < number))
                def _():
                    share_copy(b, target(i), way, c, to(way)).start()

            @pl.when(both(here, jnp.logical_not(near)))
            def _():
                absorb(b, way, target(i), c)

        c = j - done_at

        @pl.when(both(c >= 0, c < cells))
        def _():
            alive = jnp.where(c < count, 1.0, 0.0).astype(BF16)
            out_ref[b, c] = retained[b, c].astype(BF16) * alive
            pltpu.make_async_copy(out_ref.at[b, c], out_hbm.at[b, c], out_sem.at[b]).start()


    for b in range(blocks):
        part[b] = jnp.zeros(part.shape[1:], F32)
    @pl.when(ends)
    def _():
        relayout()
        meet()

    for i in range(2):
        near_start(0, i)
    start_load(0).wait()
    stiff_load(pl.ds(0, nodes)).wait()
    operator_begin(0, 0, lambda: pl.when(jnp.logical_not(ends))(meet))
    operator_end(0, 0)
    operator_begin(1, 0)
    for b in range(1, blocks):
        start_load(b).wait()
        operator_begin(0, b)
    for b in range(blocks):
        operator_end(1, b)
        if b == 0:
            for way in (RIGHT, LEFT):
                gather_own(0, way, True)
            for i in range(2):
                near_start(1, i)
            pl.when(jnp.logical_not(ends))(relayout)
            for later in range(1, blocks):
                operator_end(0, later)
                operator_begin(1, later)
        if b == 1:
            for way in (RIGHT, LEFT):
                gather_own(1, way, origin[way])
    for c in range(2, moved):
        for i in range(2):
            near_start(c, i)

    half = cells // 2
    whole = steps * cells
    links = done_at + cells
    over = 3 * cells // 4
    cut_one = jnp.where(ends, done_at, cells // 2)
    cut_two = jnp.where(ends, done_at + 2, cells)
    gather_flat(0, 0, whole)
    reduce_start(0)
    for b in range(blocks):
        following, previous = b + 1 < blocks, b > 0
        if following:
            gather_flat(b + 1, 0, half)
        if previous:
            chain([(b - 1, 0)], over if b > 1 else 0, cut_one)
        reduce_middle(b)
        if following:
            gather_flat(b + 1, half, cells)
        if previous:
            chain([(b - 1, 0)], cut_one, cut_two)
        reduce_end(b)
        coefficients(b)
        coef_start(b)
        share_start(b)
        if previous:
            chain([(b - 1, 0)], cut_two, links - over)
            chain([(b - 1, links - over), (b, 0)], 0, over)
        if following:
            gather_flat(b + 1, cells, whole)
            reduce_start(b + 1)
    chain([(blocks - 1, 0)], over if blocks > 1 else 0, links)

    for there, make in pending:

        @pl.when(there)
        def _():
            make().wait_send()

    for b in range(blocks):
        gather_drain(b)
        reduce_drain(b)
        share_drain(b)
        give_drain(b)
        pltpu.make_async_copy(out_ref.at[b], out_hbm.at[b], out_sem.at[b]).wait()


def on_device(start_block, resident, stiffness, cell_scale, potential, cell_count, face_index):
    blocks, cells, width, nodes = start_block.shape
    res = resident.shape[0]
    face = face_index.shape[2]
    doms, sts = lax.axis_size("dom"), lax.axis_size("st")
    total_states = sts * width
    rows = -(-(res + total_states) // (16 * doms)) * 16
    moved = 3 * cells // 8 if sts > 3 else 0
    given = tuple(min(moved, (2 * b + 1) * cells // 8) for b in range(blocks))
    sizes = (doms, sts, blocks, cells, width, nodes, face, res, rows, moved, given)
    near = max(moved, 1)
    dma = pltpu.SemaphoreType.DMA
    vmem = pl.BlockSpec(memory_space=pltpu.VMEM)
    smem = pl.BlockSpec(memory_space=pltpu.SMEM)
    anywhere = pl.BlockSpec(memory_space=pl.ANY)
    far = pl.BlockSpec(memory_space=pltpu.HBM)

    def hold(array):
        return pltpu.with_memory_space_constraint(array, pltpu.HBM)

    return pl.pallas_call(
        partial(kernel, sizes),
        out_shape=jax.ShapeDtypeStruct((blocks, cells, width, nodes), BF16),
        in_specs=[smem, smem, far, far, far, vmem, vmem],
        out_specs=anywhere,
        scratch_shapes=[
            pltpu.VMEM((blocks, cells, width, nodes), BF16),
            pltpu.VMEM((nodes, nodes), BF16),
            pltpu.VMEM((blocks, cells, width, nodes), BF16),
            pltpu.VMEM((blocks, cells * width, nodes), F32),
            pltpu.VMEM((blocks, cells * width, nodes), BF16),
            pltpu.VMEM((blocks, cells, total_states, nodes), BF16),
            pltpu.VMEM((blocks, doms * rows, total_states), F32),
            pltpu.VMEM((blocks, doms * rows, total_states), WIRE),
            pltpu.VMEM((blocks, doms, rows, total_states), WIRE),
            pltpu.VMEM((blocks, doms * rows, total_states), WIRE),
            pltpu.VMEM((blocks, total_states, total_states), BF16),
            pltpu.VMEM((blocks, total_states, res), BF16),
            pltpu.VMEM((blocks, sts, cells, width, nodes), BF16),
            pltpu.VMEM((2, blocks, sts, cells, width, nodes), BF16),
            pltpu.VMEM((nodes, cells, res), BF16),
            pltpu.VMEM((res // 128, face * cells, 128), F32),
            pltpu.VMEM((cells, nodes, res), BF16),
            pltpu.VMEM((2, near, nodes, res), BF16),
            pltpu.VMEM((2, blocks, total_states, res), BF16),
            pltpu.VMEM((blocks, cells, width, nodes), F32),
            pltpu.VMEM((blocks, res + total_states, total_states), F32),
            pltpu.VMEM((blocks, res + total_states, total_states), WIRE),
            pltpu.VMEM((blocks, res + total_states, total_states), WIRE),
            pltpu.VMEM((blocks, near, width, nodes), F32),
            pltpu.VMEM((2, blocks, 2, width, face), F32),
            pltpu.VMEM((2, blocks, 2, width, face), F32),
            dma((2, blocks, 2)),
            dma((2, blocks, 2)),
            dma((blocks, 2, sts)),
            dma((blocks, max(sts - 1, 1), cells)),
            dma((blocks,)),
            dma((blocks,)),
            dma((blocks,)),
            dma((blocks,)),
            dma((blocks, sts)),
            dma((blocks, sts + 1, cells)),
            dma,
            dma((blocks,)),
            dma,
            dma((blocks,)),
            dma((near, 2)),
            dma((near, 2)),
            dma((blocks,)),
            dma((blocks,)),
            dma((blocks,)),
            dma((blocks,)),
        ],
        compiler_params=pltpu.CompilerParams(
            collective_id=0, has_side_effects=True, vmem_limit_bytes=36 * 1024 * 1024
        ),
    )(
        hold(cell_scale),
        cell_count,
        hold(start_block),
        hold(jnp.transpose(resident, (2, 1, 0))),
        hold(stiffness),
        hold(potential),
        hold(face_index),
    )


def solution(mesh):
    return jax.shard_map(
        on_device,
        mesh=mesh,
        in_specs=(
            P(None, "dom", "st", None),
            P("st", "dom", None),
            P(),
            P("dom"),
            P("dom", None),
            P("dom"),
            P("dom", None, None),
        ),
        out_specs=P(None, "dom", "st", None),
        check_vma=False,
    )
```

```python
from functools import partial

import jax
import jax.numpy as jnp
from jax import lax
from jax.experimental import pallas as pl
from jax.experimental.pallas import tpu as pltpu
from jax.sharding import PartitionSpec as P

CENTER = 0.5
HALF_WIDTH = 2.0
EPSILON = 1e-06
F32 = jnp.float32
BF16 = jnp.bfloat16
WIRE = BF16
RIGHT, LEFT = 0, 1
LAG = 6
GAP = 4
MESH = pl.DeviceIdType.MESH


def dot_nn(a, b, precision=None):
    return lax.dot_general(
        a, b, (((1,), (0,)), ((), ())), precision=precision, preferred_element_type=F32
    )


def dot_nt(a, b, precision=None):
    return lax.dot_general(
        a, b, (((1,), (1,)), ((), ())), precision=precision, preferred_element_type=F32
    )


def both(*conditions):
    found = conditions[0]
    for condition in conditions[1:]:
        found = jnp.logical_and(found, condition)
    return found


def kernel(
    sizes,
    scale_ref,
    count_ref,
    start_hbm,
    res_hbm,
    stiff_hbm,
    pot_ref,
    face_ref,
    out_hbm,
    start_ref,
    stiff_ref,
    out_ref,
    local,
    inner,
    states,
    part,
    wire,
    part_recv,
    total,
    mix,
    proj,
    share,
    share_recv,
    res_in,
    res_wide,
    res_ref,
    res_near,
    proj_near,
    retained,
    near_part,
    near_wire,
    near_got,
    near_term,
    face_out,
    face_in,
    face_send_sem,
    face_recv_sem,
    gather_send_sem,
    gather_recv_sem,
    one_send_sem,
    one_recv_sem,
    two_send_sem,
    two_recv_sem,
    share_send_sem,
    share_recv_sem,
    load_sem,
    start_sem,
    stiff_sem,
    out_sem,
    near_send_sem,
    near_recv_sem,
    coef_send_sem,
    coef_recv_sem,
    give_send_sem,
    give_recv_sem,
):
    doms, sts, blocks, cells, width, nodes, face, res, rows, moved, given = sizes
    total_states = sts * width
    total_nodes = float(doms * cells * nodes)
    window = (nodes - face) // 128 * 128
    offset = nodes - face - window
    d = lax.axis_index("dom")
    s = lax.axis_index("st")
    has_right, has_left = s < sts - 1, s > 0
    has_next, has_prev = d < doms - 1, d > 0
    own = pl.ds(pl.multiple_of(s * width, width), width)
    steps = sts - 1
    last_step = jnp.maximum(s, steps - s)
    ends = jnp.logical_or(s == 0, s == steps)
    pending = []
    count = count_ref[0]
    scale = [scale_ref[c] for c in range(cells)]
    live = [jnp.where(c < count, 1.0, 0.0).astype(F32) for c in range(cells)]
    last = [jnp.where(c == count - 1, 1.0, 0.0).astype(F32) for c in range(cells)]

    def start_load(b):
        return pltpu.make_async_copy(start_hbm.at[b], start_ref.at[b], start_sem.at[b])

    def cuts(extent, number):
        step = -(-extent // (number * 16)) * 16
        return [pl.ds(at, min(step, extent - at)) for at in range(0, extent, step)]

    def stiff_load(at):
        return pltpu.make_async_copy(stiff_hbm.at[at], stiff_ref.at[at], stiff_sem)

    def res_load(at):
        return pltpu.make_async_copy(res_hbm.at[at], res_in.at[at], load_sem)

    def res_start():
        for at in cuts(nodes, 4):
            res_load(at).start()

    pl.when(ends)(res_start)
    start_load(0).start()
    for at in cuts(nodes, 2):
        stiff_load(at).start()
    for b in range(1, blocks):
        start_load(b).start()
    pl.when(jnp.logical_not(ends))(res_start)

    origin = {RIGHT: s == 0, LEFT: s == steps}
    lag = {RIGHT: LAG * jnp.maximum(s - 1, 0), LEFT: LAG * jnp.maximum(steps - 1 - s, 0)}
    early = sts > 3
    done_at = jnp.maximum(
        jnp.where(s > 0, lag[RIGHT] + (steps - s) * cells, 0),
        jnp.where(s < steps, lag[LEFT] + s * cells, 0),
    )
    sends = {RIGHT: has_right, LEFT: has_left}
    receives = {RIGHT: has_left, LEFT: has_right}
    near_end = {RIGHT: s == 1, LEFT: s == steps - 1}
    to_end = {RIGHT: s == steps - 1, LEFT: s == 1}
    gap = {way: jnp.where(near_end[way], GAP if moved else 0, 0) for way in (RIGHT, LEFT)}
    gathered_at = jnp.maximum(
        jnp.where(s > 0, gap[RIGHT] + (s - 1) * cells, 0),
        jnp.where(s < steps, gap[LEFT] + (steps - s - 1) * cells, 0),
    )

    def to(way):
        return s + 1 if way == RIGHT else s - 1

    def dom_peer(k):
        return lax.rem(d + k, doms)

    barrier = pltpu.get_barrier_semaphore()

    def greet(k, carry):
        pl.semaphore_signal(barrier, inc=1, device_id={"dom": dom_peer(k)}, device_id_type=MESH)
        return carry

    lax.fori_loop(1, doms, greet, 0)
    for way in (RIGHT, LEFT):

        @pl.when(sends[way])
        def _():
            pl.semaphore_signal(barrier, inc=1, device_id={"st": to(way)}, device_id_type=MESH)

    def meet():
        neighbours = has_right.astype(jnp.int32) + has_left.astype(jnp.int32)
        pl.semaphore_wait(barrier, doms - 1 + neighbours)

    def remote(src, dst, send_sem, recv_sem, axis, peer):
        return pltpu.make_async_remote_copy(
            src_ref=src,
            dst_ref=dst,
            send_sem=send_sem,
            recv_sem=recv_sem,
            device_id={axis: peer},
            device_id_type=MESH,
        )

    def one_hot(row, first, extent):
        node = lax.broadcasted_iota(jnp.int32, (extent, face), 0) + first
        if row == 0:
            node = node + (count - 1) * nodes
        return jnp.where(face_ref[0, row : row + 1, :] == node, 1.0, 0.0).astype(F32)

    def mask(c):
        return live[c].astype(BF16)

    def relayout():
        res_load(pl.ds(0, nodes)).wait()
        for chunk in range(nodes // face):
            at = slice(chunk * face, (chunk + 1) * face)
            wide = res_in[at].astype(F32).reshape(face * cells, res)
            for h in range(res // 128):
                lanes = slice(h * 128, (h + 1) * 128)
                res_wide[h] = wide[:, lanes]
                for c in range(cells):
                    res_ref[c, at, lanes] = res_wide[h, pl.ds(c, face, stride=cells), :].astype(BF16)


    def rows_of(c):
        return slice(c * width, (c + 1) * width)

    def face_copy(step, b, way):
        return remote(
            face_out.at[step, b, way],
            face_in.at[step, b, way],
            face_send_sem.at[step, b, way],
            face_recv_sem.at[step, b, way],
            "dom",
            d + 1 if way == RIGHT else d - 1,
        )

    def first(b, c):
        if c is None:
            return jnp.concatenate([first(b, i) for i in range(cells)], axis=0)
        return start_ref[b, c] * mask(c)

    def second(b, c):
        return inner[b] if c is None else inner[b, rows_of(c), :]

    def operator_begin(step, b, meanwhile=None):
        field = partial(second if step else first, b)
        local[b] = dot_nn(field(None), stiff_ref[...])
        last_tail = jnp.zeros((width, nodes - window), F32)
        for c in range(cells):
            value = scale[c] * local[b, rows_of(c), :] + pot_ref[c : c + 1, :] * field(c).astype(F32)
            local[b, rows_of(c), :] = value
            last_tail = last_tail + last[c] * value[:, window:]
        face_out[step, b, RIGHT] = dot_nn(
            last_tail, one_hot(0, window, nodes - window), lax.Precision.HIGHEST
        )
        face_out[step, b, LEFT] = dot_nn(
            local[b, rows_of(0), :face], one_hot(1, 0, face), lax.Precision.HIGHEST
        )
        if meanwhile is not None:
            meanwhile()
        for way, there in ((RIGHT, has_next), (LEFT, has_prev)):

            @pl.when(there)
            def _():
                face_copy(step, b, way).start()

            pending.append((there, partial(face_copy, step, b, way)))
        for c in range(cells - 1):
            pair = live[c + 1]
            tail = local[b, rows_of(c), window:]
            head = local[b, rows_of(c + 1), :face]
            padded = head
            if offset:
                padded = jnp.concatenate([jnp.zeros((width, offset), F32), head], axis=1)
            local[b, rows_of(c), window:] = tail + pair * padded
            local[b, rows_of(c + 1), :face] = head + pair * tail[:, offset:]

    def operator_end(step, b):
        for way, source in ((RIGHT, has_prev), (LEFT, has_next)):

            @pl.when(source)
            def _():
                face_copy(step, b, way).wait_recv()

            @pl.when(jnp.logical_not(source))
            def _():
                face_in[step, b, way] = jnp.zeros((width, face), F32)

        local[b, rows_of(0), :face] += dot_nt(
            face_in[step, b, RIGHT], one_hot(1, 0, face), lax.Precision.HIGHEST
        )
        tail_add = dot_nt(
            face_in[step, b, LEFT], one_hot(0, window, nodes - window), lax.Precision.HIGHEST
        )
        for c in range(cells):
            local[b, rows_of(c), window:] += last[c] * tail_add
        for c in range(cells):
            value = live[c] * local[b, rows_of(c), :]
            if step == 0:
                inner[b, rows_of(c), :] = (
                    (value - CENTER * first(b, c).astype(F32)) / HALF_WIDTH
                ).astype(BF16)
            else:
                states[b, c, own, :] = (
                    2.0 * (value - CENTER * second(b, c).astype(F32)) / HALF_WIDTH
                    - first(b, c).astype(F32)
                ).astype(BF16)


    def of_shard(shard):
        return pl.ds(pl.multiple_of(shard * width, width), width)

    def gather_copy(b, way, shard, c, here):
        at = states.at[b, c, of_shard(shard), :]
        slot = jnp.where(shard > here, shard - 1, shard)
        return remote(
            at, at, gather_send_sem.at[b, way, shard], gather_recv_sem.at[b, slot, c], "st", to(way)
        )

    def gather_whole(b, way, shard, begin):
        at = states.at[b, pl.ds(begin, cells - begin), of_shard(shard), :]
        return remote(
            at, at, gather_send_sem.at[b, way, shard], gather_recv_sem.at[b, 0, 0], "st", to(way)
        )

    def gather_own(b, way, there):
        @pl.when(jnp.logical_and(there, sends[way]))
        def _():
            def one(c, carry):
                gather_copy(b, way, s, c, to(way)).start()
                return carry

            lax.fori_loop(jnp.where(to_end[way], given[b], 0), cells, one, 0)

    def gather_flat(b, begin, end):
        wait = min(5, cells - given[b])

        def one(i, carry):
            for way in (LEFT, RIGHT):
                m = i - gap[way]
                k = lax.div(jnp.maximum(m, 0), cells) + 1
                c = lax.rem(jnp.maximum(m, 0), cells)
                shard = s - k if way == RIGHT else s + k
                here = both(m >= 0, shard >= 0, shard < sts)
                whole = c >= given[b]
                held = jnp.logical_or(whole, jnp.logical_not(ends))
                passed = jnp.logical_or(whole, jnp.logical_not(to_end[way]))

                @pl.when(both(here, held))
                def _():
                    gather_copy(b, way, shard, c, s).wait_recv()

                    @pl.when(both(sends[way], passed))
                    def _():
                        gather_copy(b, way, shard, c, to(way)).start()

                if b + 1 < blocks:
                    final = shard == (0 if way == RIGHT else steps)

                    @pl.when(both(here, final, c == cells - 1))
                    def _():
                        gather_own(b + 1, way, True)

            c = i - gathered_at

            @pl.when(both(c >= jnp.where(ends, given[b], 0), c < cells))
            def _():
                contract(b, c)

            if given[b]:
                for way in (RIGHT, LEFT):

                    @pl.when(both(near_end[way], c >= wait, c < wait + given[b]))
                    def _():
                        contract_near(b, way, c - wait)

            return carry

        lax.fori_loop(begin, end, one, 0)

    def gather_drain(b):
        def one(shard, carry):
            for way, passed in ((RIGHT, shard <= s), (LEFT, shard >= s)):

                @pl.when(both(passed, sends[way], to_end[way]))
                def _():
                    gather_whole(b, way, shard, given[b]).wait_send()

                @pl.when(both(passed, sends[way], jnp.logical_not(to_end[way])))
                def _():
                    gather_whole(b, way, shard, 0).wait_send()

            return carry

        lax.fori_loop(0, sts, one, 0)


    def contract(b, c):
        block = states[b, c]
        found = dot_nn(block, res_ref[c])
        for h in range(res // total_states):
            at = slice(h * total_states, (h + 1) * total_states)
            part[b, at, :] += found[:, at]
        part[b, res : res + total_states, :] += dot_nt(block, block)

    def give_copy(b, way):
        return remote(
            near_wire.at[b],
            near_got.at[b],
            give_send_sem.at[b],
            give_recv_sem.at[b],
            "st",
            to(1 - way),
        )

    def contract_near(b, way, c):
        @pl.when(c >= (given[b - 1] if b else 0))
        def _():
            near_wait(way, c)

        @pl.when(c == 0)
        def _():
            near_part[b] = jnp.zeros(near_part.shape[1:], F32)

        block = states[b, c]
        found = dot_nn(block, res_near[way, c])
        for h in range(res // total_states):
            at = slice(h * total_states, (h + 1) * total_states)
            near_part[b, at, :] += found[:, at]
        near_part[b, res : res + total_states, :] += dot_nt(block, block)

        @pl.when(c == given[b] - 1)
        def _():
            near_wire[b] = near_part[b].astype(WIRE)
            give_copy(b, way).start()

    def give_end(b):
        if not given[b]:
            return
        at = slice(0, res + total_states)

        @pl.when(ends)
        def _():
            give_copy(b, RIGHT).wait_recv()
            part[b, at, :] += near_got[b].astype(F32)

    def give_drain(b):
        if not given[b]:
            return

        @pl.when(jnp.logical_or(near_end[RIGHT], near_end[LEFT]))
        def _():
            give_copy(b, RIGHT).wait_send()

    def slice_of(peer):
        return pl.ds(pl.multiple_of(peer * rows, 16), rows)

    def one_copy(b, k):
        peer = dom_peer(k)
        return remote(
            wire.at[b, slice_of(peer)],
            part_recv.at[b, k],
            one_send_sem.at[b],
            one_recv_sem.at[b],
            "dom",
            peer,
        )

    def two_copy(b, k):
        at = total.at[b, slice_of(d)]
        return remote(at, at, two_send_sem.at[b], two_recv_sem.at[b], "dom", dom_peer(k))


    def one_whole(b):
        at = part_recv.at[b, pl.ds(1, doms - 1)]
        return remote(at, at, one_send_sem.at[b], one_recv_sem.at[b], "dom", dom_peer(1))

    def two_whole(b):
        at = total.at[b, pl.ds(0, (doms - 1) * rows)]
        return remote(at, at, two_send_sem.at[b], two_recv_sem.at[b], "dom", dom_peer(1))

    def peers(body):
        def step(k, carry):
            body(k)
            return carry

        lax.fori_loop(1, doms, step, 0)

    def reduce_start(b):
        give_end(b)
        wire[b] = part[b].astype(WIRE)
        peers(lambda k: one_copy(b, k).start())

    def reduce_middle(b):
        one_whole(b).wait_recv()

        def add(k, found):
            return found + part_recv[b, k].astype(F32)

        found = lax.fori_loop(1, doms, add, part[b, slice_of(d), :])
        total[b, slice_of(d), :] = found.astype(WIRE)
        peers(lambda k: two_copy(b, k).start())

    def reduce_end(b):
        two_whole(b).wait_recv()

    def reduce_drain(b):
        one_whole(b).wait_send()
        two_whole(b).wait_send()

    def coefficients(b):
        gram = total[b, res : res + total_states, :].astype(F32)
        shape = (total_states, total_states)
        eye = (
            lax.broadcasted_iota(jnp.int32, shape, 0) == lax.broadcasted_iota(jnp.int32, shape, 1)
        ).astype(F32)
        along = jnp.sum(gram * eye, axis=0, keepdims=True) / total_nodes + EPSILON
        down = jnp.sum(gram * eye, axis=1, keepdims=True) / total_nodes + EPSILON
        root_i, root_j = lax.rsqrt(along), lax.rsqrt(down)
        mixing = root_i * (1.5 * eye - 0.5 * (gram * root_i * root_j / total_nodes))
        mix[b] = mixing.astype(BF16)
        for h in range(res // total_states):
            at = slice(h * total_states, (h + 1) * total_states)
            proj[b, :, at] = dot_nn(
                mixing, total[b, at, :].astype(F32), lax.Precision.HIGHEST
            ).astype(BF16)


    def near_copy(way, c, i):
        at = cuts(nodes, 2)[i]
        return remote(
            res_ref.at[c, at],
            res_near.at[way, c, at],
            near_send_sem.at[c, i],
            near_recv_sem.at[c, i],
            "st",
            to(way),
        )

    def near_start(c, i):
        if c >= moved:
            return
        for way in (RIGHT, LEFT):
            there = both(origin[way], sends[way])

            @pl.when(there)
            def _():
                near_copy(way, c, i).start()

            pending.append((there, partial(near_copy, way, c, i)))

    def near_wait(way, c):
        for i in range(2):
            near_copy(way, c, i).wait_recv()

    def coef_copy(b, way):
        return remote(
            proj.at[b],
            proj_near.at[way, b],
            coef_send_sem.at[b],
            coef_recv_sem.at[b],
            "st",
            to(way),
        )

    def coef_start(b):
        if not moved:
            return
        for way in (RIGHT, LEFT):
            there = both(origin[way], sends[way])

            @pl.when(there)
            def _():
                coef_copy(b, way).start()

            pending.append((there, partial(coef_copy, b, way)))


    def share_copy(b, t, way, c, here):
        slot = jnp.where(jnp.logical_and(t == here, way == LEFT), sts, t)
        return remote(
            share.at[b, t, c],
            share_recv.at[way, b, t, c],
            share_send_sem.at[b, t],
            share_recv_sem.at[b, slot, c],
            "st",
            to(way),
        )

    def share_whole(b, t, way, begin):
        at = pl.ds(begin, cells - begin)
        return remote(
            share.at[b, t, at],
            share_recv.at[way, b, t, at],
            share_send_sem.at[b, t],
            share_recv_sem.at[b, t, 0],
            "st",
            to(way),
        )

    def ahead(way):
        if way == RIGHT:
            return steps - s, lambda i: steps - i
        return s, lambda i: i

    def share_cell(b, c):
        found = dot_nt(proj[b], res_ref[c])
        for t in range(sts):
            piece = found[t * width : (t + 1) * width, :]
            share[b, t, c] = piece.astype(BF16)

            @pl.when(t == s)
            def _():
                retained[b, c] = -piece

    def retain(b, c):
        retained[b, c] += dot_nn(mix[b, own, :], states[b, c])

    def share_start(b):
        def one(i, carry):
            c = lax.rem(i + moved, cells)

            @pl.when(c < given[b])
            def _():
                retained[b, c] = jnp.zeros(retained.shape[2:], F32)

            @pl.when(c >= given[b])
            def _():
                share_cell(b, c)

            for way in (RIGHT, LEFT):

                @pl.when(both(origin[way], c >= moved))
                def _():
                    share_copy(b, ahead(way)[1](0), way, c, to(way)).start()

            @pl.when(c >= given[b])
            def _():
                retain(b, c)

            return carry

        def rest(i, carry):
            for way in (RIGHT, LEFT):

                @pl.when(origin[way])
                def _():
                    t = ahead(way)[1](lax.div(i, kept) + 1)
                    share_copy(b, t, way, lax.rem(i, kept) + moved, to(way)).start()

            return carry

        kept = cells - moved

        @pl.when(ends)
        def _():
            lax.fori_loop(0, kept, one, 0)
            lax.fori_loop(0, (steps - 1) * kept, rest, 0)
            lax.fori_loop(kept, cells, one, 0)

    def share_drain(b):
        def one(t, carry):
            for way, passed in ((RIGHT, t > s), (LEFT, t < s)):

                @pl.when(both(passed, origin[way]))
                def _():
                    share_whole(b, t, way, moved).wait_send()

                @pl.when(both(passed, jnp.logical_not(origin[way])))
                def _():
                    share_whole(b, t, way, 0).wait_send()

            return carry

        lax.fori_loop(0, sts, one, 0)

    def absorb(b, way, t, c):
        share_copy(b, t, way, c, s).wait_recv()

        @pl.when(t == s)
        def _():
            retained[b, c] -= share_recv[way, b, t, c].astype(F32)

        @pl.when(t != s)
        def _():
            found = share[b, t, c].astype(F32) + share_recv[way, b, t, c].astype(F32)
            share[b, t, c] = found.astype(BF16)
            if given[b]:

                @pl.when(both(to_end[way], c < given[b]))
                def _():
                    share[b, t, c] = (found + near_term[b, c]).astype(BF16)

            share_copy(b, t, way, c, to(way)).start()

    def absorb_near(b, way, c):
        if b == 0:

            @pl.when(c >= max(given))
            def _():
                near_wait(way, c)

        @pl.when(c == 0)
        def _():
            coef_copy(b, way).wait_recv()

        found = dot_nt(proj_near[way, b], res_near[way, c])
        if given[b]:

            @pl.when(c < given[b])
            def _():
                at = (0 if way == RIGHT else steps) * width
                end = slice(at, at + width)
                near_term[b, c] = found[end, :] - dot_nn(mix[b, end, :], states[b, c])

        for t in reversed(range(sts)) if way == RIGHT else range(sts):
            piece = found[t * width : (t + 1) * width, :]

            @pl.when(t > s if way == RIGHT else t < s)
            def _():
                share[b, t, c] = (share[b, t, c].astype(F32) + piece).astype(BF16)

            @pl.when(t == s)
            def _():
                retained[b, c] -= piece

    def chain(turns, begin, end, ready=None):
        def one(j, carry):
            for b, offset in turns:
                chain_step(b, j + offset)
            if ready is not None and early:
                share_middle(ready, j - cells - 2)
            return carry

        lax.fori_loop(begin, end, one, 0)

    def share_middle(b, c):
        @pl.when(both(jnp.logical_not(ends), c >= 0, c < cells))
        def _():
            share_cell(b, c)
            retain(b, c)

    def chain_step(b, j):
        if b == 0 or not early:
            share_middle(b, j)
        for way in (RIGHT, LEFT):
            m = j - lag[way]
            i = lax.div(jnp.maximum(m, 0), cells)
            c = lax.rem(jnp.maximum(m, 0), cells)
            number, target = ahead(way)
            here = both(receives[way], m >= 0, i <= number)
            near = both(near_end[way], c < moved)
            if moved:

                @pl.when(both(here, near, i == 0))
                def _():
                    absorb_near(b, way, c)

                @pl.when(both(here, near, i < number))
                def _():
                    share_copy(b, target(i), way, c, to(way)).start()

            @pl.when(both(here, jnp.logical_not(near)))
            def _():
                absorb(b, way, target(i), c)

        c = j - done_at

        @pl.when(both(c >= 0, c < cells))
        def _():
            alive = jnp.where(c < count, 1.0, 0.0).astype(BF16)
            out_ref[b, c] = retained[b, c].astype(BF16) * alive
            pltpu.make_async_copy(out_ref.at[b, c], out_hbm.at[b, c], out_sem.at[b]).start()


    for b in range(blocks):
        part[b] = jnp.zeros(part.shape[1:], F32)
    @pl.when(ends)
    def _():
        relayout()
        meet()

    for i in range(2):
        near_start(0, i)
    start_load(0).wait()
    stiff_load(pl.ds(0, nodes)).wait()
    operator_begin(0, 0, lambda: pl.when(jnp.logical_not(ends))(meet))
    operator_end(0, 0)
    operator_begin(1, 0)
    for b in range(1, blocks):
        start_load(b).wait()
        operator_begin(0, b)
    for b in range(blocks):
        operator_end(1, b)
        if b == 0:
            for way in (RIGHT, LEFT):
                gather_own(0, way, True)
            for i in range(2):
                near_start(1, i)
            pl.when(jnp.logical_not(ends))(relayout)
            for later in range(1, blocks):
                operator_end(0, later)
                operator_begin(1, later)
        if b == 1:
            for way in (RIGHT, LEFT):
                gather_own(1, way, origin[way])
    for c in range(2, moved):
        for i in range(2):
            near_start(c, i)

    half = cells // 2
    whole = steps * cells
    links = done_at + cells
    over = cells - 2
    cut_one = jnp.where(ends, done_at, cells - 1)
    cut_two = jnp.where(ends, done_at, cells + 2)
    gather_flat(0, 0, whole)
    reduce_start(0)
    for b in range(blocks):
        following, previous = b + 1 < blocks, b > 0
        if following:
            gather_flat(b + 1, 0, half)
        if previous:
            chain([(b - 1, 0)], over if b > 1 else 0, cut_one)
        reduce_middle(b)
        if following:
            gather_flat(b + 1, half, cells)
        if previous:
            chain([(b - 1, 0)], cut_one, cut_two)
        reduce_end(b)
        coefficients(b)
        coef_start(b)
        share_start(b)
        if previous:
            chain([(b - 1, 0)], cut_two, links - over, b)
            chain([(b - 1, links - over), (b, 0)], 0, over)
        if following:
            gather_flat(b + 1, cells, whole)
            reduce_start(b + 1)
    chain([(blocks - 1, 0)], over if blocks > 1 else 0, links)

    for there, make in pending:

        @pl.when(there)
        def _():
            make().wait_send()

    for b in range(blocks):
        gather_drain(b)
        reduce_drain(b)
        share_drain(b)
        give_drain(b)
        pltpu.make_async_copy(out_ref.at[b], out_hbm.at[b], out_sem.at[b]).wait()


def on_device(start_block, resident, stiffness, cell_scale, potential, cell_count, face_index):
    blocks, cells, width, nodes = start_block.shape
    res = resident.shape[0]
    face = face_index.shape[2]
    doms, sts = lax.axis_size("dom"), lax.axis_size("st")
    total_states = sts * width
    rows = -(-(res + total_states) // (16 * doms)) * 16
    moved = 3 * cells // 8 if sts > 3 else 0
    given = tuple(min(moved, (2 * b + 1) * cells // 8) for b in range(blocks))
    sizes = (doms, sts, blocks, cells, width, nodes, face, res, rows, moved, given)
    near = max(moved, 1)
    dma = pltpu.SemaphoreType.DMA
    vmem = pl.BlockSpec(memory_space=pltpu.VMEM)
    smem = pl.BlockSpec(memory_space=pltpu.SMEM)
    anywhere = pl.BlockSpec(memory_space=pl.ANY)
    far = pl.BlockSpec(memory_space=pltpu.HBM)

    def hold(array):
        return pltpu.with_memory_space_constraint(array, pltpu.HBM)

    return pl.pallas_call(
        partial(kernel, sizes),
        out_shape=jax.ShapeDtypeStruct((blocks, cells, width, nodes), BF16),
        in_specs=[smem, smem, far, far, far, vmem, vmem],
        out_specs=anywhere,
        scratch_shapes=[
            pltpu.VMEM((blocks, cells, width, nodes), BF16),
            pltpu.VMEM((nodes, nodes), BF16),
            pltpu.VMEM((blocks, cells, width, nodes), BF16),
            pltpu.VMEM((blocks, cells * width, nodes), F32),
            pltpu.VMEM((blocks, cells * width, nodes), BF16),
            pltpu.VMEM((blocks, cells, total_states, nodes), BF16),
            pltpu.VMEM((blocks, doms * rows, total_states), F32),
            pltpu.VMEM((blocks, doms * rows, total_states), WIRE),
            pltpu.VMEM((blocks, doms, rows, total_states), WIRE),
            pltpu.VMEM((blocks, doms * rows, total_states), WIRE),
            pltpu.VMEM((blocks, total_states, total_states), BF16),
            pltpu.VMEM((blocks, total_states, res), BF16),
            pltpu.VMEM((blocks, sts, cells, width, nodes), BF16),
            pltpu.VMEM((2, blocks, sts, cells, width, nodes), BF16),
            pltpu.VMEM((nodes, cells, res), BF16),
            pltpu.VMEM((res // 128, face * cells, 128), F32),
            pltpu.VMEM((cells, nodes, res), BF16),
            pltpu.VMEM((2, near, nodes, res), BF16),
            pltpu.VMEM((2, blocks, total_states, res), BF16),
            pltpu.VMEM((blocks, cells, width, nodes), F32),
            pltpu.VMEM((blocks, res + total_states, total_states), F32),
            pltpu.VMEM((blocks, res + total_states, total_states), WIRE),
            pltpu.VMEM((blocks, res + total_states, total_states), WIRE),
            pltpu.VMEM((blocks, near, width, nodes), F32),
            pltpu.VMEM((2, blocks, 2, width, face), F32),
            pltpu.VMEM((2, blocks, 2, width, face), F32),
            dma((2, blocks, 2)),
            dma((2, blocks, 2)),
            dma((blocks, 2, sts)),
            dma((blocks, max(sts - 1, 1), cells)),
            dma((blocks,)),
            dma((blocks,)),
            dma((blocks,)),
            dma((blocks,)),
            dma((blocks, sts)),
            dma((blocks, sts + 1, cells)),
            dma,
            dma((blocks,)),
            dma,
            dma((blocks,)),
            dma((near, 2)),
            dma((near, 2)),
            dma((blocks,)),
            dma((blocks,)),
            dma((blocks,)),
            dma((blocks,)),
        ],
        compiler_params=pltpu.CompilerParams(
            collective_id=0, has_side_effects=True, vmem_limit_bytes=36 * 1024 * 1024
        ),
    )(
        hold(cell_scale),
        cell_count,
        hold(start_block),
        hold(jnp.transpose(resident, (2, 1, 0))),
        hold(stiffness),
        hold(potential),
        hold(face_index),
    )


def solution(mesh):
    return jax.shard_map(
        on_device,
        mesh=mesh,
        in_specs=(
            P(None, "dom", "st", None),
            P("st", "dom", None),
            P(),
            P("dom"),
            P("dom", None),
            P("dom"),
            P("dom", None, None),
        ),
        out_specs=P(None, "dom", "st", None),
        check_vma=False,
    )
```

```python
from functools import partial

import jax
import jax.numpy as jnp
from jax import lax
from jax.experimental import pallas as pl
from jax.experimental.pallas import tpu as pltpu
from jax.sharding import PartitionSpec as P

CENTER = 0.5
HALF_WIDTH = 2.0
EPSILON = 1e-06
F32 = jnp.float32
BF16 = jnp.bfloat16
WIRE = BF16
RIGHT, LEFT = 0, 1
LAG = 6
GAP = 4
MESH = pl.DeviceIdType.MESH


def dot_nn(a, b, precision=None):
    return lax.dot_general(
        a, b, (((1,), (0,)), ((), ())), precision=precision, preferred_element_type=F32
    )


def dot_nt(a, b, precision=None):
    return lax.dot_general(
        a, b, (((1,), (1,)), ((), ())), precision=precision, preferred_element_type=F32
    )


def both(*conditions):
    found = conditions[0]
    for condition in conditions[1:]:
        found = jnp.logical_and(found, condition)
    return found


def kernel(
    sizes,
    scale_ref,
    count_ref,
    start_hbm,
    res_hbm,
    stiff_hbm,
    pot_ref,
    face_ref,
    out_hbm,
    start_ref,
    stiff_ref,
    out_ref,
    local,
    inner,
    states,
    part,
    wire,
    part_recv,
    total,
    mix,
    proj,
    share,
    share_recv,
    res_in,
    res_wide,
    res_ref,
    res_near,
    proj_near,
    retained,
    near_part,
    near_wire,
    near_got,
    near_term,
    face_out,
    face_in,
    face_send_sem,
    face_recv_sem,
    gather_send_sem,
    gather_recv_sem,
    one_send_sem,
    one_recv_sem,
    two_send_sem,
    two_recv_sem,
    share_send_sem,
    share_recv_sem,
    load_sem,
    start_sem,
    stiff_sem,
    out_sem,
    near_send_sem,
    near_recv_sem,
    coef_send_sem,
    coef_recv_sem,
    give_send_sem,
    give_recv_sem,
):
    doms, sts, blocks, cells, width, nodes, face, res, rows, moved, given = sizes
    total_states = sts * width
    total_nodes = float(doms * cells * nodes)
    window = (nodes - face) // 128 * 128
    offset = nodes - face - window
    d = lax.axis_index("dom")
    s = lax.axis_index("st")
    has_right, has_left = s < sts - 1, s > 0
    has_next, has_prev = d < doms - 1, d > 0
    own = pl.ds(pl.multiple_of(s * width, width), width)
    steps = sts - 1
    last_step = jnp.maximum(s, steps - s)
    ends = jnp.logical_or(s == 0, s == steps)
    pending = []
    count = count_ref[0]
    scale = [scale_ref[c] for c in range(cells)]
    live = [jnp.where(c < count, 1.0, 0.0).astype(F32) for c in range(cells)]
    last = [jnp.where(c == count - 1, 1.0, 0.0).astype(F32) for c in range(cells)]

    def start_load(b):
        return pltpu.make_async_copy(start_hbm.at[b], start_ref.at[b], start_sem.at[b])

    def cuts(extent, number):
        step = -(-extent // (number * 16)) * 16
        return [pl.ds(at, min(step, extent - at)) for at in range(0, extent, step)]

    def stiff_load(at):
        return pltpu.make_async_copy(stiff_hbm.at[at], stiff_ref.at[at], stiff_sem)

    chunks = nodes // face
    parts = ((0, chunks // 2 + 1), (chunks // 2 + 1, chunks))

    def res_load(i):
        begin, end = parts[i]
        at = pl.ds(begin * face, (end - begin) * face)
        return pltpu.make_async_copy(res_hbm.at[at], res_in.at[at], load_sem.at[i])

    def res_start():
        for i in range(2):
            res_load(i).start()

    pl.when(ends)(res_start)
    start_load(0).start()
    for at in cuts(nodes, 2):
        stiff_load(at).start()
    for b in range(1, blocks):
        start_load(b).start()

    origin = {RIGHT: s == 0, LEFT: s == steps}
    lag = {RIGHT: LAG * jnp.maximum(s - 1, 0), LEFT: LAG * jnp.maximum(steps - 1 - s, 0)}
    early = sts > 3
    done_at = jnp.maximum(
        jnp.where(s > 0, lag[RIGHT] + (steps - s) * cells, 0),
        jnp.where(s < steps, lag[LEFT] + s * cells, 0),
    )
    sends = {RIGHT: has_right, LEFT: has_left}
    receives = {RIGHT: has_left, LEFT: has_right}
    near_end = {RIGHT: s == 1, LEFT: s == steps - 1}
    to_end = {RIGHT: s == steps - 1, LEFT: s == 1}
    gap = {way: jnp.where(near_end[way], GAP if moved else 0, 0) for way in (RIGHT, LEFT)}
    gathered_at = jnp.maximum(
        jnp.where(s > 0, gap[RIGHT] + (s - 1) * cells, 0),
        jnp.where(s < steps, gap[LEFT] + (steps - s - 1) * cells, 0),
    )

    def to(way):
        return s + 1 if way == RIGHT else s - 1

    def dom_peer(k):
        return lax.rem(d + k, doms)

    barrier = pltpu.get_barrier_semaphore()

    def greet(k, carry):
        pl.semaphore_signal(barrier, inc=1, device_id={"dom": dom_peer(k)}, device_id_type=MESH)
        return carry

    lax.fori_loop(1, doms, greet, 0)
    for way in (RIGHT, LEFT):

        @pl.when(sends[way])
        def _():
            pl.semaphore_signal(barrier, inc=1, device_id={"st": to(way)}, device_id_type=MESH)

    def meet():
        neighbours = has_right.astype(jnp.int32) + has_left.astype(jnp.int32)
        pl.semaphore_wait(barrier, doms - 1 + neighbours)

    def remote(src, dst, send_sem, recv_sem, axis, peer):
        return pltpu.make_async_remote_copy(
            src_ref=src,
            dst_ref=dst,
            send_sem=send_sem,
            recv_sem=recv_sem,
            device_id={axis: peer},
            device_id_type=MESH,
        )

    def one_hot(row, first, extent):
        node = lax.broadcasted_iota(jnp.int32, (extent, face), 0) + first
        if row == 0:
            node = node + (count - 1) * nodes
        return jnp.where(face_ref[0, row : row + 1, :] == node, 1.0, 0.0).astype(F32)

    def mask(c):
        return live[c].astype(BF16)

    def relayout(i):
        res_load(i).wait()
        for chunk in range(*parts[i]):
            at = slice(chunk * face, (chunk + 1) * face)
            wide = res_in[at].astype(F32).reshape(face * cells, res)
            for h in range(res // 128):
                lanes = slice(h * 128, (h + 1) * 128)
                res_wide[h] = wide[:, lanes]
                for c in range(cells):
                    res_ref[c, at, lanes] = res_wide[h, pl.ds(c, face, stride=cells), :].astype(BF16)


    def rows_of(c):
        return slice(c * width, (c + 1) * width)

    def face_copy(step, b, way):
        return remote(
            face_out.at[step, b, way],
            face_in.at[step, b, way],
            face_send_sem.at[step, b, way],
            face_recv_sem.at[step, b, way],
            "dom",
            d + 1 if way == RIGHT else d - 1,
        )

    def first(b, c):
        if c is None:
            return jnp.concatenate([first(b, i) for i in range(cells)], axis=0)
        return start_ref[b, c] * mask(c)

    def second(b, c):
        return inner[b] if c is None else inner[b, rows_of(c), :]

    def operator_begin(step, b, meanwhile=None):
        field = partial(second if step else first, b)
        local[b] = dot_nn(field(None), stiff_ref[...])

        def value(c, at):
            potential = pot_ref[c : c + 1, at] * field(c)[:, at].astype(F32)
            return scale[c] * local[b, rows_of(c), at] + potential

        last_tail = jnp.zeros((width, nodes - window), F32)
        for c in range(cells):
            last_tail = last_tail + last[c] * value(c, slice(window, nodes))
        face_out[step, b, RIGHT] = dot_nn(
            last_tail, one_hot(0, window, nodes - window), lax.Precision.HIGHEST
        )
        face_out[step, b, LEFT] = dot_nn(
            value(0, slice(0, face)), one_hot(1, 0, face), lax.Precision.HIGHEST
        )
        if meanwhile is not None:
            meanwhile()
        for way, there in ((RIGHT, has_next), (LEFT, has_prev)):

            @pl.when(there)
            def _():
                face_copy(step, b, way).start()

            pending.append((there, partial(face_copy, step, b, way)))
        for c in range(cells):
            local[b, rows_of(c), :] = value(c, slice(0, nodes))
        for c in range(cells - 1):
            pair = live[c + 1]
            tail = local[b, rows_of(c), window:]
            head = local[b, rows_of(c + 1), :face]
            padded = head
            if offset:
                padded = jnp.concatenate([jnp.zeros((width, offset), F32), head], axis=1)
            local[b, rows_of(c), window:] = tail + pair * padded
            local[b, rows_of(c + 1), :face] = head + pair * tail[:, offset:]

    def operator_end(step, b):
        for way, source in ((RIGHT, has_prev), (LEFT, has_next)):

            @pl.when(source)
            def _():
                face_copy(step, b, way).wait_recv()

            @pl.when(jnp.logical_not(source))
            def _():
                face_in[step, b, way] = jnp.zeros((width, face), F32)

        local[b, rows_of(0), :face] += dot_nt(
            face_in[step, b, RIGHT], one_hot(1, 0, face), lax.Precision.HIGHEST
        )
        tail_add = dot_nt(
            face_in[step, b, LEFT], one_hot(0, window, nodes - window), lax.Precision.HIGHEST
        )
        for c in range(cells):
            local[b, rows_of(c), window:] += last[c] * tail_add
        for c in range(cells):
            value = live[c] * local[b, rows_of(c), :]
            if step == 0:
                inner[b, rows_of(c), :] = (
                    (value - CENTER * first(b, c).astype(F32)) / HALF_WIDTH
                ).astype(BF16)
            else:
                states[b, c, own, :] = (
                    2.0 * (value - CENTER * second(b, c).astype(F32)) / HALF_WIDTH
                    - first(b, c).astype(F32)
                ).astype(BF16)


    def of_shard(shard):
        return pl.ds(pl.multiple_of(shard * width, width), width)

    def gather_copy(b, way, shard, c, here):
        at = states.at[b, c, of_shard(shard), :]
        slot = jnp.where(shard > here, shard - 1, shard)
        return remote(
            at, at, gather_send_sem.at[b, way, shard], gather_recv_sem.at[b, slot, c], "st", to(way)
        )

    def gather_whole(b, way, shard, begin):
        at = states.at[b, pl.ds(begin, cells - begin), of_shard(shard), :]
        return remote(
            at, at, gather_send_sem.at[b, way, shard], gather_recv_sem.at[b, 0, 0], "st", to(way)
        )

    def gather_own(b, way, there):
        @pl.when(jnp.logical_and(there, sends[way]))
        def _():
            def one(c, carry):
                gather_copy(b, way, s, c, to(way)).start()
                return carry

            lax.fori_loop(jnp.where(to_end[way], given[b], 0), cells, one, 0)

    def gather_flat(b, begin, end):
        wait = min(5, cells - given[b])

        def one(i, carry):
            for way in (LEFT, RIGHT):
                m = i - gap[way]
                k = lax.div(jnp.maximum(m, 0), cells) + 1
                c = lax.rem(jnp.maximum(m, 0), cells)
                shard = s - k if way == RIGHT else s + k
                here = both(m >= 0, shard >= 0, shard < sts)
                whole = c >= given[b]
                held = jnp.logical_or(whole, jnp.logical_not(ends))
                passed = jnp.logical_or(whole, jnp.logical_not(to_end[way]))

                @pl.when(both(here, held))
                def _():
                    gather_copy(b, way, shard, c, s).wait_recv()

                    @pl.when(both(sends[way], passed))
                    def _():
                        gather_copy(b, way, shard, c, to(way)).start()

                if b + 1 < blocks:
                    final = shard == (0 if way == RIGHT else steps)

                    @pl.when(both(here, final, c == cells - 1))
                    def _():
                        gather_own(b + 1, way, True)

            c = i - gathered_at

            @pl.when(both(c >= jnp.where(ends, given[b], 0), c < cells))
            def _():
                contract(b, c)

            if given[b]:
                for way in (RIGHT, LEFT):

                    @pl.when(both(near_end[way], c >= wait, c < wait + given[b]))
                    def _():
                        contract_near(b, way, c - wait)

            return carry

        lax.fori_loop(begin, end, one, 0)

    def gather_drain(b):
        def one(shard, carry):
            for way, passed in ((RIGHT, shard <= s), (LEFT, shard >= s)):

                @pl.when(both(passed, sends[way], to_end[way]))
                def _():
                    gather_whole(b, way, shard, given[b]).wait_send()

                @pl.when(both(passed, sends[way], jnp.logical_not(to_end[way])))
                def _():
                    gather_whole(b, way, shard, 0).wait_send()

            return carry

        lax.fori_loop(0, sts, one, 0)


    def contract(b, c):
        block = states[b, c]
        found = dot_nn(block, res_ref[c])
        for h in range(res // total_states):
            at = slice(h * total_states, (h + 1) * total_states)
            part[b, at, :] += found[:, at]
        part[b, res : res + total_states, :] += dot_nt(block, block)

    def give_copy(b, way):
        return remote(
            near_wire.at[b],
            near_got.at[b],
            give_send_sem.at[b],
            give_recv_sem.at[b],
            "st",
            to(1 - way),
        )

    def contract_near(b, way, c):
        @pl.when(c >= (given[b - 1] if b else 0))
        def _():
            near_wait(way, c)

        @pl.when(c == 0)
        def _():
            near_part[b] = jnp.zeros(near_part.shape[1:], F32)

        block = states[b, c]
        found = dot_nn(block, res_near[way, c])
        for h in range(res // total_states):
            at = slice(h * total_states, (h + 1) * total_states)
            near_part[b, at, :] += found[:, at]
        near_part[b, res : res + total_states, :] += dot_nt(block, block)

        @pl.when(c == given[b] - 1)
        def _():
            near_wire[b] = near_part[b].astype(WIRE)
            give_copy(b, way).start()

    def give_end(b):
        if not given[b]:
            return
        at = slice(0, res + total_states)

        @pl.when(ends)
        def _():
            give_copy(b, RIGHT).wait_recv()
            part[b, at, :] += near_got[b].astype(F32)

    def give_drain(b):
        if not given[b]:
            return

        @pl.when(jnp.logical_or(near_end[RIGHT], near_end[LEFT]))
        def _():
            give_copy(b, RIGHT).wait_send()

    def slice_of(peer):
        return pl.ds(pl.multiple_of(peer * rows, 16), rows)

    def one_copy(b, k):
        peer = dom_peer(k)
        return remote(
            wire.at[b, slice_of(peer)],
            part_recv.at[b, k],
            one_send_sem.at[b],
            one_recv_sem.at[b],
            "dom",
            peer,
        )

    def two_copy(b, k):
        at = total.at[b, slice_of(d)]
        return remote(at, at, two_send_sem.at[b], two_recv_sem.at[b], "dom", dom_peer(k))


    def one_whole(b):
        at = part_recv.at[b, pl.ds(1, doms - 1)]
        return remote(at, at, one_send_sem.at[b], one_recv_sem.at[b], "dom", dom_peer(1))

    def two_whole(b):
        at = total.at[b, pl.ds(0, (doms - 1) * rows)]
        return remote(at, at, two_send_sem.at[b], two_recv_sem.at[b], "dom", dom_peer(1))

    def peers(body):
        def step(k, carry):
            body(k)
            return carry

        lax.fori_loop(1, doms, step, 0)

    def reduce_start(b):
        give_end(b)
        wire[b] = part[b].astype(WIRE)
        peers(lambda k: one_copy(b, k).start())

    def reduce_middle(b):
        one_whole(b).wait_recv()

        def add(k, found):
            return found + part_recv[b, k].astype(F32)

        found = lax.fori_loop(1, doms, add, part[b, slice_of(d), :])
        total[b, slice_of(d), :] = found.astype(WIRE)
        peers(lambda k: two_copy(b, k).start())

    def reduce_end(b):
        two_whole(b).wait_recv()

    def reduce_drain(b):
        one_whole(b).wait_send()
        two_whole(b).wait_send()

    def coefficients(b):
        gram = total[b, res : res + total_states, :].astype(F32)
        shape = (total_states, total_states)
        eye = (
            lax.broadcasted_iota(jnp.int32, shape, 0) == lax.broadcasted_iota(jnp.int32, shape, 1)
        ).astype(F32)
        along = jnp.sum(gram * eye, axis=0, keepdims=True) / total_nodes + EPSILON
        down = jnp.sum(gram * eye, axis=1, keepdims=True) / total_nodes + EPSILON
        root_i, root_j = lax.rsqrt(along), lax.rsqrt(down)
        mixing = root_i * (1.5 * eye - 0.5 * (gram * root_i * root_j / total_nodes))
        mix[b] = mixing.astype(BF16)
        for h in range(res // total_states):
            at = slice(h * total_states, (h + 1) * total_states)
            proj[b, :, at] = dot_nn(
                mixing, total[b, at, :].astype(F32), lax.Precision.HIGHEST
            ).astype(BF16)


    def near_copy(way, c, i):
        at = cuts(nodes, 2)[i]
        return remote(
            res_ref.at[c, at],
            res_near.at[way, c, at],
            near_send_sem.at[c, i],
            near_recv_sem.at[c, i],
            "st",
            to(way),
        )

    def near_start(c, i):
        if c >= moved:
            return
        for way in (RIGHT, LEFT):
            there = both(origin[way], sends[way])

            @pl.when(there)
            def _():
                near_copy(way, c, i).start()

            pending.append((there, partial(near_copy, way, c, i)))

    def near_wait(way, c):
        for i in range(2):
            near_copy(way, c, i).wait_recv()

    def coef_copy(b, way):
        return remote(
            proj.at[b],
            proj_near.at[way, b],
            coef_send_sem.at[b],
            coef_recv_sem.at[b],
            "st",
            to(way),
        )

    def coef_start(b):
        if not moved:
            return
        for way in (RIGHT, LEFT):
            there = both(origin[way], sends[way])

            @pl.when(there)
            def _():
                coef_copy(b, way).start()

            pending.append((there, partial(coef_copy, b, way)))


    def share_copy(b, t, way, c, here):
        slot = jnp.where(jnp.logical_and(t == here, way == LEFT), sts, t)
        return remote(
            share.at[b, t, c],
            share_recv.at[way, b, t, c],
            share_send_sem.at[b, t],
            share_recv_sem.at[b, slot, c],
            "st",
            to(way),
        )

    def share_whole(b, t, way, begin):
        at = pl.ds(begin, cells - begin)
        return remote(
            share.at[b, t, at],
            share_recv.at[way, b, t, at],
            share_send_sem.at[b, t],
            share_recv_sem.at[b, t, 0],
            "st",
            to(way),
        )

    def ahead(way):
        if way == RIGHT:
            return steps - s, lambda i: steps - i
        return s, lambda i: i

    def share_cell(b, c):
        found = dot_nt(proj[b], res_ref[c])
        for t in range(sts):
            piece = found[t * width : (t + 1) * width, :]
            share[b, t, c] = piece.astype(BF16)

            @pl.when(t == s)
            def _():
                retained[b, c] = -piece

    def retain(b, c):
        retained[b, c] += dot_nn(mix[b, own, :], states[b, c])

    def share_start(b):
        def one(i, carry):
            c = lax.rem(i + moved, cells)

            @pl.when(c < given[b])
            def _():
                retained[b, c] = jnp.zeros(retained.shape[2:], F32)

            @pl.when(c >= given[b])
            def _():
                share_cell(b, c)

            for way in (RIGHT, LEFT):

                @pl.when(both(origin[way], c >= moved))
                def _():
                    share_copy(b, ahead(way)[1](0), way, c, to(way)).start()

            @pl.when(c >= given[b])
            def _():
                retain(b, c)

            return carry

        def rest(i, carry):
            for way in (RIGHT, LEFT):

                @pl.when(origin[way])
                def _():
                    t = ahead(way)[1](lax.div(i, kept) + 1)
                    share_copy(b, t, way, lax.rem(i, kept) + moved, to(way)).start()

            return carry

        kept = cells - moved

        @pl.when(ends)
        def _():
            lax.fori_loop(0, kept, one, 0)
            lax.fori_loop(0, (steps - 1) * kept, rest, 0)
            lax.fori_loop(kept, cells, one, 0)

    def share_drain(b):
        def one(t, carry):
            for way, passed in ((RIGHT, t > s), (LEFT, t < s)):

                @pl.when(both(passed, origin[way]))
                def _():
                    share_whole(b, t, way, moved).wait_send()

                @pl.when(both(passed, jnp.logical_not(origin[way])))
                def _():
                    share_whole(b, t, way, 0).wait_send()

            return carry

        lax.fori_loop(0, sts, one, 0)

    def absorb(b, way, t, c):
        share_copy(b, t, way, c, s).wait_recv()

        @pl.when(t == s)
        def _():
            retained[b, c] -= share_recv[way, b, t, c].astype(F32)

        @pl.when(t != s)
        def _():
            found = share[b, t, c].astype(F32) + share_recv[way, b, t, c].astype(F32)
            share[b, t, c] = found.astype(BF16)
            if given[b]:

                @pl.when(both(to_end[way], c < given[b]))
                def _():
                    share[b, t, c] = (found + near_term[b, c]).astype(BF16)

            share_copy(b, t, way, c, to(way)).start()

    def absorb_near(b, way, c):
        if b == 0:

            @pl.when(c >= max(given))
            def _():
                near_wait(way, c)

        @pl.when(c == 0)
        def _():
            coef_copy(b, way).wait_recv()

        found = dot_nt(proj_near[way, b], res_near[way, c])
        if given[b]:

            @pl.when(c < given[b])
            def _():
                at = (0 if way == RIGHT else steps) * width
                end = slice(at, at + width)
                near_term[b, c] = found[end, :] - dot_nn(mix[b, end, :], states[b, c])

        for t in reversed(range(sts)) if way == RIGHT else range(sts):
            piece = found[t * width : (t + 1) * width, :]

            @pl.when(t > s if way == RIGHT else t < s)
            def _():
                share[b, t, c] = (share[b, t, c].astype(F32) + piece).astype(BF16)

            @pl.when(t == s)
            def _():
                retained[b, c] -= piece

    def chain(turns, begin, end, ready=None):
        def one(j, carry):
            for b, offset in turns:
                chain_step(b, j + offset)
            if ready is not None and early:
                share_middle(ready, j - cells - 2)
            return carry

        lax.fori_loop(begin, end, one, 0)

    def share_middle(b, c):
        @pl.when(both(jnp.logical_not(ends), c >= 0, c < cells))
        def _():
            share_cell(b, c)
            retain(b, c)

    def chain_step(b, j):
        if b == 0 or not early:
            share_middle(b, j)
        for way in (RIGHT, LEFT):
            m = j - lag[way]
            i = lax.div(jnp.maximum(m, 0), cells)
            c = lax.rem(jnp.maximum(m, 0), cells)
            number, target = ahead(way)
            here = both(receives[way], m >= 0, i <= number)
            near = both(near_end[way], c < moved)
            if moved:

                @pl.when(both(here, near, i == 0))
                def _():
                    absorb_near(b, way, c)

                @pl.when(both(here, near, i < number))
                def _():
                    share_copy(b, target(i), way, c, to(way)).start()

            @pl.when(both(here, jnp.logical_not(near)))
            def _():
                absorb(b, way, target(i), c)

        c = j - done_at

        @pl.when(both(c >= 0, c < cells))
        def _():
            alive = jnp.where(c < count, 1.0, 0.0).astype(BF16)
            out_ref[b, c] = retained[b, c].astype(BF16) * alive
            pltpu.make_async_copy(out_ref.at[b, c], out_hbm.at[b, c], out_sem.at[b]).start()


    for b in range(blocks):
        part[b] = jnp.zeros(part.shape[1:], F32)
    @pl.when(ends)
    def _():
        relayout(0)
        meet()

    near_start(0, 0)
    pl.when(ends)(partial(relayout, 1))
    near_start(0, 1)
    start_load(0).wait()
    stiff_load(pl.ds(0, nodes)).wait()
    pl.when(jnp.logical_not(ends))(res_start)
    operator_begin(0, 0, lambda: pl.when(jnp.logical_not(ends))(meet))
    operator_end(0, 0)
    operator_begin(1, 0)
    for b in range(1, blocks):
        start_load(b).wait()
        operator_begin(0, b)
    for b in range(blocks):
        operator_end(1, b)
        if b == 0:
            for way in (RIGHT, LEFT):
                gather_own(0, way, True)
            for i in range(2):
                near_start(1, i)
            for i in range(2):
                pl.when(jnp.logical_not(ends))(partial(relayout, i))
            for later in range(1, blocks):
                operator_end(0, later)
                operator_begin(1, later)
        if b == 1:
            for way in (RIGHT, LEFT):
                gather_own(1, way, origin[way])
    for c in range(2, moved):
        for i in range(2):
            near_start(c, i)

    half = cells // 2
    whole = steps * cells
    links = done_at + cells
    over = cells - 2
    cut_one = jnp.where(ends, done_at, cells - 1)
    cut_two = jnp.where(ends, done_at, cells + 2)
    gather_flat(0, 0, whole)
    reduce_start(0)
    for b in range(blocks):
        following, previous = b + 1 < blocks, b > 0
        if following:
            gather_flat(b + 1, 0, half)
        if previous:
            chain([(b - 1, 0)], over if b > 1 else 0, cut_one)
        reduce_middle(b)
        if following:
            gather_flat(b + 1, half, cells)
        if previous:
            chain([(b - 1, 0)], cut_one, cut_two)
        reduce_end(b)
        coefficients(b)
        coef_start(b)
        share_start(b)
        if previous:
            chain([(b - 1, 0)], cut_two, links - over, b)
            chain([(b - 1, links - over), (b, 0)], 0, over)
        if following:
            gather_flat(b + 1, cells, whole)
            reduce_start(b + 1)
    chain([(blocks - 1, 0)], over if blocks > 1 else 0, links)

    for there, make in pending:

        @pl.when(there)
        def _():
            make().wait_send()

    for b in range(blocks):
        gather_drain(b)
        reduce_drain(b)
        share_drain(b)
        give_drain(b)
        pltpu.make_async_copy(out_ref.at[b], out_hbm.at[b], out_sem.at[b]).wait()


def on_device(start_block, resident, stiffness, cell_scale, potential, cell_count, face_index):
    blocks, cells, width, nodes = start_block.shape
    res = resident.shape[0]
    face = face_index.shape[2]
    doms, sts = lax.axis_size("dom"), lax.axis_size("st")
    total_states = sts * width
    rows = -(-(res + total_states) // (16 * doms)) * 16
    moved = 3 * cells // 8 if sts > 3 else 0
    given = tuple(min(moved, (2 * b + 1) * cells // 8) for b in range(blocks))
    sizes = (doms, sts, blocks, cells, width, nodes, face, res, rows, moved, given)
    near = max(moved, 1)
    dma = pltpu.SemaphoreType.DMA
    vmem = pl.BlockSpec(memory_space=pltpu.VMEM)
    smem = pl.BlockSpec(memory_space=pltpu.SMEM)
    anywhere = pl.BlockSpec(memory_space=pl.ANY)
    far = pl.BlockSpec(memory_space=pltpu.HBM)

    def hold(array):
        return pltpu.with_memory_space_constraint(array, pltpu.HBM)

    return pl.pallas_call(
        partial(kernel, sizes),
        out_shape=jax.ShapeDtypeStruct((blocks, cells, width, nodes), BF16),
        in_specs=[smem, smem, far, far, far, vmem, vmem],
        out_specs=anywhere,
        scratch_shapes=[
            pltpu.VMEM((blocks, cells, width, nodes), BF16),
            pltpu.VMEM((nodes, nodes), BF16),
            pltpu.VMEM((blocks, cells, width, nodes), BF16),
            pltpu.VMEM((blocks, cells * width, nodes), F32),
            pltpu.VMEM((blocks, cells * width, nodes), BF16),
            pltpu.VMEM((blocks, cells, total_states, nodes), BF16),
            pltpu.VMEM((blocks, doms * rows, total_states), F32),
            pltpu.VMEM((blocks, doms * rows, total_states), WIRE),
            pltpu.VMEM((blocks, doms, rows, total_states), WIRE),
            pltpu.VMEM((blocks, doms * rows, total_states), WIRE),
            pltpu.VMEM((blocks, total_states, total_states), BF16),
            pltpu.VMEM((blocks, total_states, res), BF16),
            pltpu.VMEM((blocks, sts, cells, width, nodes), BF16),
            pltpu.VMEM((2, blocks, sts, cells, width, nodes), BF16),
            pltpu.VMEM((nodes, cells, res), BF16),
            pltpu.VMEM((res // 128, face * cells, 128), F32),
            pltpu.VMEM((cells, nodes, res), BF16),
            pltpu.VMEM((2, near, nodes, res), BF16),
            pltpu.VMEM((2, blocks, total_states, res), BF16),
            pltpu.VMEM((blocks, cells, width, nodes), F32),
            pltpu.VMEM((blocks, res + total_states, total_states), F32),
            pltpu.VMEM((blocks, res + total_states, total_states), WIRE),
            pltpu.VMEM((blocks, res + total_states, total_states), WIRE),
            pltpu.VMEM((blocks, near, width, nodes), F32),
            pltpu.VMEM((2, blocks, 2, width, face), F32),
            pltpu.VMEM((2, blocks, 2, width, face), F32),
            dma((2, blocks, 2)),
            dma((2, blocks, 2)),
            dma((blocks, 2, sts)),
            dma((blocks, max(sts - 1, 1), cells)),
            dma((blocks,)),
            dma((blocks,)),
            dma((blocks,)),
            dma((blocks,)),
            dma((blocks, sts)),
            dma((blocks, sts + 1, cells)),
            dma((2,)),
            dma((blocks,)),
            dma,
            dma((blocks,)),
            dma((near, 2)),
            dma((near, 2)),
            dma((blocks,)),
            dma((blocks,)),
            dma((blocks,)),
            dma((blocks,)),
        ],
        compiler_params=pltpu.CompilerParams(
            collective_id=0, has_side_effects=True, vmem_limit_bytes=36 * 1024 * 1024
        ),
    )(
        hold(cell_scale),
        cell_count,
        hold(start_block),
        hold(jnp.transpose(resident, (2, 1, 0))),
        hold(stiffness),
        hold(potential),
        hold(face_index),
    )


def solution(mesh):
    return jax.shard_map(
        on_device,
        mesh=mesh,
        in_specs=(
            P(None, "dom", "st", None),
            P("st", "dom", None),
            P(),
            P("dom"),
            P("dom", None),
            P("dom"),
            P("dom", None, None),
        ),
        out_specs=P(None, "dom", "st", None),
        check_vma=False,
    )
```

```python
from functools import partial

import jax
import jax.numpy as jnp
from jax import lax
from jax.experimental import pallas as pl
from jax.experimental.pallas import tpu as pltpu
from jax.sharding import PartitionSpec as P

CENTER = 0.5
HALF_WIDTH = 2.0
EPSILON = 1e-06
F32 = jnp.float32
BF16 = jnp.bfloat16
WIRE = BF16
RIGHT, LEFT = 0, 1
LAG = 6
GAP = 4
MESH = pl.DeviceIdType.MESH


def dot_nn(a, b, precision=None):
    return lax.dot_general(
        a, b, (((1,), (0,)), ((), ())), precision=precision, preferred_element_type=F32
    )


def dot_nt(a, b, precision=None):
    return lax.dot_general(
        a, b, (((1,), (1,)), ((), ())), precision=precision, preferred_element_type=F32
    )


def both(*conditions):
    found = conditions[0]
    for condition in conditions[1:]:
        found = jnp.logical_and(found, condition)
    return found


def kernel(
    sizes,
    scale_ref,
    count_ref,
    start_hbm,
    res_hbm,
    stiff_hbm,
    pot_ref,
    face_ref,
    out_hbm,
    start_ref,
    stiff_ref,
    out_ref,
    local,
    inner,
    states,
    part,
    wire,
    part_recv,
    total,
    mix,
    proj,
    share,
    share_recv,
    res_in,
    res_wide,
    res_ref,
    res_near,
    proj_near,
    retained,
    near_part,
    near_wire,
    near_got,
    near_term,
    face_out,
    face_in,
    face_send_sem,
    face_recv_sem,
    gather_send_sem,
    gather_recv_sem,
    one_send_sem,
    one_recv_sem,
    two_send_sem,
    two_recv_sem,
    share_send_sem,
    share_recv_sem,
    load_sem,
    start_sem,
    stiff_sem,
    out_sem,
    near_send_sem,
    near_recv_sem,
    coef_send_sem,
    coef_recv_sem,
    give_send_sem,
    give_recv_sem,
):
    doms, sts, blocks, cells, width, nodes, face, res, rows, moved, given = sizes
    total_states = sts * width
    total_nodes = float(doms * cells * nodes)
    window = (nodes - face) // 128 * 128
    offset = nodes - face - window
    d = lax.axis_index("dom")
    s = lax.axis_index("st")
    has_right, has_left = s < sts - 1, s > 0
    has_next, has_prev = d < doms - 1, d > 0
    own = pl.ds(pl.multiple_of(s * width, width), width)
    steps = sts - 1
    last_step = jnp.maximum(s, steps - s)
    ends = jnp.logical_or(s == 0, s == steps)
    pending = []
    count = count_ref[0]
    scale = [scale_ref[c] for c in range(cells)]
    live = [jnp.where(c < count, 1.0, 0.0).astype(F32) for c in range(cells)]
    last = [jnp.where(c == count - 1, 1.0, 0.0).astype(F32) for c in range(cells)]

    def start_load(b):
        return pltpu.make_async_copy(start_hbm.at[b], start_ref.at[b], start_sem.at[b])

    def cuts(extent, number):
        step = -(-extent // (number * 16)) * 16
        return [pl.ds(at, min(step, extent - at)) for at in range(0, extent, step)]

    def stiff_load(at):
        return pltpu.make_async_copy(stiff_hbm.at[at], stiff_ref.at[at], stiff_sem)

    chunks = nodes // face
    parts = ((0, chunks // 2 + 1), (chunks // 2 + 1, chunks))

    def res_load(i):
        begin, end = parts[i]
        at = pl.ds(begin * face, (end - begin) * face)
        return pltpu.make_async_copy(res_hbm.at[at], res_in.at[at], load_sem.at[i])

    def res_start():
        for i in range(2):
            res_load(i).start()

    pl.when(ends)(res_start)
    start_load(0).start()
    for at in cuts(nodes, 2):
        stiff_load(at).start()
    for b in range(1, blocks):
        start_load(b).start()

    origin = {RIGHT: s == 0, LEFT: s == steps}
    lag = {RIGHT: LAG * jnp.maximum(s - 1, 0), LEFT: LAG * jnp.maximum(steps - 1 - s, 0)}
    early = sts > 3
    done_at = jnp.maximum(
        jnp.where(s > 0, lag[RIGHT] + (steps - s) * cells, 0),
        jnp.where(s < steps, lag[LEFT] + s * cells, 0),
    )
    sends = {RIGHT: has_right, LEFT: has_left}
    receives = {RIGHT: has_left, LEFT: has_right}
    near_end = {RIGHT: s == 1, LEFT: s == steps - 1}
    to_end = {RIGHT: s == steps - 1, LEFT: s == 1}
    gap = {way: jnp.where(near_end[way], GAP if moved else 0, 0) for way in (RIGHT, LEFT)}
    gathered_at = jnp.maximum(
        jnp.where(s > 0, gap[RIGHT] + (s - 1) * cells, 0),
        jnp.where(s < steps, gap[LEFT] + (steps - s - 1) * cells, 0),
    )

    def to(way):
        return s + 1 if way == RIGHT else s - 1

    def dom_peer(k):
        return lax.rem(d + k, doms)

    barrier = pltpu.get_barrier_semaphore()

    def greet(k, carry):
        pl.semaphore_signal(barrier, inc=1, device_id={"dom": dom_peer(k)}, device_id_type=MESH)
        return carry

    lax.fori_loop(1, doms, greet, 0)
    for way in (RIGHT, LEFT):

        @pl.when(sends[way])
        def _():
            pl.semaphore_signal(barrier, inc=1, device_id={"st": to(way)}, device_id_type=MESH)

    def meet():
        neighbours = has_right.astype(jnp.int32) + has_left.astype(jnp.int32)
        pl.semaphore_wait(barrier, doms - 1 + neighbours)

    def remote(src, dst, send_sem, recv_sem, axis, peer):
        return pltpu.make_async_remote_copy(
            src_ref=src,
            dst_ref=dst,
            send_sem=send_sem,
            recv_sem=recv_sem,
            device_id={axis: peer},
            device_id_type=MESH,
        )

    def one_hot(row, first, extent):
        node = lax.broadcasted_iota(jnp.int32, (extent, face), 0) + first
        if row == 0:
            node = node + (count - 1) * nodes
        return jnp.where(face_ref[0, row : row + 1, :] == node, 1.0, 0.0).astype(F32)

    def mask(c):
        return live[c].astype(BF16)

    def relayout(i):
        res_load(i).wait()
        for chunk in range(*parts[i]):
            at = slice(chunk * face, (chunk + 1) * face)
            wide = res_in[at].astype(F32).reshape(face * cells, res)
            for h in range(res // 128):
                lanes = slice(h * 128, (h + 1) * 128)
                res_wide[h] = wide[:, lanes]
                for c in range(cells):
                    res_ref[c, at, lanes] = res_wide[h, pl.ds(c, face, stride=cells), :].astype(BF16)


    def rows_of(c):
        return slice(c * width, (c + 1) * width)

    def face_copy(step, b, way):
        return remote(
            face_out.at[step, b, way],
            face_in.at[step, b, way],
            face_send_sem.at[step, b, way],
            face_recv_sem.at[step, b, way],
            "dom",
            d + 1 if way == RIGHT else d - 1,
        )

    def first(b, c):
        if c is None:
            return jnp.concatenate([first(b, i) for i in range(cells)], axis=0)
        return start_ref[b, c] * mask(c)

    def second(b, c):
        return inner[b] if c is None else inner[b, rows_of(c), :]

    def operator_begin(step, b, meanwhile=None):
        field = partial(second if step else first, b)
        local[b] = dot_nn(field(None), stiff_ref[...])

        def value(c, at):
            potential = pot_ref[c : c + 1, at] * field(c)[:, at].astype(F32)
            return scale[c] * local[b, rows_of(c), at] + potential

        last_tail = jnp.zeros((width, nodes - window), F32)
        for c in range(cells):
            last_tail = last_tail + last[c] * value(c, slice(window, nodes))
        face_out[step, b, RIGHT] = dot_nn(
            last_tail, one_hot(0, window, nodes - window), lax.Precision.HIGHEST
        )
        face_out[step, b, LEFT] = dot_nn(
            value(0, slice(0, face)), one_hot(1, 0, face), lax.Precision.HIGHEST
        )
        if meanwhile is not None:
            meanwhile()
        for way, there in ((RIGHT, has_next), (LEFT, has_prev)):

            @pl.when(there)
            def _():
                face_copy(step, b, way).start()

            pending.append((there, partial(face_copy, step, b, way)))
        for c in range(cells):
            local[b, rows_of(c), :] = value(c, slice(0, nodes))
        for c in range(cells - 1):
            pair = live[c + 1]
            tail = local[b, rows_of(c), window:]
            head = local[b, rows_of(c + 1), :face]
            padded = head
            if offset:
                padded = jnp.concatenate([jnp.zeros((width, offset), F32), head], axis=1)
            local[b, rows_of(c), window:] = tail + pair * padded
            local[b, rows_of(c + 1), :face] = head + pair * tail[:, offset:]

    def operator_end(step, b):
        for way, source in ((RIGHT, has_prev), (LEFT, has_next)):

            @pl.when(source)
            def _():
                face_copy(step, b, way).wait_recv()

            @pl.when(jnp.logical_not(source))
            def _():
                face_in[step, b, way] = jnp.zeros((width, face), F32)

        local[b, rows_of(0), :face] += dot_nt(
            face_in[step, b, RIGHT], one_hot(1, 0, face), lax.Precision.HIGHEST
        )
        tail_add = dot_nt(
            face_in[step, b, LEFT], one_hot(0, window, nodes - window), lax.Precision.HIGHEST
        )
        for c in range(cells):
            local[b, rows_of(c), window:] += last[c] * tail_add
        for c in range(cells):
            value = live[c] * local[b, rows_of(c), :]
            if step == 0:
                inner[b, rows_of(c), :] = (
                    (value - CENTER * first(b, c).astype(F32)) / HALF_WIDTH
                ).astype(BF16)
            else:
                states[b, c, own, :] = (
                    2.0 * (value - CENTER * second(b, c).astype(F32)) / HALF_WIDTH
                    - first(b, c).astype(F32)
                ).astype(BF16)


    def of_shard(shard):
        return pl.ds(pl.multiple_of(shard * width, width), width)

    def gather_copy(b, way, shard, c, here):
        at = states.at[b, c, of_shard(shard), :]
        slot = jnp.where(shard > here, shard - 1, shard)
        return remote(
            at, at, gather_send_sem.at[b, way, shard], gather_recv_sem.at[b, slot, c], "st", to(way)
        )

    def gather_whole(b, way, shard, begin):
        at = states.at[b, pl.ds(begin, cells - begin), of_shard(shard), :]
        return remote(
            at, at, gather_send_sem.at[b, way, shard], gather_recv_sem.at[b, 0, 0], "st", to(way)
        )

    def gather_own(b, way, there):
        @pl.when(jnp.logical_and(there, sends[way]))
        def _():
            def one(c, carry):
                gather_copy(b, way, s, c, to(way)).start()
                return carry

            lax.fori_loop(jnp.where(to_end[way], given[b], 0), cells, one, 0)

    def gather_flat(b, begin, end):
        wait = min(5, cells - given[b])

        def one(i, carry):
            for way in (LEFT, RIGHT):
                m = i - gap[way]
                k = lax.div(jnp.maximum(m, 0), cells) + 1
                c = lax.rem(jnp.maximum(m, 0), cells)
                shard = s - k if way == RIGHT else s + k
                here = both(m >= 0, shard >= 0, shard < sts)
                whole = c >= given[b]
                held = jnp.logical_or(whole, jnp.logical_not(ends))
                passed = jnp.logical_or(whole, jnp.logical_not(to_end[way]))

                @pl.when(both(here, held))
                def _():
                    gather_copy(b, way, shard, c, s).wait_recv()

                    @pl.when(both(sends[way], passed))
                    def _():
                        gather_copy(b, way, shard, c, to(way)).start()

                if b + 1 < blocks:
                    final = shard == (0 if way == RIGHT else steps)

                    @pl.when(both(here, final, c == cells - 1))
                    def _():
                        gather_own(b + 1, way, True)

            c = i - gathered_at

            @pl.when(both(c >= jnp.where(ends, given[b], 0), c < cells))
            def _():
                contract(b, c)

            if given[b]:
                for way in (RIGHT, LEFT):

                    @pl.when(both(near_end[way], c >= wait, c < wait + given[b]))
                    def _():
                        contract_near(b, way, c - wait)

            return carry

        lax.fori_loop(begin, end, one, 0)

    def gather_drain(b):
        def one(shard, carry):
            for way, passed in ((RIGHT, shard <= s), (LEFT, shard >= s)):

                @pl.when(both(passed, sends[way], to_end[way]))
                def _():
                    gather_whole(b, way, shard, given[b]).wait_send()

                @pl.when(both(passed, sends[way], jnp.logical_not(to_end[way])))
                def _():
                    gather_whole(b, way, shard, 0).wait_send()

            return carry

        lax.fori_loop(0, sts, one, 0)


    def contract(b, c):
        block = states[b, c]
        found = dot_nn(block, res_ref[c])
        for h in range(res // total_states):
            at = slice(h * total_states, (h + 1) * total_states)
            part[b, at, :] += found[:, at]
        part[b, res : res + total_states, :] += dot_nt(block, block)

    def give_copy(b, way):
        return remote(
            near_wire.at[b],
            near_got.at[b],
            give_send_sem.at[b],
            give_recv_sem.at[b],
            "st",
            to(1 - way),
        )

    def contract_near(b, way, c):
        @pl.when(c >= (given[b - 1] if b else 0))
        def _():
            near_wait(way, c)

        @pl.when(c == 0)
        def _():
            near_part[b] = jnp.zeros(near_part.shape[1:], F32)

        block = states[b, c]
        found = dot_nn(block, res_near[way, c])
        for h in range(res // total_states):
            at = slice(h * total_states, (h + 1) * total_states)
            near_part[b, at, :] += found[:, at]
        near_part[b, res : res + total_states, :] += dot_nt(block, block)

        @pl.when(c == given[b] - 1)
        def _():
            near_wire[b] = near_part[b].astype(WIRE)
            give_copy(b, way).start()

    def give_end(b):
        if not given[b]:
            return
        at = slice(0, res + total_states)

        @pl.when(ends)
        def _():
            give_copy(b, RIGHT).wait_recv()
            part[b, at, :] += near_got[b].astype(F32)

    def give_drain(b):
        if not given[b]:
            return

        @pl.when(jnp.logical_or(near_end[RIGHT], near_end[LEFT]))
        def _():
            give_copy(b, RIGHT).wait_send()

    def slice_of(peer):
        return pl.ds(pl.multiple_of(peer * rows, 16), rows)

    def one_copy(b, k):
        peer = dom_peer(k)
        return remote(
            wire.at[b, slice_of(peer)],
            part_recv.at[b, k],
            one_send_sem.at[b],
            one_recv_sem.at[b],
            "dom",
            peer,
        )

    def two_copy(b, k):
        at = total.at[b, slice_of(d)]
        return remote(at, at, two_send_sem.at[b], two_recv_sem.at[b], "dom", dom_peer(k))


    def one_whole(b):
        at = part_recv.at[b, pl.ds(1, doms - 1)]
        return remote(at, at, one_send_sem.at[b], one_recv_sem.at[b], "dom", dom_peer(1))

    def two_whole(b):
        at = total.at[b, pl.ds(0, (doms - 1) * rows)]
        return remote(at, at, two_send_sem.at[b], two_recv_sem.at[b], "dom", dom_peer(1))

    def peers(body):
        def step(k, carry):
            body(k)
            return carry

        lax.fori_loop(1, doms, step, 0)

    def reduce_start(b):
        give_end(b)
        wire[b] = part[b].astype(WIRE)
        peers(lambda k: one_copy(b, k).start())

    def reduce_middle(b):
        one_whole(b).wait_recv()

        def add(k, found):
            return found + part_recv[b, k].astype(F32)

        found = lax.fori_loop(1, doms, add, part[b, slice_of(d), :])
        total[b, slice_of(d), :] = found.astype(WIRE)
        peers(lambda k: two_copy(b, k).start())

    def reduce_end(b):
        two_whole(b).wait_recv()

    def reduce_drain(b):
        one_whole(b).wait_send()
        two_whole(b).wait_send()

    def coefficients(b):
        gram = total[b, res : res + total_states, :].astype(F32)
        shape = (total_states, total_states)
        eye = (
            lax.broadcasted_iota(jnp.int32, shape, 0) == lax.broadcasted_iota(jnp.int32, shape, 1)
        ).astype(F32)
        along = jnp.sum(gram * eye, axis=0, keepdims=True) / total_nodes + EPSILON
        down = jnp.sum(gram * eye, axis=1, keepdims=True) / total_nodes + EPSILON
        root_i, root_j = lax.rsqrt(along), lax.rsqrt(down)
        mixing = root_i * (1.5 * eye - 0.5 * (gram * root_i * root_j / total_nodes))
        mix[b] = mixing.astype(BF16)
        for h in range(res // total_states):
            at = slice(h * total_states, (h + 1) * total_states)
            proj[b, :, at] = dot_nn(
                mixing, total[b, at, :].astype(F32), lax.Precision.HIGHEST
            ).astype(BF16)


    def near_copy(way, c, i):
        at = cuts(nodes, 2)[i]
        return remote(
            res_ref.at[c, at],
            res_near.at[way, c, at],
            near_send_sem.at[c, i],
            near_recv_sem.at[c, i],
            "st",
            to(way),
        )

    def near_start(c, i):
        if c >= moved:
            return
        for way in (RIGHT, LEFT):
            there = both(origin[way], sends[way])

            @pl.when(there)
            def _():
                near_copy(way, c, i).start()

            pending.append((there, partial(near_copy, way, c, i)))

    def near_wait(way, c):
        for i in range(2):
            near_copy(way, c, i).wait_recv()

    def coef_copy(b, way):
        return remote(
            proj.at[b],
            proj_near.at[way, b],
            coef_send_sem.at[b],
            coef_recv_sem.at[b],
            "st",
            to(way),
        )

    def coef_start(b):
        if not moved:
            return
        for way in (RIGHT, LEFT):
            there = both(origin[way], sends[way])

            @pl.when(there)
            def _():
                coef_copy(b, way).start()

            pending.append((there, partial(coef_copy, b, way)))


    def share_copy(b, t, way, c, here):
        slot = jnp.where(jnp.logical_and(t == here, way == LEFT), sts, t)
        return remote(
            share.at[b, t, c],
            share_recv.at[way, b, t, c],
            share_send_sem.at[b, t],
            share_recv_sem.at[b, slot, c],
            "st",
            to(way),
        )

    def share_whole(b, t, way, begin):
        at = pl.ds(begin, cells - begin)
        return remote(
            share.at[b, t, at],
            share_recv.at[way, b, t, at],
            share_send_sem.at[b, t],
            share_recv_sem.at[b, t, 0],
            "st",
            to(way),
        )

    def ahead(way):
        if way == RIGHT:
            return steps - s, lambda i: steps - i
        return s, lambda i: i

    def share_cell(b, c):
        found = dot_nt(proj[b], res_ref[c])
        for t in range(sts):
            piece = found[t * width : (t + 1) * width, :]
            share[b, t, c] = piece.astype(BF16)

            @pl.when(t == s)
            def _():
                retained[b, c] = -piece

    def retain(b, c):
        retained[b, c] += dot_nn(mix[b, own, :], states[b, c])

    def share_start(b):
        def one(i, carry):
            c = lax.rem(i + moved, cells)

            @pl.when(c < given[b])
            def _():
                retained[b, c] = jnp.zeros(retained.shape[2:], F32)

            @pl.when(c >= given[b])
            def _():
                share_cell(b, c)

            for way in (RIGHT, LEFT):

                @pl.when(both(origin[way], c >= moved))
                def _():
                    share_copy(b, ahead(way)[1](0), way, c, to(way)).start()

            @pl.when(c >= given[b])
            def _():
                retain(b, c)

            return carry

        def rest(i, carry):
            for way in (RIGHT, LEFT):

                @pl.when(origin[way])
                def _():
                    t = ahead(way)[1](lax.div(i, kept) + 1)
                    share_copy(b, t, way, lax.rem(i, kept) + moved, to(way)).start()

            return carry

        kept = cells - moved

        @pl.when(ends)
        def _():
            lax.fori_loop(0, kept, one, 0)
            lax.fori_loop(0, (steps - 1) * kept, rest, 0)
            lax.fori_loop(kept, cells, one, 0)

    def share_drain(b):
        def one(t, carry):
            for way, passed in ((RIGHT, t > s), (LEFT, t < s)):

                @pl.when(both(passed, origin[way]))
                def _():
                    share_whole(b, t, way, moved).wait_send()

                @pl.when(both(passed, jnp.logical_not(origin[way])))
                def _():
                    share_whole(b, t, way, 0).wait_send()

            return carry

        lax.fori_loop(0, sts, one, 0)

    def absorb(b, way, t, c):
        share_copy(b, t, way, c, s).wait_recv()

        @pl.when(t == s)
        def _():
            retained[b, c] -= share_recv[way, b, t, c].astype(F32)

        @pl.when(t != s)
        def _():
            found = share[b, t, c].astype(F32) + share_recv[way, b, t, c].astype(F32)
            share[b, t, c] = found.astype(BF16)
            if given[b]:

                @pl.when(both(to_end[way], c < given[b]))
                def _():
                    share[b, t, c] = (found + near_term[b, c]).astype(BF16)

            share_copy(b, t, way, c, to(way)).start()

    def absorb_near(b, way, c):
        if b == 0:

            @pl.when(c >= max(given))
            def _():
                near_wait(way, c)

        @pl.when(c == 0)
        def _():
            coef_copy(b, way).wait_recv()

        found = dot_nt(proj_near[way, b], res_near[way, c])
        if given[b]:

            @pl.when(c < given[b])
            def _():
                at = (0 if way == RIGHT else steps) * width
                end = slice(at, at + width)
                near_term[b, c] = found[end, :] - dot_nn(mix[b, end, :], states[b, c])

        for t in reversed(range(sts)) if way == RIGHT else range(sts):
            piece = found[t * width : (t + 1) * width, :]

            @pl.when(t > s if way == RIGHT else t < s)
            def _():
                share[b, t, c] = (share[b, t, c].astype(F32) + piece).astype(BF16)

            @pl.when(t == s)
            def _():
                retained[b, c] -= piece

    def chain(turns, begin, end, ready=None):
        def one(j, carry):
            for b, offset in turns:
                chain_step(b, j + offset)
            if ready is not None and early:
                share_middle(ready, j - cells - 2)
            return carry

        lax.fori_loop(begin, end, one, 0)

    def share_middle(b, c):
        @pl.when(both(jnp.logical_not(ends), c >= 0, c < cells))
        def _():
            share_cell(b, c)
            retain(b, c)

    def chain_step(b, j):
        if b == 0 and early:
            pl.when(j >= moved)(partial(share_middle, b, j))
        elif not early:
            share_middle(b, j)
        for way in (RIGHT, LEFT):
            m = j - lag[way]
            i = lax.div(jnp.maximum(m, 0), cells)
            c = lax.rem(jnp.maximum(m, 0), cells)
            number, target = ahead(way)
            here = both(receives[way], m >= 0, i <= number)
            near = both(near_end[way], c < moved)
            if moved:

                @pl.when(both(here, near, i == 0))
                def _():
                    absorb_near(b, way, c)

                @pl.when(both(here, near, i < number))
                def _():
                    share_copy(b, target(i), way, c, to(way)).start()

            @pl.when(both(here, jnp.logical_not(near)))
            def _():
                absorb(b, way, target(i), c)

        c = j - done_at

        @pl.when(both(c >= 0, c < cells))
        def _():
            alive = jnp.where(c < count, 1.0, 0.0).astype(BF16)
            out_ref[b, c] = retained[b, c].astype(BF16) * alive
            pltpu.make_async_copy(out_ref.at[b, c], out_hbm.at[b, c], out_sem.at[b]).start()


    for b in range(blocks):
        part[b] = jnp.zeros(part.shape[1:], F32)
    @pl.when(ends)
    def _():
        relayout(0)
        meet()

    near_start(0, 0)
    pl.when(ends)(partial(relayout, 1))
    near_start(0, 1)
    start_load(0).wait()
    stiff_load(pl.ds(0, nodes)).wait()
    pl.when(jnp.logical_not(ends))(res_start)
    operator_begin(0, 0, lambda: pl.when(jnp.logical_not(ends))(meet))
    operator_end(0, 0)
    operator_begin(1, 0)
    for b in range(1, blocks):
        start_load(b).wait()
        operator_begin(0, b)
    for b in range(blocks):
        operator_end(1, b)
        if b == 0:
            for way in (RIGHT, LEFT):
                gather_own(0, way, True)
            for i in range(2):
                near_start(1, i)
            for i in range(2):
                pl.when(jnp.logical_not(ends))(partial(relayout, i))
            for later in range(1, blocks):
                operator_end(0, later)
                operator_begin(1, later)
        if b == 1:
            for way in (RIGHT, LEFT):
                gather_own(1, way, origin[way])
    for c in range(2, moved):
        for i in range(2):
            near_start(c, i)

    half = cells // 2
    whole = steps * cells
    links = done_at + cells
    over = cells - 2
    cut_one = jnp.where(ends, done_at, cells - 1)
    cut_two = jnp.where(ends, done_at, cells + 2)
    gather_flat(0, 0, whole)
    reduce_start(0)
    for b in range(blocks):
        following, previous = b + 1 < blocks, b > 0
        if following:
            gather_flat(b + 1, 0, half)
        if previous:
            chain([(b - 1, 0)], over if b > 1 else 0, cut_one)
        reduce_middle(b)
        if following:
            gather_flat(b + 1, half, cells)
        if previous:
            chain([(b - 1, 0)], cut_one, cut_two)
        reduce_end(b)
        coefficients(b)
        coef_start(b)
        share_start(b)
        if b == 0 and early:
            for c in range(moved):
                share_middle(b, c)
        if previous:
            chain([(b - 1, 0)], cut_two, links - over, b)
            chain([(b - 1, links - over), (b, 0)], 0, over)
        if following:
            gather_flat(b + 1, cells, whole)
            reduce_start(b + 1)
    chain([(blocks - 1, 0)], over if blocks > 1 else 0, links)

    for there, make in pending:

        @pl.when(there)
        def _():
            make().wait_send()

    for b in range(blocks):
        gather_drain(b)
        reduce_drain(b)
        share_drain(b)
        give_drain(b)
        pltpu.make_async_copy(out_ref.at[b], out_hbm.at[b], out_sem.at[b]).wait()


def on_device(start_block, resident, stiffness, cell_scale, potential, cell_count, face_index):
    blocks, cells, width, nodes = start_block.shape
    res = resident.shape[0]
    face = face_index.shape[2]
    doms, sts = lax.axis_size("dom"), lax.axis_size("st")
    total_states = sts * width
    rows = -(-(res + total_states) // (16 * doms)) * 16
    moved = 3 * cells // 8 if sts > 3 else 0
    given = tuple(min(moved, (2 * b + 1) * cells // 8) for b in range(blocks))
    sizes = (doms, sts, blocks, cells, width, nodes, face, res, rows, moved, given)
    near = max(moved, 1)
    dma = pltpu.SemaphoreType.DMA
    vmem = pl.BlockSpec(memory_space=pltpu.VMEM)
    smem = pl.BlockSpec(memory_space=pltpu.SMEM)
    anywhere = pl.BlockSpec(memory_space=pl.ANY)
    far = pl.BlockSpec(memory_space=pltpu.HBM)

    def hold(array):
        return pltpu.with_memory_space_constraint(array, pltpu.HBM)

    return pl.pallas_call(
        partial(kernel, sizes),
        out_shape=jax.ShapeDtypeStruct((blocks, cells, width, nodes), BF16),
        in_specs=[smem, smem, far, far, far, vmem, vmem],
        out_specs=anywhere,
        scratch_shapes=[
            pltpu.VMEM((blocks, cells, width, nodes), BF16),
            pltpu.VMEM((nodes, nodes), BF16),
            pltpu.VMEM((blocks, cells, width, nodes), BF16),
            pltpu.VMEM((blocks, cells * width, nodes), F32),
            pltpu.VMEM((blocks, cells * width, nodes), BF16),
            pltpu.VMEM((blocks, cells, total_states, nodes), BF16),
            pltpu.VMEM((blocks, doms * rows, total_states), F32),
            pltpu.VMEM((blocks, doms * rows, total_states), WIRE),
            pltpu.VMEM((blocks, doms, rows, total_states), WIRE),
            pltpu.VMEM((blocks, doms * rows, total_states), WIRE),
            pltpu.VMEM((blocks, total_states, total_states), BF16),
            pltpu.VMEM((blocks, total_states, res), BF16),
            pltpu.VMEM((blocks, sts, cells, width, nodes), BF16),
            pltpu.VMEM((2, blocks, sts, cells, width, nodes), BF16),
            pltpu.VMEM((nodes, cells, res), BF16),
            pltpu.VMEM((res // 128, face * cells, 128), F32),
            pltpu.VMEM((cells, nodes, res), BF16),
            pltpu.VMEM((2, near, nodes, res), BF16),
            pltpu.VMEM((2, blocks, total_states, res), BF16),
            pltpu.VMEM((blocks, cells, width, nodes), F32),
            pltpu.VMEM((blocks, res + total_states, total_states), F32),
            pltpu.VMEM((blocks, res + total_states, total_states), WIRE),
            pltpu.VMEM((blocks, res + total_states, total_states), WIRE),
            pltpu.VMEM((blocks, near, width, nodes), F32),
            pltpu.VMEM((2, blocks, 2, width, face), F32),
            pltpu.VMEM((2, blocks, 2, width, face), F32),
            dma((2, blocks, 2)),
            dma((2, blocks, 2)),
            dma((blocks, 2, sts)),
            dma((blocks, max(sts - 1, 1), cells)),
            dma((blocks,)),
            dma((blocks,)),
            dma((blocks,)),
            dma((blocks,)),
            dma((blocks, sts)),
            dma((blocks, sts + 1, cells)),
            dma((2,)),
            dma((blocks,)),
            dma,
            dma((blocks,)),
            dma((near, 2)),
            dma((near, 2)),
            dma((blocks,)),
            dma((blocks,)),
            dma((blocks,)),
            dma((blocks,)),
        ],
        compiler_params=pltpu.CompilerParams(
            collective_id=0, has_side_effects=True, vmem_limit_bytes=36 * 1024 * 1024
        ),
    )(
        hold(cell_scale),
        cell_count,
        hold(start_block),
        hold(jnp.transpose(resident, (2, 1, 0))),
        hold(stiffness),
        hold(potential),
        hold(face_index),
    )


def solution(mesh):
    return jax.shard_map(
        on_device,
        mesh=mesh,
        in_specs=(
            P(None, "dom", "st", None),
            P("st", "dom", None),
            P(),
            P("dom"),
            P("dom", None),
            P("dom"),
            P("dom", None, None),
        ),
        out_specs=P(None, "dom", "st", None),
        check_vma=False,
    )
```
